256 devices in a mesh: seq: 32 (over y, x, core), tp: 8 (over z).
Axes of the slice: x: 4, y: 4, z: 8, core: 2. Of those that a mesh axis runs over, the one named last changes fastest.
Arguments:
- tokens: bfloat16 [8192, 4096], P('seq', 'tp'), may hold values from -11 to 11
- grad_out: bfloat16 [8192, 4096], P('seq', 'tp'), may hold values from -1.5 to 1.5
- in_weight: bfloat16 [4096, 4096], P('seq', 'tp'), may hold values from -0.09880682 to 0.09880682
- in_scale: float32 [4096], P('tp'), may hold values from 0.0008238636 to 0.010511364
- out_weight: bfloat16 [4096, 4096], P('seq', 'tp'), may hold values from -0.053943182 to 0.053943182
- out_scale: float32 [4096], replicated, may hold values from 0.00139204545 to 0.0057386364
- state_in: bfloat16 [8192, 128], P('seq'), may hold values from -0.0625 to 0.0625
- state_out: bfloat16 [8192, 128], P('seq'), may hold values from -6 to 6
- log_decay: float32 [8192, 64], P('seq', 'tp'), may hold values from -1.6 to 0
Outputs:
- grad_tokens: bfloat16 [8192, 4096], P('seq', 'tp')
- grad_in_weight: float32 [4096, 4096], P('seq', 'tp')
- grad_in_scale: float32 [4096], P('tp')
- grad_out_weight: float32 [4096, 4096], P('seq', 'tp')
- grad_out_scale: float32 [4096], P('seq')
The draws below stay inside these ranges and needn't reach their ends.
All inputs are finite; a program needn't handle non-finite values.
Results may differ from the reference program's by a relative error of at most 0.027.
Values may be sent and summed in bfloat16 or wider, within the bound.
No kernel may reach another device: no remote copies, remote signals or barrier semaphores. Data moves between devices by JAX's collectives and lax.ppermute only.
A program may use at most 128 MiB of HBM per device.

```python
import jax
import jax.numpy as jnp
from jax import lax

D = 4096
HEADS = 64
HEAD_DIM = 64
STATE = 128
STRETCH = 256
QMAX = 7
TOK_DEV = 256
SEQ_LEN = 8192
N_SEQ = 32
N_TP = 8


def draw_tokens(key, part):
    columns = jnp.arange(D, dtype=jnp.float32) / (D - 1)
    noise = jnp.clip(jax.random.normal(key, (SEQ_LEN, D), jnp.float32), -6.0, 6.0)
    rising = 0.6 * 3.0 ** columns
    return (noise * rising[None, :]).astype(jnp.bfloat16)


def input_pair(key):
    width = HEADS * HEAD_DIM
    first, second, third = jax.random.split(jax.random.fold_in(key, 101), 3)
    channels = jnp.arange(width, dtype=jnp.float32) / (width - 1)
    spread = jax.random.uniform(first, (width,), jnp.float32, -0.7, 0.7)
    scales = 0.6 * 3.0 ** channels * jnp.exp(spread) / (5.5 * D ** 0.5)
    levels = jax.random.randint(second, (D, width), -9, 10).astype(jnp.float32)
    offsets = jax.random.uniform(third, (D, width), jnp.float32, -0.35, 0.35)
    return ((levels + offsets) * scales[None, :], scales)


def output_pair(key):
    width = HEADS * HEAD_DIM
    first, second, third = jax.random.split(jax.random.fold_in(key, 202), 3)
    spread = jax.random.uniform(first, (D,), jnp.float32, -0.7, 0.7)
    scales = jnp.exp(spread) / (5.5 * width ** 0.5)
    levels = jax.random.randint(second, (D, width), -9, 10).astype(jnp.float32)
    offsets = jax.random.uniform(third, (D, width), jnp.float32, -0.35, 0.35)
    return ((levels + offsets) * scales[:, None], scales)


def draw_in_weight(key, part):
    return input_pair(key)[0].astype(jnp.bfloat16)


def draw_in_scale(key, part):
    return input_pair(key)[1]


def draw_out_weight(key, part):
    return output_pair(key)[0].astype(jnp.bfloat16)


def draw_out_scale(key, part):
    return output_pair(key)[1]


def draw_log_decay(key, part):
    keys = jax.random.split(key, 7)
    share = 0.5
    quick = jax.random.uniform(keys[0], (HEADS,), jnp.float32) < share
    quick_rate = jnp.exp(jax.random.uniform(keys[1], (HEADS,), jnp.float32, jnp.log(1.0 / 40.0), jnp.log(1.0 / 15.0)))
    slow_rate = jnp.exp(jax.random.uniform(keys[2], (HEADS,), jnp.float32, jnp.log(0.1), jnp.log(0.5))) / SEQ_LEN
    fading_factors = jnp.where(quick, quick_rate, slow_rate)
    approximate_guess = jax.random.uniform(keys[3], (SEQ_LEN, HEADS), jnp.float32, 0.3, 1.7)
    spans = SEQ_LEN // TOK_DEV
    extent_factor = jnp.exp(jax.random.uniform(keys[4], (spans, 1, HEADS), jnp.float32, -0.5, 0.5))
    extent_factor = jnp.broadcast_to(extent_factor, (spans, TOK_DEV, HEADS)).reshape(SEQ_LEN, HEADS)
    slot_numbers = jax.random.randint(keys[5], (4,), 0, SEQ_LEN)
    objective_scalars = jnp.log(1.0 - jax.random.uniform(keys[6], (4,), jnp.float32, 0.2, 0.5))
    sequence_offsets = jnp.arange(SEQ_LEN)
    packet_batches = jnp.sum(jnp.where(sequence_offsets[:, None] == slot_numbers[None, :], objective_scalars[None, :], 0.0), axis=1)
    return -fading_factors[None, :] * approximate_guess * extent_factor + packet_batches[:, None]


def block_levels(key, extent, cuts, least, high):
    factor_of = 1.0
    for axis_at, blocks in cuts:
        draws = jax.random.uniform(jax.random.fold_in(jax.random.fold_in(key, 6), axis_at), (blocks,), jnp.float32, least / len(cuts), high / len(cuts))
        factor_of = factor_of * jnp.repeat(jnp.exp(draws), extent[axis_at] // blocks).reshape((-1,) + (1,) * (len(extent) - 1 - axis_at))
    return factor_of


def centred(stream_key, extent, scale, most, shards=(), kind=jnp.bfloat16):
    drawn = scale * jax.random.normal(stream_key, extent, jnp.float32)
    if shards:
        drawn = drawn * block_levels(stream_key, extent, shards, -0.22, 0.18)
    return jnp.clip(drawn, -most, most).astype(kind)


def setup_inputs(seed: int = 0) -> dict:
    seeds = jax.random.split(jax.random.key(seed), 10)
    tokens = draw_tokens(jax.random.fold_in(seeds[9], 71), 0)
    grad_out = centred(seeds[1], (SEQ_LEN, D), ((TOK_DEV * N_SEQ) ** -0.25), 1.5, ((0, 32), (1, 8)))
    in_weight = draw_in_weight(jax.random.fold_in(seeds[9], 71), 0)
    in_scale = draw_in_scale(jax.random.fold_in(seeds[9], 71), 0)
    out_weight = draw_out_weight(jax.random.fold_in(seeds[9], 71), 0)
    out_scale = draw_out_scale(jax.random.fold_in(seeds[9], 71), 0)
    state_in = centred(seeds[6], (SEQ_LEN, STATE), (4 / (STATE * TOK_DEV * N_SEQ) ** 0.5), 0.0625, ((0, 32),))
    state_out = centred(seeds[7], (SEQ_LEN, STATE), 1.0, 6.0, ((0, 32),))
    log_decay = draw_log_decay(jax.random.fold_in(seeds[9], 71), 0)
    return dict(tokens=tokens, grad_out=grad_out, in_weight=in_weight, in_scale=in_scale, out_weight=out_weight, out_scale=out_scale, state_in=state_in, state_out=state_out, log_decay=log_decay)


precise = lax.Precision.HIGHEST

def quantize(weight, channel_scale):
    ratios = weight.astype(jnp.float32) / channel_scale
    clipped = jnp.clip(ratios, -QMAX, QMAX)
    levels = jnp.floor(clipped + 0.5)
    inside = jnp.abs(ratios) <= QMAX
    slopes = jnp.where(inside, levels - ratios, levels)
    return (levels, slopes, inside.astype(jnp.float32))

def stretch_terms(decay_logs, inputs_f, outputs_f):
    cumul = jnp.cumsum(decay_logs, axis=0)
    ending = cumul[-1]
    spread = cumul[:, None, :] - cumul[None, :, :]
    length = decay_logs.shape[0]
    causal = jnp.arange(length)[:, None] >= jnp.arange(length)[None, :]
    mixing = jnp.exp(jnp.where(causal[:, :, None], spread, -jnp.inf))
    intersection = jnp.dot(outputs_f, inputs_f.T, precision=precise)
    return (cumul, ending, mixing * intersection[:, :, None])

def forward_stretch(carried, pieces):
    values, decay_logs, inputs_f, outputs_f = pieces
    cumul, ending, weights = stretch_terms(decay_logs, inputs_f, outputs_f)
    inner = jnp.einsum('sth,thp->shp', weights, values, precision=precise)
    outer = jnp.exp(cumul)[:, :, None] * jnp.einsum('sn,hnp->shp', outputs_f, carried, precision=precise)
    fresh = jnp.einsum('th,tn,thp->hnp', jnp.exp(ending[None, :] - cumul), inputs_f, values, precision=precise)
    return (jnp.exp(ending)[:, None, None] * carried + fresh, inner + outer)

def backward_stretch(carried, pieces):
    grads, decay_logs, inputs_f, outputs_f = pieces
    cumul, ending, weights = stretch_terms(decay_logs, inputs_f, outputs_f)
    inner = jnp.einsum('sth,shp->thp', weights, grads, precision=precise)
    outer = jnp.exp(ending[None, :] - cumul)[:, :, None] * jnp.einsum('tn,hnp->thp', inputs_f, carried, precision=precise)
    fresh = jnp.einsum('sh,sn,shp->hnp', jnp.exp(cumul), outputs_f, grads, precision=precise)
    return (jnp.exp(ending)[:, None, None] * carried + fresh, inner + outer)

def reference(tokens, grad_out, in_weight, in_scale, out_weight, out_scale, state_in, state_out, log_decay):
    width = HEADS * HEAD_DIM
    length = tokens.shape[0]
    blocks = length // STRETCH
    in_levels, in_slopes, in_inside = quantize(in_weight, in_scale[None, :])
    out_levels, out_slopes, out_inside = quantize(out_weight, out_scale[:, None])
    in_codes = in_levels.astype(jnp.bfloat16)
    out_codes = out_levels.astype(jnp.bfloat16)
    projected = jnp.dot(tokens, in_codes, preferred_element_type=jnp.float32) * in_scale[None, :]
    scaled_grad = (grad_out.astype(jnp.float32) * out_scale[None, :]).astype(jnp.bfloat16)
    grad_mixed = jnp.dot(scaled_grad, out_codes, preferred_element_type=jnp.float32)
    decay_blocks = log_decay.reshape(blocks, STRETCH, HEADS)
    inputs_f = state_in.astype(jnp.float32).reshape(blocks, STRETCH, STATE)
    outputs_f = state_out.astype(jnp.float32).reshape(blocks, STRETCH, STATE)
    empty = jnp.zeros((HEADS, STATE, HEAD_DIM), jnp.float32)
    value_blocks = projected.reshape(blocks, STRETCH, HEADS, HEAD_DIM)
    grad_blocks = grad_mixed.reshape(blocks, STRETCH, HEADS, HEAD_DIM)
    _, mixed = lax.scan(forward_stretch, empty, (value_blocks, decay_blocks, inputs_f, outputs_f))
    _, grad_values = lax.scan(backward_stretch, empty, (grad_blocks, decay_blocks, inputs_f, outputs_f), reverse=True)
    mixed = mixed.reshape(length, width)
    grad_values = grad_values.reshape(length, width)
    mixed_b = mixed.astype(jnp.bfloat16)
    grad_b = grad_values.astype(jnp.bfloat16)
    grad_scaled = (grad_values * in_scale[None, :]).astype(jnp.bfloat16)

    def add_block(totals, pieces):
        feats, grads_part, cotans, mixes = pieces
        in_piece = jnp.dot(feats.T, grads_part, preferred_element_type=jnp.float32).astype(jnp.bfloat16)
        out_piece = jnp.dot(cotans.T, mixes, preferred_element_type=jnp.float32).astype(jnp.bfloat16)
        in_piece, out_piece = lax.optimization_barrier((in_piece, out_piece))
        return ((totals[0] + in_piece.astype(jnp.float32), totals[1] + out_piece.astype(jnp.float32)), None)
    zero_grad = jnp.zeros((D, width), jnp.float32)
    (in_total, out_total), _ = lax.scan(add_block, (zero_grad, zero_grad), (tokens.reshape(N_SEQ, TOK_DEV, D), grad_b.reshape(N_SEQ, TOK_DEV, width), grad_out.reshape(N_SEQ, TOK_DEV, D), mixed_b.reshape(N_SEQ, TOK_DEV, width)))
    group = width // N_TP

    def add_heads(total, pieces):
        grads_part, codes_part = pieces
        piece = jnp.dot(grads_part, codes_part.T, preferred_element_type=jnp.float32).astype(jnp.bfloat16)
        piece = lax.optimization_barrier(piece)
        return (total + piece.astype(jnp.float32), None)
    token_total, _ = lax.scan(add_heads, jnp.zeros((length, D), jnp.float32), (grad_scaled.reshape(length, N_TP, group).transpose(1, 0, 2), in_codes.reshape(D, N_TP, group).transpose(1, 0, 2)))
    grad_tokens = token_total.astype(jnp.bfloat16)
    grad_in_weight = in_total * in_inside
    grad_out_weight = out_total * out_inside
    grad_in_scale = lax.optimization_barrier(jnp.sum(in_total * in_slopes, axis=0)) / jnp.sqrt(jnp.float32(D * QMAX))
    grad_out_scale = lax.optimization_barrier(jnp.sum(out_total * out_slopes, axis=1)) / jnp.sqrt(jnp.float32(width * QMAX))
    return (grad_tokens, grad_in_weight, grad_in_scale, grad_out_weight, grad_out_scale)
```

```python
import functools

import jax
import jax.numpy as jnp
from jax import lax
from jax.experimental import pallas as pl
from jax.experimental.pallas import tpu as pltpu
from jax.sharding import PartitionSpec as P

D = 4096
HEADS = 64
HEAD_DIM = 64
QMAX = 7

NY, NX, NC, NZ = 4, 4, 2, 8
T = 256
W = 512
R = 128
N = 128
HP = 8
PAIRS = 4

f32 = jnp.float32
bf16 = jnp.bfloat16


def seq_hop(v, dy=0, dx=0, dc=0):
    pairs = []
    for y in range(NY):
        for x in range(NX):
            for c in range(NC):
                to = (((y + dy) % NY) * NX + (x + dx) % NX) * NC + (c + dc) % NC
                pairs.append(((y * NX + x) * NC + c, to))
    return lax.ppermute(v, "seq", pairs)


def seq_xor(v, by=0, bx=0, bc=0):
    pairs = []
    for y in range(NY):
        for x in range(NX):
            for c in range(NC):
                pairs.append(((y * NX + x) * NC + c, ((y ^ by) * NX + (x ^ bx)) * NC + (c ^ bc)))
    return lax.ppermute(v, "seq", pairs)


def z_hop(v, d):
    return lax.ppermute(v, "tp", [(z, (z + d) % NZ) for z in range(NZ)])


def z_xor(v, b):
    return lax.ppermute(v, "tp", [(z, z ^ b) for z in range(NZ)])


def quantize(weight, channel_scale):
    ratios = weight.astype(f32) / channel_scale
    clipped = jnp.clip(ratios, -QMAX, QMAX)
    levels = jnp.floor(clipped + 0.5)
    inside = jnp.abs(ratios) <= QMAX
    slopes = jnp.where(inside, levels - ratios, levels)
    return (levels, slopes, inside.astype(f32))


def gather_z(own):
    r1 = z_hop(own, 1)
    l1 = z_hop(own, -1)
    r2 = z_hop(r1, 1)
    l2 = z_hop(l1, -1)
    r3 = z_hop(r2, 1)
    l3 = z_hop(l2, -1)
    half = T // 2
    top = z_hop(r3[:half], 1)
    bot = z_hop(l3[half:], -1)
    return [own, l1, l2, l3, top, bot, r3, r2, r1]


def vmem(n):
    return [pl.BlockSpec(memory_space=pltpu.VMEM)] * n


smem = pl.BlockSpec(memory_space=pltpu.SMEM)


def call(body, outs, n_in, flops, nbytes, name):
    return pl.pallas_call(
        body,
        out_shape=outs,
        in_specs=[smem] + vmem(n_in),
        out_specs=jax.tree.map(lambda _: pl.BlockSpec(memory_space=pltpu.VMEM), outs),
        compiler_params=pltpu.CompilerParams(vmem_limit_bytes=48 * 2**20),
        cost_estimate=pl.CostEstimate(flops=flops, bytes_accessed=nbytes, transcendentals=0),
        name=name,
    )


def sds(shape, dtype):
    return jax.ShapeDtypeStruct(shape, dtype)


def dot(a, b, ca=1, cb=0):
    return lax.dot_general(a, b, (((ca,), (cb,)), ((), ())), preferred_element_type=f32)


def lane_pair(first, second):
    lane = lax.broadcasted_iota(jnp.int32, (1, 128), 1)
    return jnp.where(lane < HEAD_DIM, first, second)


def assemble_body(pos, *refs):
    out = refs[-1]
    y, x, c = pos[0], pos[1], pos[2]
    for side in range(2):
        core = lax.rem(c + side, 2)
        for i in range(4):
            a_ref = refs[side * 8 + i]
            b_ref = refs[side * 8 + 4 + i]
            for j in range(4):
                chip_a = lax.rem(y + i, 4) * NX + lax.rem(x + j, 4)
                row = pl.multiple_of((chip_a * NC + core) * R, R)
                out[pl.ds(row, R), 0:256] = a_ref[j]
                chip_b = lax.rem(y + j, 4) * NX + lax.rem(x + i, 4)
                row = pl.multiple_of((chip_b * NC + core) * R, R)
                out[pl.ds(row, R), 256:512] = b_ref[j]


def gather_weight(pos, levels):
    a = levels[:, :256]
    b = levels[:, 256:]
    a_row = jnp.stack([a] + [seq_hop(a, dx=-d) for d in (1, 2, 3)])
    b_row = jnp.stack([b] + [seq_hop(b, dy=-d) for d in (1, 2, 3)])
    a_all = [a_row] + [seq_hop(a_row, dy=-d) for d in (1, 2, 3)]
    b_all = [b_row] + [seq_hop(b_row, dx=-d) for d in (1, 2, 3)]
    mine = a_all + b_all
    theirs = [seq_hop(v, dc=1) for v in mine]
    return call(
        assemble_body, sds((D, W), bf16), 16, 1000, 8 * 2**20, "assemble"
    )(pos, *mine, *theirs)


def project_body(scaled, pos, *refs):
    own, l1, l2, l3, top, bot, r3, r2, r1, w_ref, scale_ref, xt_ref, ew_ref = refs[:13]
    v_ref, mine_ref, sib_ref = refs[13:]
    c, z = pos[2], pos[3]

    def rows(k):
        return w_ref[pl.ds(pl.multiple_of(lax.rem(z + k, NZ) * W, W), W), :]

    total = dot(own[...], rows(0))
    for k, blk in ((1, l1), (2, l2), (3, l3), (5, r3), (6, r2), (7, r1)):
        total += dot(blk[...], rows(k))
    far = rows(4)
    total += jnp.concatenate([dot(top[...], far), dot(bot[...], far)], axis=0)
    if scaled:
        total = total * scale_ref[...]
    v = total.astype(bf16)
    v_ref[...] = v
    xt = xt_ref[...]
    for j in range(PAIRS):
        vj = v[:, 128 * j : 128 * j + 128]
        first = dot((xt * ew_ref[2 * j : 2 * j + 1, :]).astype(bf16), vj)
        second = dot((xt * ew_ref[2 * j + 1 : 2 * j + 2, :]).astype(bf16), vj)
        state = lane_pair(first, second).astype(bf16)

        @pl.when(c == j // 2)
        def _():
            mine_ref[j % 2] = state

        @pl.when(c != j // 2)
        def _():
            sib_ref[j % 2] = state


def project(scaled, pos, blocks, weight, scale, xt, ew, name):
    outs = (sds((T, W), bf16), sds((2, N, 128), bf16), sds((2, N, 128), bf16))
    return call(
        functools.partial(project_body, scaled), outs, 13, 2 * T * D * W, 7 * 2**20, name
    )(pos, *blocks, weight, scale, xt, ew)


def local_body(backward, pos, v_ref, b_ref, c_ref, a_ref, at_ref, out_ref):
    first, second = (b_ref, c_ref) if backward else (c_ref, b_ref)
    meet = dot(first[...], second[...], 1, 1)
    row = lax.broadcasted_iota(jnp.int32, (T, T), 0)
    col = lax.broadcasted_iota(jnp.int32, (T, T), 1)
    keep = (col >= row) if backward else (row >= col)
    for j in range(PAIRS):
        vj = v_ref[:, 128 * j : 128 * j + 128]
        parts = []
        for h in (2 * j, 2 * j + 1):
            spread = a_ref[:, h : h + 1] - at_ref[h : h + 1, :]
            if backward:
                spread = -spread
            mix = jnp.exp(jnp.where(keep, spread, -1e30)) * meet
            parts.append(dot(mix.astype(bf16), vj))
        out_ref[:, 128 * j : 128 * j + 128] = lane_pair(*parts)


def local_mix(backward, pos, v, b, c, a, at, name):
    return call(
        functools.partial(local_body, backward), sds((T, W), f32), 5, 10**9, 2**21, name
    )(pos, v, b, c, a, at)


def finish(pos, local_ref, x_ref, eo_ref, mine_ref, sib_ref, j):
    c = pos[2]
    kept = mine_ref[j % 2]
    came = sib_ref[j % 2]
    state = jnp.where(c == j // 2, kept.astype(f32), came.astype(f32)).astype(bf16)
    eo = lane_pair(eo_ref[:, 2 * j : 2 * j + 1], eo_ref[:, 2 * j + 1 : 2 * j + 2])
    return local_ref[:, 128 * j : 128 * j + 128] + eo * dot(x_ref[...], state)


def tokens_body(pos, local_ref, x_ref, eo_ref, mine_ref, sib_ref, scale_ref, w_ref, gb_ref, *outs):
    gs_ref = outs[-1]
    outs = outs[:-1]
    z = pos[3]
    for j in range(PAIRS):
        vals = finish(pos, local_ref, x_ref, eo_ref, mine_ref, sib_ref, j)
        at = slice(128 * j, 128 * j + 128)
        gb_ref[:, at] = vals.astype(bf16)
        gs_ref[:, at] = (vals * scale_ref[:, at]).astype(bf16)
    for k in (4, 3, 5, 2, 6, 1, 7, 0):
        rows = w_ref[pl.ds(pl.multiple_of(lax.rem(z + k, NZ) * W, W), W), :]
        outs[k][...] = dot(gs_ref[...], rows, 1, 1).astype(bf16)


def token_parts(pos, local, x, eo, mine, sib, scale, weight):
    outs = [sds((T, W), bf16)] * 9
    fn = pl.pallas_call(
        tokens_body,
        out_shape=outs,
        in_specs=[smem] + vmem(7),
        out_specs=vmem(9),
        scratch_shapes=[pltpu.VMEM((T, W), bf16)],
        compiler_params=pltpu.CompilerParams(vmem_limit_bytes=48 * 2**20),
        cost_estimate=pl.CostEstimate(
            flops=2 * T * D * W, bytes_accessed=7 * 2**20, transcendentals=0
        ),
        name="token_parts",
    )
    res = fn(pos, local, x, eo, mine, sib, scale, weight)
    return res[0], res[1:]


def store_total(pos, blocks, gb, refs):
    keep_a, keep_b, send_a, send_b = refs
    y, x, c, z = pos[0], pos[1], pos[2], pos[3]
    own, l1, l2, l3, top, bot, r3, r2, r1 = blocks
    for k, blk in enumerate((own, l1, l2, l3, None, r3, r2, r1)):
        if blk is None:
            half = T // 2
            part = dot(top[...], gb[:half], 0, 0) + dot(bot[...], gb[half:], 0, 0)
        else:
            part = dot(blk[...], gb[...], 0, 0)
        part = part.astype(bf16)
        base = lax.rem(z + k, NZ) * 2
        for i in range(4):
            chip = base + i // 2
            dy = lax.rem(chip // NX - y + NY, NY)
            dx = lax.rem(lax.rem(chip, NX) - x + NX, NX)
            a = part[R * i : R * i + R, :256]
            b = part[R * i : R * i + R, 256:]

            @pl.when(c == i % 2)
            def _():
                keep_a[dx, dy] = a
                keep_b[dy, dx] = b

            @pl.when(c != i % 2)
            def _():
                send_a[dx, dy] = a
                send_b[dy, dx] = b


def in_total_body(pos, *refs):
    store_total(pos, refs[:9], refs[9], refs[10:])


def out_total_body(pos, *refs):
    blocks = refs[:9]
    local_ref, x_ref, eo_ref, mine_ref, sib_ref = refs[9:14]
    mb = refs[-1]
    for j in range(PAIRS):
        at = slice(128 * j, 128 * j + 128)
        mb[:, at] = finish(pos, local_ref, x_ref, eo_ref, mine_ref, sib_ref, j).astype(bf16)
    store_total(pos, blocks, mb, refs[14:18])


TOTALS = [jax.ShapeDtypeStruct((4, 4, R, 256), jnp.bfloat16)] * 4


def in_parts(pos, blocks, gb):
    return call(in_total_body, TOTALS, 10, 2 * T * D * W, 7 * 2**20, "in_parts")(pos, *blocks, gb)


def out_parts(pos, blocks, local, x, eo, mine, sib):
    return pl.pallas_call(
        out_total_body,
        out_shape=TOTALS,
        in_specs=[smem] + vmem(14),
        out_specs=vmem(4),
        scratch_shapes=[pltpu.VMEM((T, W), bf16)],
        compiler_params=pltpu.CompilerParams(vmem_limit_bytes=48 * 2**20),
        cost_estimate=pl.CostEstimate(
            flops=2 * T * D * W, bytes_accessed=7 * 2**20, transcendentals=0
        ),
        name="out_parts",
    )(pos, *blocks, local, x, eo, mine, sib)


def add(*parts):
    total = parts[0].astype(f32)
    for part in parts[1:]:
        total = total + part.astype(f32)
    return total


def scatter_seq(parts):
    keep_a, keep_b, send_a, send_b = parts
    came_a = seq_hop(send_a, dc=1)
    came_b = seq_hop(send_b, dc=1)
    msg_a = [add(keep_a[d], came_a[d]).astype(bf16) for d in (1, 2, 3)]
    msg_b = [add(keep_b[d], came_b[d]).astype(bf16) for d in (1, 2, 3)]
    got_a = [seq_hop(m, dx=d) for m, d in zip(msg_a, (1, 2, 3))]
    got_b = [seq_hop(m, dy=d) for m, d in zip(msg_b, (1, 2, 3))]
    sum_a = add(keep_a[0], came_a[0], *got_a)
    sum_b = add(keep_b[0], came_b[0], *got_b)
    end_a = [seq_hop(sum_a[d].astype(bf16), dy=d) for d in (1, 2, 3)]
    end_b = [seq_hop(sum_b[d].astype(bf16), dx=d) for d in (1, 2, 3)]
    return jnp.concatenate([add(sum_a[0], *end_a), add(sum_b[0], *end_b)], axis=1)


def scatter_z(p):
    half = T // 2
    right = z_hop(p[4][:half], 1)
    left = z_hop(p[4][half:], -1)
    p3 = jnp.concatenate([add(p[3][:half], right).astype(bf16), p[3][half:]], axis=0)
    p5 = jnp.concatenate([p[5][:half], add(p[5][half:], left).astype(bf16)], axis=0)
    right = z_hop(p3, 1)
    left = z_hop(p5, -1)
    right = z_hop(add(p[2], right).astype(bf16), 1)
    left = z_hop(add(p[6], left).astype(bf16), -1)
    right = z_hop(add(p[1], right).astype(bf16), 1)
    left = z_hop(add(p[7], left).astype(bf16), -1)
    return add(p[0], right, left).astype(bf16)


def lanes(coef):
    return jnp.repeat(coef.reshape(PAIRS, 2), HEAD_DIM, axis=1).reshape(PAIRS, 1, 128)


def my_pairs(arr, c):
    return lax.dynamic_slice_in_dim(arr, 2 * c, 2, 0)


def between(table, first, last):
    at = jnp.arange(NY * NX * NC)
    mask = (at >= first) & (at <= last)
    return jnp.exp(jnp.sum(jnp.where(mask[:, None], table, 0.0), axis=0))


def totals_table(total, y, x, c):
    sib = seq_xor(total, bc=1)
    pair = jnp.stack([jnp.where(c == 0, total, sib), jnp.where(c == 0, sib, total)])
    row = jnp.stack([pair] + [seq_hop(pair, dx=d) for d in (1, 2, 3)])
    row = jnp.take(row, jnp.mod(x - jnp.arange(4), 4), axis=0)
    rows = jnp.stack([row] + [seq_hop(row, dy=d) for d in (1, 2, 3)])
    rows = jnp.take(rows, jnp.mod(y - jnp.arange(4), 4), axis=0)
    return rows.reshape(NY * NX * NC, HP)


def exchange(backward, mine, sib, table, y, x, c):
    chip = (y * NX + x) * NC
    row0 = y * NX * NC
    dev0 = between(table, chip, chip)
    dev1 = between(table, chip + 1, chip + 1)

    def cf(v):
        return my_pairs(lanes(v), c)

    other = seq_xor(sib, bc=1).astype(f32)
    own = mine.astype(f32)
    s0 = jnp.where(c == 0, own, other)
    s1 = jnp.where(c == 0, other, own)
    whole = s0 + cf(dev0) * s1 if backward else cf(dev1) * s0 + s1
    q = whole.astype(bf16)
    sign = -1 if backward else 1
    got = [seq_hop(q, dx=sign * d) for d in (1, 2, 3)]
    enter = 0.0
    row_sum = 0.0
    for d, g in zip((0, 1, 2, 3), [q] + got):
        src = jnp.mod(x - sign * d, NX)
        g = g.astype(f32)
        if backward:
            near = between(table, chip + 2, row0 + src * NC - 1)
            ok = src > x
            end = between(table, row0, row0 + src * NC - 1)
        else:
            near = between(table, row0 + src * NC + 2, chip - 1)
            ok = src < x
            end = between(table, row0 + src * NC + 2, row0 + NX * NC - 1)
        if d:
            enter = enter + cf(jnp.where(ok, near, 0.0)) * g
        row_sum = row_sum + cf(end) * g
    u = row_sum.astype(bf16)
    got = [seq_hop(u, dy=sign * d) for d in (1, 2, 3)]
    for d, g in zip((1, 2, 3), got):
        src = jnp.mod(y - sign * d, NY)
        if backward:
            near = between(table, chip + 2, src * NX * NC - 1)
            ok = src > y
        else:
            near = between(table, (src + 1) * NX * NC, chip - 1)
            ok = src < y
        enter = enter + cf(jnp.where(ok, near, 0.0)) * g.astype(f32)
    if backward:
        e1 = enter
        e0 = cf(dev1) * enter + s1
    else:
        e0 = enter
        e1 = cf(dev0) * enter + s0
    own = jnp.where(c == 0, e0, e1).astype(bf16)
    give = jnp.where(c == 0, e1, e0).astype(bf16)
    return own, seq_xor(give, bc=1)


def per_device(
    tokens, grad_out, in_weight, in_scale, out_weight, out_scale, state_in, state_out, log_decay
):
    s = lax.axis_index("seq")
    z = lax.axis_index("tp")
    y, x, c = s // (NX * NC), (s // NC) % NX, s % NC
    pos = jnp.stack([y, x, c, z]).astype(jnp.int32)
    scale_rows = lax.dynamic_slice_in_dim(out_scale, s * R, R)
    scale_cols = lax.dynamic_slice_in_dim(out_scale, z * W, W)
    in_levels, in_slopes, in_inside = quantize(in_weight, in_scale[None, :])
    out_levels, out_slopes, out_inside = quantize(out_weight, scale_rows[:, None])
    scaled = (grad_out.astype(f32) * scale_cols[None, :]).astype(bf16)

    cots = gather_z(scaled)
    out_codes = gather_weight(pos, out_levels.astype(bf16))
    in_codes = lax.all_gather(in_levels.astype(bf16), "seq", axis=0, tiled=True)
    feats = gather_z(tokens)

    run = jnp.cumsum(log_decay, axis=0)
    run_t = run.T
    total = run[-1]
    table = totals_table(total, y, x, c)
    up = jnp.exp(run)
    down = jnp.exp(total[None, :] - run)
    ct = state_out.astype(f32).T
    bt = state_in.astype(f32).T
    scale = in_scale[None, :]

    g, g_mine, g_sib = project(False, pos, cots, out_codes, scale, ct, up.T, "grad_mixed")
    g_local = local_mix(True, pos, g, state_in, state_out, run, run_t, "grad_local")
    g_in = exchange(True, g_mine, g_sib, table, y, x, c)
    gb, parts = token_parts(pos, g_local, state_in, down, *g_in, scale, in_codes)
    grad_tokens = scatter_z(parts)
    in_total = scatter_seq(in_parts(pos, feats, gb))

    v, v_mine, v_sib = project(True, pos, feats, in_codes, scale, bt, down.T, "projected")
    v_local = local_mix(False, pos, v, state_in, state_out, run, run_t, "mixed_local")
    v_in = exchange(False, v_mine, v_sib, table, y, x, c)
    out_total = scatter_seq(out_parts(pos, cots, v_local, state_out, up, *v_in))
    out_total = out_total / scale_rows[:, None]

    in_sum = jnp.sum(in_total * in_slopes, axis=0)[None]
    for hop in (dict(bc=1), dict(bx=1), dict(bx=2), dict(by=1), dict(by=2)):
        in_sum = in_sum + seq_xor(in_sum, **hop)
    out_sum = jnp.sum(out_total * out_slopes, axis=1)[None]
    for b in (1, 2, 4):
        out_sum = out_sum + z_xor(out_sum, b)
    return (
        grad_tokens,
        in_total * in_inside,
        in_sum[0] / jnp.sqrt(f32(D * QMAX)),
        out_total * out_inside,
        out_sum[0] / jnp.sqrt(f32(HEADS * HEAD_DIM * QMAX)),
    )


def solution(mesh):
    placed = (
        P("seq", "tp"),
        P("seq", "tp"),
        P("seq", "tp"),
        P("tp"),
        P("seq", "tp"),
        P(),
        P("seq", None),
        P("seq", None),
        P("seq", "tp"),
    )
    return jax.shard_map(
        per_device,
        mesh=mesh,
        in_specs=placed,
        out_specs=(P("seq", "tp"), P("seq", "tp"), P("tp"), P("seq", "tp"), P("seq")),
        check_vma=False,
    )
```

```python
import jax
import jax.numpy as jnp
from jax import lax
from jax.experimental import pallas as pl
from jax.experimental.pallas import tpu as pltpu
from jax.sharding import PartitionSpec as P

D = 4096
HEADS = 64
HEAD_DIM = 64
QMAX = 7

NY, NX, NC, NZ = 4, 4, 2, 8
T = 256
W = 512
R = 128
N = 128
HP = 8
PAIRS = 4

f32 = jnp.float32
bf16 = jnp.bfloat16


def seq_at(y, x, c):
    return ((y % NY) * NX + x % NX) * NC + c % NC


def hop(v, d, second=False):
    pairs = []
    for y in range(NY):
        for x in range(NX):
            for c in range(NC):
                along_x = (c == 0) != second
                to = seq_at(y, x + d, c) if along_x else seq_at(y + d, x, c)
                pairs.append((seq_at(y, x, c), to))
    return lax.ppermute(v, "seq", pairs)


def axis_hop(v, dy=0, dx=0):
    pairs = []
    for y in range(NY):
        for x in range(NX):
            for c in range(NC):
                pairs.append((seq_at(y, x, c), seq_at(y + dy, x + dx, c)))
    return lax.ppermute(v, "seq", pairs)


def seq_xor(v, bits):
    return lax.ppermute(v, "seq", [(s, s ^ bits) for s in range(NY * NX * NC)])


def swap(v):
    return seq_xor(v, 1)


def z_hop(v, d):
    return lax.ppermute(v, "tp", [(z, (z + d) % NZ) for z in range(NZ)])


def z_xor(v, b):
    return lax.ppermute(v, "tp", [(z, z ^ b) for z in range(NZ)])


FIRST = [[seq_at(y, x, 0) for x in range(NX)] for y in range(NY)] + [
    [seq_at(y, x, 1) for y in range(NY)] for x in range(NX)
]
SECOND = [[seq_at(y, x, 0) for y in range(NY)] for x in range(NX)] + [
    [seq_at(y, x, 1) for x in range(NX)] for y in range(NY)
]


def gather_z(own):
    r1 = z_hop(own, 1)
    l1 = z_hop(own, -1)
    r2 = z_hop(r1, 1)
    l2 = z_hop(l1, -1)
    r3 = z_hop(r2, 1)
    l3 = z_hop(l2, -1)
    top = z_hop(r3[:T], 1)
    bot = z_hop(l3[T:], -1)
    return [own, l1, l2, l3, r3, r2, r1, top, bot]


RELATIVE = (0, 1, 2, 3, 5, 6, 7)
smem = pl.BlockSpec(memory_space=pltpu.SMEM)
vmem = pl.BlockSpec(memory_space=pltpu.VMEM)


def sds(shape, dtype):
    return jax.ShapeDtypeStruct(shape, dtype)


def call(body, name, outs, args, flops=10**6, scratch=()):
    nbytes = sum(a.size * a.dtype.itemsize for a in args)
    nbytes += sum(o.size * o.dtype.itemsize for o in outs)
    return pl.pallas_call(
        body,
        out_shape=outs,
        in_specs=[smem] + [vmem] * (len(args) - 1),
        out_specs=[vmem] * len(outs),
        scratch_shapes=scratch,
        compiler_params=pltpu.CompilerParams(vmem_limit_bytes=56 * 2**20),
        cost_estimate=pl.CostEstimate(flops=flops, bytes_accessed=nbytes, transcendentals=0),
        name=name,
    )(*args)


def dot(a, b, ca=1, cb=0):
    return lax.dot_general(a, b, (((ca,), (cb,)), ((), ())), preferred_element_type=f32)


def iota(shape, dim):
    return lax.broadcasted_iota(jnp.int32, shape, dim)


def lane_pair(first, second):
    return jnp.where(iota((1, 128), 1) < HEAD_DIM, first, second)


def split3(v):
    hi = v.astype(bf16)
    rest = v - hi.astype(f32)
    mid = rest.astype(bf16)
    return hi, mid, (rest - mid.astype(f32)).astype(bf16)


def levels_of(weight, step):
    ratios = weight.astype(f32) / step
    return jnp.floor(jnp.clip(ratios, -QMAX, QMAX) + 0.5)


def prep_body(
    pos, tok, go, iw, isc, ow, os_rows, os_cols, ld, b_ref, c_ref,
    merged, o_keep, o_give, i_keep, i_give, run, run_t, up, down, up_t, down_t, bt, ct,
):
    c, z = pos[2], pos[3]
    s = (pos[0] * NX + pos[1]) * NC + c
    merged[:T, :] = (go[...].astype(f32) * os_cols[pl.ds(z, 1), :]).astype(bf16)
    merged[T:, :] = tok[...]
    square = (R, R)
    eye = iota(square, 0) == iota(square, 1)
    step = jnp.sum(jnp.where(eye, os_rows[pl.ds(s, 1), :], 0.0), axis=1, keepdims=True)
    out_lv = levels_of(ow[...], step).astype(bf16)
    in_lv = levels_of(iw[...], isc[...]).astype(bf16)
    for core in range(2):
        mine, other = slice(256 * core, 256 * core + 256), slice(256 - 256 * core, 512 - 256 * core)

        @pl.when(c == core)
        def _():
            o_keep[0:R, :] = out_lv[:, mine]
            o_give[0:R, :] = out_lv[:, other]
            i_keep[...] = in_lv[:, mine]
            i_give[...] = in_lv[:, other]

    parts = split3(ld[...])
    tri = (iota((T, T), 0) >= iota((T, T), 1)).astype(bf16)
    cum = dot(tri, parts[0]) + dot(tri, parts[1]) + dot(tri, parts[2])
    cum_t = sum(dot(p, tri, 0, 1) for p in parts)
    total = cum[T - 1 : T, :]
    run[...] = cum
    run_t[...] = cum_t
    up[...] = jnp.exp(cum)
    down[...] = jnp.exp(total - cum)
    up_t[...] = jnp.exp(cum_t)
    down_t[...] = jnp.exp(cum_t[:, T - 1 : T] - cum_t)
    lane = iota((1, 256), 1) // HEAD_DIM
    rows = []
    for half in range(2):
        spread = jnp.zeros((1, 256), f32)
        for h in range(4):
            spread = jnp.where(lane == h, total[:, 4 * half + h : 4 * half + h + 1], spread)
        rows += [p.astype(f32) for p in split3(spread)]
    tile_row = iota((16, 256), 0)
    tile = jnp.zeros((16, 256), f32)
    for i, row in enumerate(rows):
        tile = jnp.where(tile_row == i, row, tile)
    o_keep[R:, :] = tile.astype(bf16)
    o_give[R:, :] = tile.astype(bf16)
    bt[...] = b_ref[...].astype(f32).T
    ct[...] = c_ref[...].astype(f32).T


def place(c, core_of, y, x, first, second):
    ch_y = jnp.where(core_of == 0, second, first)
    ch_x = jnp.where(core_of == 0, first, second)
    return lax.rem(y + ch_y, NY) * NX + lax.rem(x + ch_x, NX)


def project_body(pos, *refs):
    blocks = refs[:9]
    o_mine, o_theirs = refs[9:13], refs[13:17]
    i_mine, i_theirs, isc, up_t, down_t, bt, ct = refs[17:24]
    v_ref, g_ref, mine_ref, sib_ref, cots, feats, w_in, coef = refs[24:32]
    w_out, acc, table = refs[32:]
    y, x, c, z = pos[0], pos[1], pos[2], pos[3]
    for k, blk in zip(RELATIVE, blocks[:7]):
        at = lax.rem(z + k, NZ)
        cots[at] = blk[:T, :]
        feats[at] = blk[T:, :]
    at = lax.rem(z + 4, NZ)
    cots[at] = blocks[7][...]
    feats[at] = blocks[8][...]
    for side, pieces in ((0, o_mine), (1, o_theirs)):
        half = lax.rem(c + side, 2)
        for e in range(4):
            for d in range(4):
                chip = place(c, half, y, x, d, e)
                for r in range(2):
                    s = chip * NC + lax.rem(half + r, 2)
                    row = pl.multiple_of(s * R, R)
                    w_out[half, pl.ds(row, R), :] = pieces[e][d, r, 0:R, :]
                    if side == 0:
                        tile = pieces[e][d, r, R:, :].astype(f32)
                        low = tile[0:1] + tile[1:2] + tile[2:3]
                        high = tile[3:4] + tile[4:5] + tile[5:6]
                        table[pl.ds(s, 1), :] = jnp.where(c == 0, low, high)
    for side, pieces in ((0, i_mine), (1, i_theirs)):
        half = lax.rem(c + side, 2)
        for second in range(4):
            for first in range(4):
                chip = place(c, half, 0, 0, first, second)
                for r in range(2):
                    row = pl.multiple_of((chip * NC + lax.rem(half + r, 2)) * R, R)
                    w_in[half, pl.ds(row, R), :] = pieces[(second * 4 + first) * 2 + r]

    chip0, row0 = (y * NX + x) * NC, y * NX * NC
    number = iota((NY * NX * NC, 1), 0)
    totals = table[...]

    def between(at, first, last, ok=None):
        inside = (number >= first) & (number <= last)
        value = jnp.exp(jnp.sum(jnp.where(inside, totals, 0.0), axis=0, keepdims=True))
        if ok is not None:
            value = jnp.where(ok, value, 0.0)
        coef[at : at + 1, :] = value

    between(0, chip0, chip0)
    between(1, chip0 + 1, chip0 + 1)
    for d in range(4):
        src = lax.rem(x - d + NX, NX)
        between(5 + d, row0 + src * NC + 2, row0 + NX * NC - 1)
        between(15 + d, row0, row0 + src * NC - 1)
        if d:
            between(1 + d, row0 + src * NC + 2, chip0 - 1, src < x)
            between(11 + d, chip0 + 2, row0 + src * NC - 1, src > x)
            src = lax.rem(y - d + NY, NY)
            between(8 + d, (src + 1) * NX * NC, chip0 - 1, src < y)
            between(18 + d, chip0 + 2, src * NX * NC - 1, src > y)
    coef[22:24, :] = jnp.zeros((2, 256), f32)

    for which, (src, weight, out) in enumerate(((cots, w_out, g_ref), (feats, w_in, v_ref))):
        acc[...] = jnp.zeros((T, W), f32)

        def step(b, _):
            lhs = src[b]
            row = pl.multiple_of(b * W, W)
            for half in range(2):
                at = slice(256 * half, 256 * half + 256)
                acc[:, at] += dot(lhs, weight[half, pl.ds(row, W), :])
            return 0

        lax.fori_loop(0, NZ, step, 0)
        total = acc[...]
        if which == 1:
            total = total * isc[...]
        out[...] = total.astype(bf16)

    for base, vals, xt, ew in ((0, v_ref, bt, down_t), (2, g_ref, ct, up_t)):
        for j in range(PAIRS):
            vj = vals[:, 128 * j : 128 * j + 128]
            first = dot((xt[...] * ew[2 * j : 2 * j + 1, :]).astype(bf16), vj)
            second = dot((xt[...] * ew[2 * j + 1 : 2 * j + 2, :]).astype(bf16), vj)
            state = lane_pair(first, second).astype(bf16)

            @pl.when(c == j // 2)
            def _():
                mine_ref[base + j % 2] = state

            @pl.when(c != j // 2)
            def _():
                sib_ref[base + j % 2] = state


def pair_coef(coef, at, i):
    j = i % 2
    return coef[at : at + 1, 128 * j : 128 * j + 128]


def join_chip_body(pos, mine, other, coef, q):
    c = pos[2]
    for i in range(4):
        own, oth = mine[i].astype(f32), other[i].astype(f32)
        s0 = jnp.where(c == 0, own, oth)
        s1 = jnp.where(c == 0, oth, own)
        if i < 2:
            q[i] = (pair_coef(coef, 1, i) * s0 + s1).astype(bf16)
        else:
            q[i] = (s0 + pair_coef(coef, 0, i) * s1).astype(bf16)


def join_row_body(pos, q, g1, g2, g3, coef, u, enter):
    for i in range(4):
        near, end = (2, 5) if i < 2 else (12, 15)
        row = pair_coef(coef, end, i) * q[i].astype(f32)
        reach = jnp.zeros((N, 128), f32)
        for d, g in ((1, g1), (2, g2), (3, g3)):
            val = g[i].astype(f32)
            row += pair_coef(coef, end + d, i) * val
            reach += pair_coef(coef, near + d - 1, i) * val
        u[i] = row.astype(bf16)
        enter[i] = reach


def join_rows_body(pos, enter, g1, g2, g3, mine, other, coef, own, give):
    c = pos[2]
    for i in range(4):
        near = 9 if i < 2 else 19
        chip = enter[i]
        for d, g in ((1, g1), (2, g2), (3, g3)):
            chip += pair_coef(coef, near + d - 1, i) * g[i].astype(f32)
        o, t = mine[i].astype(f32), other[i].astype(f32)
        if i < 2:
            e0 = chip
            e1 = pair_coef(coef, 0, i) * chip + jnp.where(c == 0, o, t)
        else:
            e0 = pair_coef(coef, 1, i) * chip + jnp.where(c == 0, t, o)
            e1 = chip
        own[i] = jnp.where(c == 0, e0, e1).astype(bf16)
        give[i] = jnp.where(c == 0, e1, e0).astype(bf16)


STATES = sds((4, N, 128), bf16)


def exchange(pos, mine, sib, coef):
    other = swap(sib)
    (q,) = call(join_chip_body, "join_chip", [STATES], (pos, mine, other, coef))
    got = [axis_hop(q, dx=d) for d in (1, 2, 3)]
    u, enter = call(
        join_row_body, "join_row", [STATES, sds((4, N, 128), f32)], (pos, q, *got, coef)
    )
    got = [axis_hop(u, dy=d) for d in (1, 2, 3)]
    own, give = call(
        join_rows_body, "join_rows", [STATES, STATES], (pos, enter, *got, mine, other, coef)
    )
    return own, swap(give)


def local_body(pos, v_ref, g_ref, b_ref, c_ref, a_ref, at_ref, mixed, grad):
    row, col = iota((T, T), 0), iota((T, T), 1)
    for vals, out, backward in ((g_ref, grad, True), (v_ref, mixed, False)):
        first, second = (b_ref, c_ref) if backward else (c_ref, b_ref)
        meet = dot(first[...], second[...], 1, 1)
        keep = (col >= row) if backward else (row >= col)
        for j in range(PAIRS):
            vj = vals[:, 128 * j : 128 * j + 128]
            parts = []
            for h in (2 * j, 2 * j + 1):
                spread = a_ref[:, h : h + 1] - at_ref[h : h + 1, :]
                if backward:
                    spread = -spread
                mix = jnp.exp(jnp.where(keep, spread, -1e30)) * meet
                parts.append(dot(mix.astype(bf16), vj))
            out[:, 128 * j : 128 * j + 128] = lane_pair(*parts)


def finish(c, base, local_ref, x_ref, eo_ref, mine_ref, sib_ref, j):
    at = base + j % 2
    state = jnp.where(c == j // 2, mine_ref[at].astype(f32), sib_ref[at].astype(f32)).astype(bf16)
    eo = lane_pair(eo_ref[:, 2 * j : 2 * j + 1], eo_ref[:, 2 * j + 1 : 2 * j + 2])
    return local_ref[:, 128 * j : 128 * j + 128] + eo * dot(x_ref[...], state)


def tokens_body(pos, local_ref, x_ref, eo_ref, mine_ref, sib_ref, isc, w_in, gb_ref, out, gs_ref):
    c = pos[2]
    for j in range(PAIRS):
        vals = finish(c, 2, local_ref, x_ref, eo_ref, mine_ref, sib_ref, j)
        at = slice(128 * j, 128 * j + 128)
        gb_ref[:, at] = vals.astype(bf16)
        gs_ref[:, at] = (vals * isc[:, at]).astype(bf16)

    def step(b, _):
        row = pl.multiple_of(b * W, W)
        total = dot(gs_ref[:, :256], w_in[0, pl.ds(row, W), :], 1, 1)
        total += dot(gs_ref[:, 256:], w_in[1, pl.ds(row, W), :], 1, 1)
        out[b] = total.astype(bf16)
        return 0

    lax.fori_loop(0, NZ, step, 0)


def store_total(pos, blocks, right, keep, send):
    y, x, c = pos[0], pos[1], pos[2]

    def step(b, _):
        part = dot(blocks[b], right[...], 0, 0).astype(bf16)
        for i in range(2):
            chip = b * 2 + i
            dy = lax.rem(chip // NX - y + NY, NY)
            dx = lax.rem(lax.rem(chip, NX) - x + NX, NX)
            left = part[256 * i : 256 * i + 256, :256]
            rest = part[256 * i : 256 * i + 256, 256:]

            @pl.when(c == 0)
            def _():
                keep[dx, dy] = left
                send[dy, dx] = rest

            @pl.when(c == 1)
            def _():
                keep[dy, dx] = rest
                send[dx, dy] = left

        return 0

    lax.fori_loop(0, NZ, step, 0)


def in_total_body(pos, blocks, gb, keep, send):
    store_total(pos, blocks, gb, keep, send)


def out_total_body(pos, blocks, local_ref, x_ref, eo_ref, mine_ref, sib_ref, keep, send, mb):
    for j in range(PAIRS):
        at = slice(128 * j, 128 * j + 128)
        vals = finish(pos[2], 0, local_ref, x_ref, eo_ref, mine_ref, sib_ref, j)
        mb[:, at] = vals.astype(bf16)
    store_total(pos, blocks, mb, keep, send)


TOTALS = [sds((4, 4, 256, 256), bf16)] * 2
MATMUL = 2 * T * D * W


def add(*parts):
    total = parts[0].astype(f32)
    for part in parts[1:]:
        total = total + part.astype(f32)
    return total


def scatter_seq(c, keep, send):
    came = swap(send)
    got = [hop(add(keep[d], came[d]).astype(bf16), d) for d in (1, 2, 3)]
    total = add(keep[0], came[0], *got)
    got = [hop(total[d].astype(bf16), d, True) for d in (1, 2, 3)]
    total = add(total[0], *got)
    upper, lower = total[:R], total[R:]
    mine = jnp.where(c == 0, upper, lower)
    theirs = swap(jnp.where(c == 0, lower, upper))
    return jnp.concatenate(
        [jnp.where(c == 0, mine, theirs), jnp.where(c == 0, theirs, mine)], axis=1
    )


def slopes_of(weight, step):
    ratios = weight.astype(f32) / step
    levels = jnp.floor(jnp.clip(ratios, -QMAX, QMAX) + 0.5)
    inside = jnp.abs(ratios) <= QMAX
    return jnp.where(inside, levels - ratios, levels), inside.astype(f32)


def per_device(
    tokens, grad_out, in_weight, in_scale, out_weight, out_scale, state_in, state_out, log_decay
):
    s = lax.axis_index("seq")
    z = lax.axis_index("tp")
    y, x, c = s // (NX * NC), (s // NC) % NX, s % NC
    pos = jnp.stack([y, x, c, z]).astype(jnp.int32)
    scale = in_scale[None, :]

    outs = [sds((2 * T, W), bf16)]
    outs += [sds((R + 16, 256), bf16)] * 2 + [sds((R, 256), bf16)] * 2
    outs += [sds((T, HP), f32), sds((HP, T), f32), sds((T, HP), f32), sds((T, HP), f32)]
    outs += [sds((HP, T), f32)] * 2 + [sds((N, T), f32)] * 2
    args = (
        pos, tokens, grad_out, in_weight, scale, out_weight,
        out_scale.reshape(NY * NX * NC, R), out_scale.reshape(NZ, W), log_decay, state_in, state_out,
    )
    merged, o_keep, o_give, i_keep, i_give, run, run_t, up, down, up_t, down_t, bt, ct = call(
        prep_body, "prep", outs, args
    )

    in_row = jnp.stack([i_keep, swap(i_give)])
    in_row = lax.all_gather(in_row, "seq", axis=0, tiled=True, axis_index_groups=FIRST)
    in_all = lax.all_gather(in_row, "seq", axis=0, tiled=True, axis_index_groups=SECOND)
    out_own = jnp.stack([o_keep, swap(o_give)])
    out_row = jnp.stack([out_own] + [hop(out_own, -d) for d in (1, 2, 3)])
    out_all = [out_row] + [hop(out_row, -d, True) for d in (1, 2, 3)]
    blocks = gather_z(merged)
    out_theirs = [swap(v) for v in out_all]
    in_theirs = swap(in_all)

    outs = [sds((T, W), bf16)] * 2 + [STATES] * 2 + [sds((NZ, T, W), bf16)] * 2
    outs += [sds((2, D, 256), bf16), sds((24, 256), f32)]
    v, g, mine, sib, cots, feats, w_in, coef = call(
        project_body,
        "project",
        outs,
        (pos, *blocks, *out_all, *out_theirs, in_all, in_theirs, scale, up_t, down_t, bt, ct),
        2 * MATMUL,
        [pltpu.VMEM((2, D, 256), bf16), pltpu.VMEM((T, W), f32), pltpu.VMEM((32, 256), f32)],
    )
    own, came = exchange(pos, mine, sib, coef)
    mixed, grad = call(
        local_body,
        "local",
        [sds((T, W), f32)] * 2,
        (pos, v, g, state_in, state_out, run, run_t),
        10**9,
    )
    wide = [pltpu.VMEM((T, W), bf16)]
    gb, parts = call(
        tokens_body,
        "token_parts",
        [sds((T, W), bf16), sds((NZ, T, W), bf16)],
        (pos, grad, state_in, down, own, came, scale, w_in),
        MATMUL,
        wide,
    )
    grad_tokens = lax.psum_scatter(
        parts.reshape(NZ * T, W), "tp", scatter_dimension=0, tiled=True
    )
    in_total = scatter_seq(c, *call(in_total_body, "in_parts", TOTALS, (pos, feats, gb), MATMUL))
    out_total = scatter_seq(
        c,
        *call(
            out_total_body,
            "out_parts",
            TOTALS,
            (pos, cots, mixed, state_out, up, own, came),
            MATMUL,
            wide,
        ),
    )
    scale_rows = lax.dynamic_slice_in_dim(out_scale, s * R, R)[:, None]
    out_total = out_total / scale_rows

    in_slopes, in_inside = slopes_of(in_weight, scale)
    out_slopes, out_inside = slopes_of(out_weight, scale_rows)
    in_sum = jnp.sum(in_total * in_slopes, axis=0)[None]
    for bits in (1, 2, 4, 8, 16):
        in_sum = in_sum + seq_xor(in_sum, bits)
    out_sum = jnp.sum(out_total * out_slopes, axis=1)[None]
    for bits in (1, 2, 4):
        out_sum = out_sum + z_xor(out_sum, bits)
    return (
        grad_tokens,
        in_total * in_inside,
        in_sum[0] / jnp.sqrt(f32(D * QMAX)),
        out_total * out_inside,
        out_sum[0] / jnp.sqrt(f32(HEADS * HEAD_DIM * QMAX)),
    )


def solution(mesh):
    placed = (
        P("seq", "tp"),
        P("seq", "tp"),
        P("seq", "tp"),
        P("tp"),
        P("seq", "tp"),
        P(),
        P("seq", None),
        P("seq", None),
        P("seq", "tp"),
    )
    return jax.shard_map(
        per_device,
        mesh=mesh,
        in_specs=placed,
        out_specs=(P("seq", "tp"), P("seq", "tp"), P("tp"), P("seq", "tp"), P("seq")),
        check_vma=False,
    )
```

```python
import jax
import jax.numpy as jnp
from jax import lax
from jax.experimental import pallas as pl
from jax.experimental.pallas import tpu as pltpu
from jax.sharding import PartitionSpec as P

D = 4096
HEADS = 64
HEAD_DIM = 64
QMAX = 7

NY, NX, NC, NZ = 4, 4, 2, 8
T = 256
W = 512
R = 128
N = 128
HP = 8
PAIRS = 4

f32 = jnp.float32
bf16 = jnp.bfloat16


def seq_at(y, x, c):
    return ((y % NY) * NX + x % NX) * NC + c % NC


def hop(v, d, second=False):
    pairs = []
    for y in range(NY):
        for x in range(NX):
            for c in range(NC):
                along_x = (c == 0) != second
                to = seq_at(y, x + d, c) if along_x else seq_at(y + d, x, c)
                pairs.append((seq_at(y, x, c), to))
    return lax.ppermute(v, "seq", pairs)


def axis_hop(v, dy=0, dx=0):
    pairs = []
    for y in range(NY):
        for x in range(NX):
            for c in range(NC):
                pairs.append((seq_at(y, x, c), seq_at(y + dy, x + dx, c)))
    return lax.ppermute(v, "seq", pairs)


def seq_xor(v, bits):
    return lax.ppermute(v, "seq", [(s, s ^ bits) for s in range(NY * NX * NC)])


def swap(v):
    return seq_xor(v, 1)


def z_hop(v, d):
    return lax.ppermute(v, "tp", [(z, (z + d) % NZ) for z in range(NZ)])


def z_xor(v, b):
    return lax.ppermute(v, "tp", [(z, z ^ b) for z in range(NZ)])


def gather_z(own):
    r1 = z_hop(own, 1)
    l1 = z_hop(own, -1)
    r2 = z_hop(r1, 1)
    l2 = z_hop(l1, -1)
    r3 = z_hop(r2, 1)
    l3 = z_hop(l2, -1)
    top = z_hop(r3[:T], 1)
    bot = z_hop(l3[T:], -1)
    return [own, l1, l2, l3, r3, r2, r1, top, bot]


RELATIVE = (0, 1, 2, 3, 5, 6, 7)
smem = pl.BlockSpec(memory_space=pltpu.SMEM)
vmem = pl.BlockSpec(memory_space=pltpu.VMEM)


def sds(shape, dtype):
    return jax.ShapeDtypeStruct(shape, dtype)


def call(body, name, outs, args, flops=10**6, scratch=(), away=0):
    nbytes = sum(a.size * a.dtype.itemsize for a in args)
    nbytes += sum(o.size * o.dtype.itemsize for o in outs)
    return pl.pallas_call(
        body,
        out_shape=outs,
        in_specs=[smem] + [pl.BlockSpec(memory_space=pl.ANY)] * away + [vmem] * (len(args) - 1 - away),
        out_specs=[vmem] * len(outs),
        scratch_shapes=scratch,
        compiler_params=pltpu.CompilerParams(vmem_limit_bytes=56 * 2**20),
        cost_estimate=pl.CostEstimate(flops=flops, bytes_accessed=nbytes, transcendentals=0),
        name=name,
    )(*args)


def dot(a, b, ca=1, cb=0):
    return lax.dot_general(a, b, (((ca,), (cb,)), ((), ())), preferred_element_type=f32)


def iota(shape, dim):
    return lax.broadcasted_iota(jnp.int32, shape, dim)


def lane_pair(first, second):
    return jnp.where(iota((1, 128), 1) < HEAD_DIM, first, second)


def split3(v):
    hi = v.astype(bf16)
    rest = v - hi.astype(f32)
    mid = rest.astype(bf16)
    return hi, mid, (rest - mid.astype(f32)).astype(bf16)


def levels_of(weight, step):
    ratios = weight.astype(f32) / step
    return jnp.floor(jnp.clip(ratios, -QMAX, QMAX) + 0.5)


def prep_body(
    pos, tok, go, iw, isc, ow, os_rows, os_cols, ld, b_ref, c_ref,
    merged, o_keep, o_give, i_levels, run, run_t, up, down, up_t, down_t, bt, ct,
):
    c, z = pos[2], pos[3]
    s = (pos[0] * NX + pos[1]) * NC + c
    merged[:T, :] = (go[...].astype(f32) * os_cols[pl.ds(z, 1), :]).astype(bf16)
    merged[T:, :] = tok[...]
    square = (R, R)
    eye = iota(square, 0) == iota(square, 1)
    step = jnp.sum(jnp.where(eye, os_rows[pl.ds(s, 1), :], 0.0), axis=1, keepdims=True)
    out_lv = levels_of(ow[...], step).astype(bf16)
    i_levels[...] = levels_of(iw[...], isc[...]).astype(bf16)
    for core in range(2):
        mine, other = slice(256 * core, 256 * core + 256), slice(256 - 256 * core, 512 - 256 * core)

        @pl.when(c == core)
        def _():
            o_keep[0:R, :] = out_lv[:, mine]
            o_give[0:R, :] = out_lv[:, other]

    parts = split3(ld[...])
    tri = (iota((T, T), 0) >= iota((T, T), 1)).astype(bf16)
    cum = dot(tri, parts[0]) + dot(tri, parts[1]) + dot(tri, parts[2])
    cum_t = sum(dot(p, tri, 0, 1) for p in parts)
    total = cum[T - 1 : T, :]
    run[...] = cum
    run_t[...] = cum_t
    up[...] = jnp.exp(cum)
    down[...] = jnp.exp(total - cum)
    up_t[...] = jnp.exp(cum_t)
    down_t[...] = jnp.exp(cum_t[:, T - 1 : T] - cum_t)
    lane = iota((1, 256), 1) // HEAD_DIM
    rows = []
    for half in range(2):
        spread = jnp.zeros((1, 256), f32)
        for h in range(4):
            spread = jnp.where(lane == h, total[:, 4 * half + h : 4 * half + h + 1], spread)
        rows += [p.astype(f32) for p in split3(spread)]
    tile_row = iota((16, 256), 0)
    tile = jnp.zeros((16, 256), f32)
    for i, row in enumerate(rows):
        tile = jnp.where(tile_row == i, row, tile)
    o_keep[R:, :] = tile.astype(bf16)
    o_give[R:, :] = tile.astype(bf16)
    bt[...] = b_ref[...].astype(f32).T
    ct[...] = c_ref[...].astype(f32).T


def place(c, core_of, y, x, first, second):
    ch_y = jnp.where(core_of == 0, second, first)
    ch_x = jnp.where(core_of == 0, first, second)
    return lax.rem(y + ch_y, NY) * NX + lax.rem(x + ch_x, NX)


def assemble_body(pos, *refs):
    mine, theirs = refs[:4], refs[4:8]
    w_out, coef, table = refs[8:]
    y, x, c = pos[0], pos[1], pos[2]

    def copy(side, pieces, half):
        for e in range(4):

            def step(d, _):
                core = lax.rem(c + side, 2)
                chip = place(c, core, y, x, d, e)
                for r in range(2):
                    s = chip * NC + lax.rem(core + r, 2)
                    row = pl.multiple_of(s * R, R)
                    w_out[pl.ds(row, R), 256 * half : 256 * half + 256] = pieces[e][d, r, 0:R, :]
                    if side == 0:
                        tile = pieces[e][d, r, R:, :].astype(f32)
                        low = tile[0:1] + tile[1:2] + tile[2:3]
                        high = tile[3:4] + tile[4:5] + tile[5:6]
                        table[pl.ds(s, 1), :] = jnp.where(c == 0, low, high)
                return 0

            lax.fori_loop(0, 4, step, 0)

    for side, pieces in ((0, mine), (1, theirs)):
        for half in range(2):
            pl.when(lax.rem(c + side, 2) == half)(lambda: copy(side, pieces, half))

    chip0, row0 = (y * NX + x) * NC, y * NX * NC
    number = iota((NY * NX * NC, 1), 0)
    totals = table[...]

    def between(at, first, last, ok=None):
        inside = (number >= first) & (number <= last)
        value = jnp.exp(jnp.sum(jnp.where(inside, totals, 0.0), axis=0, keepdims=True))
        if ok is not None:
            value = jnp.where(ok, value, 0.0)
        coef[at : at + 1, :] = value

    between(0, chip0, chip0)
    between(1, chip0 + 1, chip0 + 1)
    for d in range(4):
        src = lax.rem(x - d + NX, NX)
        between(5 + d, row0 + src * NC + 2, row0 + NX * NC - 1)
        between(15 + d, row0, row0 + src * NC - 1)
        if d:
            between(1 + d, row0 + src * NC + 2, chip0 - 1, src < x)
            between(11 + d, chip0 + 2, row0 + src * NC - 1, src > x)
            src = lax.rem(y - d + NY, NY)
            between(8 + d, (src + 1) * NX * NC, chip0 - 1, src < y)
            between(18 + d, chip0 + 2, src * NX * NC - 1, src > y)
    coef[22:24, :] = jnp.zeros((2, 256), f32)


def fetch(blocks, into, sems, first, rows):
    copies = []
    for k, ref in zip(RELATIVE, blocks[:7]):
        copies.append(pltpu.make_async_copy(ref.at[first : first + rows], into.at[k], sems.at[k]))
    if rows == 2 * T:
        copies.append(pltpu.make_async_copy(blocks[7], into.at[4, 0:T], sems.at[4]))
        copies.append(pltpu.make_async_copy(blocks[8], into.at[4, T : 2 * T], sems.at[8]))
    else:
        copies.append(pltpu.make_async_copy(blocks[7 if first == 0 else 8], into.at[4], sems.at[4]))
    for copy in copies:
        copy.start()
    return copies


def project_body(pos, *refs):
    blocks = refs[:9]
    w_out, w_in, isc, up_t, down_t, bt, ct = refs[9:16]
    v_ref, g_ref, mine_ref, sib_ref = refs[16:20]
    held, wo, wi, acc_g, acc_v, sems, w_sems = refs[20:]
    c, z = pos[2], pos[3]
    copies = []
    for k in range(NZ):
        row = pl.multiple_of(lax.rem(z + k, NZ) * W, W)
        for i, (src, dst) in enumerate(((w_out, wo), (w_in, wi))):
            copy = pltpu.make_async_copy(src.at[pl.ds(row, W), :], dst.at[k], w_sems.at[i, k])
            copy.start()
            copies.append(copy)
    copies += fetch(blocks, held, sems, 0, 2 * T)
    acc_g[...] = jnp.zeros((T, W), f32)
    acc_v[...] = jnp.zeros((T, W), f32)
    for copy in copies:
        copy.wait()

    def step(k, _):
        acc_g[...] += dot(held[k, :T, :], wo[k])
        acc_v[...] += dot(held[k, T:, :], wi[k])
        return 0

    lax.fori_loop(0, NZ, step, 0)
    g_ref[...] = acc_g[...].astype(bf16)
    v_ref[...] = (acc_v[...] * isc[...]).astype(bf16)

    for base, vals, xt, ew in ((0, v_ref, bt, down_t), (2, g_ref, ct, up_t)):
        for j in range(PAIRS):
            vj = vals[:, 128 * j : 128 * j + 128]
            first = dot((xt[...] * ew[2 * j : 2 * j + 1, :]).astype(bf16), vj)
            second = dot((xt[...] * ew[2 * j + 1 : 2 * j + 2, :]).astype(bf16), vj)
            state = lane_pair(first, second).astype(bf16)

            @pl.when(c == j // 2)
            def _():
                mine_ref[base + j % 2] = state

            @pl.when(c != j // 2)
            def _():
                sib_ref[base + j % 2] = state


def pair_coef(coef, at, i):
    j = i % 2
    return coef[at : at + 1, 128 * j : 128 * j + 128]


def join_chip_body(pos, mine, other, coef, q):
    c = pos[2]
    for i in range(4):
        own, oth = mine[i].astype(f32), other[i].astype(f32)
        s0 = jnp.where(c == 0, own, oth)
        s1 = jnp.where(c == 0, oth, own)
        if i < 2:
            q[i] = (pair_coef(coef, 1, i) * s0 + s1).astype(bf16)
        else:
            q[i] = (s0 + pair_coef(coef, 0, i) * s1).astype(bf16)


def join_row_body(pos, q, g1, g2, g3, coef, u, enter):
    for i in range(4):
        near, end = (2, 5) if i < 2 else (12, 15)
        row = pair_coef(coef, end, i) * q[i].astype(f32)
        reach = jnp.zeros((N, 128), f32)
        for d, g in ((1, g1), (2, g2), (3, g3)):
            val = g[i].astype(f32)
            row += pair_coef(coef, end + d, i) * val
            reach += pair_coef(coef, near + d - 1, i) * val
        u[i] = row.astype(bf16)
        enter[i] = reach


def join_rows_body(pos, enter, g1, g2, g3, mine, other, coef, own, give):
    c = pos[2]
    for i in range(4):
        near = 9 if i < 2 else 19
        chip = enter[i]
        for d, g in ((1, g1), (2, g2), (3, g3)):
            chip += pair_coef(coef, near + d - 1, i) * g[i].astype(f32)
        o, t = mine[i].astype(f32), other[i].astype(f32)
        if i < 2:
            e0 = chip
            e1 = pair_coef(coef, 0, i) * chip + jnp.where(c == 0, o, t)
        else:
            e0 = pair_coef(coef, 1, i) * chip + jnp.where(c == 0, t, o)
            e1 = chip
        own[i] = jnp.where(c == 0, e0, e1).astype(bf16)
        give[i] = jnp.where(c == 0, e1, e0).astype(bf16)


STATES = sds((4, N, 128), bf16)


def exchange(pos, mine, sib, coef):
    other = swap(sib)
    (q,) = call(join_chip_body, "join_chip", [STATES], (pos, mine, other, coef))
    got = [axis_hop(q, dx=d) for d in (1, 2, 3)]
    u, enter = call(
        join_row_body, "join_row", [STATES, sds((4, N, 128), f32)], (pos, q, *got, coef)
    )
    got = [axis_hop(u, dy=d) for d in (1, 2, 3)]
    own, give = call(
        join_rows_body, "join_rows", [STATES, STATES], (pos, enter, *got, mine, other, coef)
    )
    return own, swap(give)


def local_body(pos, v_ref, g_ref, b_ref, c_ref, a_ref, at_ref, mixed, grad):
    row, col = iota((T, T), 0), iota((T, T), 1)
    head = iota((1, HP), 1)
    for vals, out, backward in ((g_ref, grad, True), (v_ref, mixed, False)):
        first, second = (b_ref, c_ref) if backward else (c_ref, b_ref)
        meet = dot(first[...], second[...], 1, 1)
        keep = (col >= row) if backward else (row >= col)

        def step(j, _):
            at = pl.ds(pl.multiple_of(128 * j, 128), 128)
            vj = vals[:, at]
            parts = []
            for i in range(2):
                h = 2 * j + i
                down = jnp.sum(jnp.where(head == h, a_ref[...], 0.0), axis=1, keepdims=True)
                spread = down - at_ref[pl.ds(h, 1), :]
                if backward:
                    spread = -spread
                mix = jnp.exp(jnp.where(keep, spread, -1e30)) * meet
                parts.append(dot(mix.astype(bf16), vj))
            out[:, at] = lane_pair(*parts)
            return 0

        lax.fori_loop(0, PAIRS, step, 0)


def finish(c, base, local_ref, x_ref, eo_ref, mine_ref, sib_ref, j):
    at = base + j % 2
    state = jnp.where(c == j // 2, mine_ref[at].astype(f32), sib_ref[at].astype(f32)).astype(bf16)
    eo = lane_pair(eo_ref[:, 2 * j : 2 * j + 1], eo_ref[:, 2 * j + 1 : 2 * j + 2])
    return local_ref[:, 128 * j : 128 * j + 128] + eo * dot(x_ref[...], state)


def tokens_body(pos, local_ref, x_ref, eo_ref, mine_ref, sib_ref, isc, w_in, gb_ref, out, gs_ref):
    c = pos[2]
    for j in range(PAIRS):
        vals = finish(c, 2, local_ref, x_ref, eo_ref, mine_ref, sib_ref, j)
        at = slice(128 * j, 128 * j + 128)
        gb_ref[:, at] = vals.astype(bf16)
        gs_ref[:, at] = (vals * isc[:, at]).astype(bf16)

    def step(b, _):
        row = pl.multiple_of(b * W, W)
        out[b] = dot(gs_ref[...], w_in[pl.ds(row, W), :], 1, 1).astype(bf16)
        return 0

    lax.fori_loop(0, NZ, step, 0)


def store_total(pos, held, right, keep, send):
    y, x, c, z = pos[0], pos[1], pos[2], pos[3]

    def step(k, _):
        part = dot(held[k], right[...], 0, 0).astype(bf16)
        for i in range(2):
            chip = lax.rem(z + k, NZ) * 2 + i
            dy = lax.rem(chip // NX - y + NY, NY)
            dx = lax.rem(lax.rem(chip, NX) - x + NX, NX)
            left = part[256 * i : 256 * i + 256, :256]
            rest = part[256 * i : 256 * i + 256, 256:]

            @pl.when(c == 0)
            def _():
                keep[dx, dy] = left
                send[dy, dx] = rest

            @pl.when(c == 1)
            def _():
                keep[dy, dx] = rest
                send[dx, dy] = left

        return 0

    lax.fori_loop(0, NZ, step, 0)


def in_total_body(pos, *refs):
    gb, keep, send, held, sems = refs[9:]
    for copy in fetch(refs[:9], held, sems, T, T):
        copy.wait()
    store_total(pos, held, gb, keep, send)


def out_total_body(pos, *refs):
    local_ref, x_ref, eo_ref, mine_ref, sib_ref, keep, send, held, sems, mb = refs[9:]
    copies = fetch(refs[:9], held, sems, 0, T)
    for j in range(PAIRS):
        at = slice(128 * j, 128 * j + 128)
        vals = finish(pos[2], 0, local_ref, x_ref, eo_ref, mine_ref, sib_ref, j)
        mb[:, at] = vals.astype(bf16)
    for copy in copies:
        copy.wait()
    store_total(pos, held, mb, keep, send)


TOTALS = [sds((4, 4, 256, 256), bf16)] * 2
MATMUL = 2 * T * D * W


def add(*parts):
    total = parts[0].astype(f32)
    for part in parts[1:]:
        total = total + part.astype(f32)
    return total


def scatter_seq(c, keep, send):
    came = swap(send)
    far = add(keep[2], came[2]).astype(bf16)
    right = hop(far[:2], 1)
    left = hop(far[2:], -1)
    near = jnp.concatenate([add(keep[1, :2], came[1, :2], right), add(keep[1, 2:], came[1, 2:])])
    back = jnp.concatenate([add(keep[3, :2], came[3, :2]), add(keep[3, 2:], came[3, 2:], left)])
    total = add(keep[0], came[0], hop(near.astype(bf16), 1), hop(back.astype(bf16), -1))
    got = [hop(total[d].astype(bf16), d, True) for d in (1, 2, 3)]
    total = add(total[0], *got)
    upper, lower = total[:R], total[R:]
    mine = jnp.where(c == 0, upper, lower)
    theirs = swap(jnp.where(c == 0, lower, upper))
    return jnp.concatenate(
        [jnp.where(c == 0, mine, theirs), jnp.where(c == 0, theirs, mine)], axis=1
    )


def slopes_of(weight, step):
    ratios = weight.astype(f32) / step
    levels = jnp.floor(jnp.clip(ratios, -QMAX, QMAX) + 0.5)
    inside = jnp.abs(ratios) <= QMAX
    return jnp.where(inside, levels - ratios, levels), inside.astype(f32)


def per_device(
    tokens, grad_out, in_weight, in_scale, out_weight, out_scale, state_in, state_out, log_decay
):
    s = lax.axis_index("seq")
    z = lax.axis_index("tp")
    y, x, c = s // (NX * NC), (s // NC) % NX, s % NC
    pos = jnp.stack([y, x, c, z]).astype(jnp.int32)
    scale = in_scale[None, :]

    outs = [sds((2 * T, W), bf16)]
    outs += [sds((R + 16, 256), bf16)] * 2 + [sds((R, W), bf16)]
    outs += [sds((T, HP), f32), sds((HP, T), f32), sds((T, HP), f32), sds((T, HP), f32)]
    outs += [sds((HP, T), f32)] * 2 + [sds((N, T), f32)] * 2
    args = (
        pos, tokens, grad_out, in_weight, scale, out_weight,
        out_scale.reshape(NY * NX * NC, R), out_scale.reshape(NZ, W), log_decay, state_in, state_out,
    )
    merged, o_keep, o_give, i_levels, run, run_t, up, down, up_t, down_t, bt, ct = call(
        prep_body, "prep", outs, args
    )

    w_in = lax.all_gather(i_levels, "seq", axis=0, tiled=True)
    out_own = jnp.stack([o_keep, swap(o_give)])
    out_row = jnp.stack([out_own] + [hop(out_own, -d) for d in (1, 2, 3)])
    out_all = [out_row] + [hop(out_row, -d, True) for d in (1, 2, 3)]
    blocks = gather_z(merged)
    w_out, coef = call(
        assemble_body,
        "assemble",
        [sds((D, W), bf16), sds((24, 256), f32)],
        (pos, *out_all, *[swap(v) for v in out_all]),
        10**6,
        [pltpu.VMEM((32, 256), f32)],
    )
    v, g, mine, sib = call(
        project_body,
        "project",
        [sds((T, W), bf16)] * 2 + [STATES] * 2,
        (pos, *blocks, w_out, w_in, scale, up_t, down_t, bt, ct),
        2 * MATMUL,
        [pltpu.VMEM((NZ, 2 * T, W), bf16)]
        + [pltpu.VMEM((NZ, W, W), bf16)] * 2
        + [pltpu.VMEM((T, W), f32)] * 2
        + [pltpu.SemaphoreType.DMA((9,)), pltpu.SemaphoreType.DMA((2, NZ))],
        away=11,
    )
    own, came = exchange(pos, mine, sib, coef)
    mixed, grad = call(
        local_body,
        "local",
        [sds((T, W), f32)] * 2,
        (pos, v, g, state_in, state_out, run, run_t),
        10**9,
    )
    wide = [pltpu.VMEM((T, W), bf16)]
    gb, parts = call(
        tokens_body,
        "token_parts",
        [sds((T, W), bf16), sds((NZ, T, W), bf16)],
        (pos, grad, state_in, down, own, came, scale, w_in),
        MATMUL,
        wide,
    )
    grad_tokens = lax.psum_scatter(
        parts.reshape(NZ * T, W), "tp", scatter_dimension=0, tiled=True
    )
    held = [pltpu.VMEM((NZ, T, W), bf16), pltpu.SemaphoreType.DMA((9,))]
    in_total = scatter_seq(
        c, *call(in_total_body, "in_parts", TOTALS, (pos, *blocks, gb), MATMUL, held, away=9)
    )
    out_total = scatter_seq(
        c,
        *call(
            out_total_body,
            "out_parts",
            TOTALS,
            (pos, *blocks, mixed, state_out, up, own, came),
            MATMUL,
            held + wide,
            away=9,
        ),
    )
    scale_rows = lax.dynamic_slice_in_dim(out_scale, s * R, R)[:, None]
    out_total = out_total / scale_rows

    in_slopes, in_inside = slopes_of(in_weight, scale)
    out_slopes, out_inside = slopes_of(out_weight, scale_rows)
    in_sum = jnp.sum(in_total * in_slopes, axis=0)[None]
    for bits in (1, 2, 4, 8, 16):
        in_sum = in_sum + seq_xor(in_sum, bits)
    out_sum = jnp.sum(out_total * out_slopes, axis=1)[None]
    for bits in (1, 2, 4):
        out_sum = out_sum + z_xor(out_sum, bits)
    return (
        grad_tokens,
        in_total * in_inside,
        in_sum[0] / jnp.sqrt(f32(D * QMAX)),
        out_total * out_inside,
        out_sum[0] / jnp.sqrt(f32(HEADS * HEAD_DIM * QMAX)),
    )


def solution(mesh):
    placed = (
        P("seq", "tp"),
        P("seq", "tp"),
        P("seq", "tp"),
        P("tp"),
        P("seq", "tp"),
        P(),
        P("seq", None),
        P("seq", None),
        P("seq", "tp"),
    )
    return jax.shard_map(
        per_device,
        mesh=mesh,
        in_specs=placed,
        out_specs=(P("seq", "tp"), P("seq", "tp"), P("tp"), P("seq", "tp"), P("seq")),
        check_vma=False,
    )
```

```python
import functools

import jax
import jax.numpy as jnp
from jax import lax
from jax.experimental import pallas as pl
from jax.experimental.pallas import tpu as pltpu
from jax.sharding import PartitionSpec as P

D = 4096
HEADS = 64
HEAD_DIM = 64
QMAX = 7

NY, NX, NC, NZ = 4, 4, 2, 8
T = 256
W = 512
R = 128
N = 128
HP = 8
PAIRS = 4

f32 = jnp.float32
bf16 = jnp.bfloat16


def seq_at(y, x, c):
    return ((y % NY) * NX + x % NX) * NC + c % NC


def hop(v, d, second=False):
    pairs = []
    for y in range(NY):
        for x in range(NX):
            for c in range(NC):
                along_x = (c == 0) != second
                to = seq_at(y, x + d, c) if along_x else seq_at(y + d, x, c)
                pairs.append((seq_at(y, x, c), to))
    return lax.ppermute(v, "seq", pairs)


def axis_hop(v, dy=0, dx=0):
    pairs = []
    for y in range(NY):
        for x in range(NX):
            for c in range(NC):
                pairs.append((seq_at(y, x, c), seq_at(y + dy, x + dx, c)))
    return lax.ppermute(v, "seq", pairs)


def seq_xor(v, bits):
    return lax.ppermute(v, "seq", [(s, s ^ bits) for s in range(NY * NX * NC)])


def swap(v):
    return seq_xor(v, 1)


def z_hop(v, d):
    return lax.ppermute(v, "tp", [(z, (z + d) % NZ) for z in range(NZ)])


def z_xor(v, b):
    return lax.ppermute(v, "tp", [(z, z ^ b) for z in range(NZ)])


FIRST = [[seq_at(y, x, 0) for x in range(NX)] for y in range(NY)] + [
    [seq_at(y, x, 1) for y in range(NY)] for x in range(NX)
]


def gather_z(own):
    r1 = z_hop(own, 1)
    l1 = z_hop(own, -1)
    r2 = z_hop(r1, 1)
    l2 = z_hop(l1, -1)
    r3 = z_hop(r2, 1)
    l3 = z_hop(l2, -1)
    top = z_hop(r3[:T], 1)
    bot = z_hop(l3[T:], -1)
    return [own, l1, l2, l3, r3, r2, r1, top, bot]


RELATIVE = (0, 1, 2, 3, 5, 6, 7)
smem = pl.BlockSpec(memory_space=pltpu.SMEM)
vmem = pl.BlockSpec(memory_space=pltpu.VMEM)
anyw = pl.BlockSpec(memory_space=pl.ANY)


def sds(shape, dtype):
    return jax.ShapeDtypeStruct(shape, dtype)


def call(body, name, outs, args, flops=10**6, scratch=(), away=0, out_away=()):
    nbytes = sum(a.size * a.dtype.itemsize for a in args)
    nbytes += sum(o.size * o.dtype.itemsize for o in outs)
    return pl.pallas_call(
        body,
        out_shape=outs,
        in_specs=[smem] + [anyw] * away + [vmem] * (len(args) - 1 - away),
        out_specs=[anyw if i in out_away else vmem for i in range(len(outs))],
        scratch_shapes=scratch,
        compiler_params=pltpu.CompilerParams(vmem_limit_bytes=56 * 2**20),
        cost_estimate=pl.CostEstimate(flops=flops, bytes_accessed=nbytes, transcendentals=0),
        name=name,
    )(*args)


def dot(a, b, ca=1, cb=0):
    return lax.dot_general(a, b, (((ca,), (cb,)), ((), ())), preferred_element_type=f32)


def iota(shape, dim):
    return lax.broadcasted_iota(jnp.int32, shape, dim)


def lane_pair(first, second):
    return jnp.where(iota((1, 128), 1) < HEAD_DIM, first, second)


def split3(v):
    hi = v.astype(bf16)
    rest = v - hi.astype(f32)
    mid = rest.astype(bf16)
    return hi, mid, (rest - mid.astype(f32)).astype(bf16)


def levels_of(weight, step):
    ratios = weight.astype(f32) / step
    return jnp.floor(jnp.clip(ratios, -QMAX, QMAX) + 0.5)


def prep_body(
    pos, tok, go, iw, isc, ow, os_rows, ld_t, b_ref, c_ref,
    merged, o_keep, o_give, i_levels, run, run_t, up, down, up_t, down_t, bt, ct,
):
    c, z = pos[2], pos[3]
    s = (pos[0] * NX + pos[1]) * NC + c
    for i in range(4):
        at = slice(R * i, R * i + R)
        step = os_rows[pl.ds(4 * z + i, 1), :]
        merged[:T, at] = (go[:, at].astype(f32) * step).astype(bf16)
    merged[T:, :] = tok[...]
    square = (R, R)
    eye = iota(square, 0) == iota(square, 1)
    step = jnp.sum(jnp.where(eye, os_rows[pl.ds(s, 1), :], 0.0), axis=1, keepdims=True)
    out_lv = levels_of(ow[...], step).astype(bf16)
    i_levels[...] = levels_of(iw[...], isc[...]).astype(bf16)
    for core in range(2):
        mine, other = slice(256 * core, 256 * core + 256), slice(256 - 256 * core, 512 - 256 * core)

        @pl.when(c == core)
        def _():
            o_keep[0:R, :] = out_lv[:, mine]
            o_give[0:R, :] = out_lv[:, other]

    parts = split3(ld_t[...])
    tri = (iota((T, T), 0) >= iota((T, T), 1)).astype(bf16)
    cum = sum(dot(tri, p, 1, 1) for p in parts)
    cum_t = sum(dot(p, tri, 1, 1) for p in parts)
    total = cum[T - 1 : T, :]
    run[...] = cum
    run_t[...] = cum_t
    up[...] = jnp.exp(cum)
    down[...] = jnp.exp(total - cum)
    up_t[...] = jnp.exp(cum_t)
    down_t[...] = jnp.exp(cum_t[:, T - 1 : T] - cum_t)
    lane = iota((1, 256), 1) // HEAD_DIM
    rows = []
    for half in range(2):
        spread = jnp.zeros((1, 256), f32)
        for h in range(4):
            spread = jnp.where(lane == h, total[:, 4 * half + h : 4 * half + h + 1], spread)
        rows += [p.astype(f32) for p in split3(spread)]
    tile_row = iota((16, 256), 0)
    tile = jnp.zeros((16, 256), f32)
    for i, row in enumerate(rows):
        tile = jnp.where(tile_row == i, row, tile)
    o_keep[R:, :] = tile.astype(bf16)
    o_give[R:, :] = tile.astype(bf16)
    bt[...] = b_ref[...].astype(f32).T
    ct[...] = c_ref[...].astype(f32).T


def place(c, core_of, y, x, first, second):
    ch_y = jnp.where(core_of == 0, second, first)
    ch_x = jnp.where(core_of == 0, first, second)
    return lax.rem(y + ch_y, NY) * NX + lax.rem(x + ch_x, NX)


def assemble_body(pos, *refs):
    mine, theirs = refs[:4], refs[4:8]
    w_out, coef, table = refs[8:]
    y, x, c = pos[0], pos[1], pos[2]

    def copy(side, pieces, half):
        for e in range(4):

            def step(d, _):
                core = lax.rem(c + side, 2)
                chip = place(c, core, y, x, d, e)
                for r in range(2):
                    s = chip * NC + lax.rem(core + r, 2)
                    row = pl.multiple_of(s * R, R)
                    w_out[pl.ds(row, R), 256 * half : 256 * half + 256] = pieces[e][d, r, 0:R, :]
                    if side == 0:
                        tile = pieces[e][d, r, R:, :].astype(f32)
                        low = tile[0:1] + tile[1:2] + tile[2:3]
                        high = tile[3:4] + tile[4:5] + tile[5:6]
                        table[pl.ds(s, 1), :] = jnp.where(c == 0, low, high)
                return 0

            lax.fori_loop(0, 4, step, 0)

    for side, pieces in ((0, mine), (1, theirs)):
        for half in range(2):
            pl.when(lax.rem(c + side, 2) == half)(lambda: copy(side, pieces, half))

    chip0, row0 = (y * NX + x) * NC, y * NX * NC
    number = iota((NY * NX * NC, 1), 0)
    totals = table[...]

    def between(at, first, last, ok=None):
        inside = (number >= first) & (number <= last)
        value = jnp.exp(jnp.sum(jnp.where(inside, totals, 0.0), axis=0, keepdims=True))
        if ok is not None:
            value = jnp.where(ok, value, 0.0)
        coef[at : at + 1, :] = value

    between(0, chip0, chip0)
    between(1, chip0 + 1, chip0 + 1)
    for d in range(4):
        src = lax.rem(x - d + NX, NX)
        between(5 + d, row0 + src * NC + 2, row0 + NX * NC - 1)
        between(15 + d, row0, row0 + src * NC - 1)
        if d:
            between(1 + d, row0 + src * NC + 2, chip0 - 1, src < x)
            between(11 + d, chip0 + 2, row0 + src * NC - 1, src > x)
            src = lax.rem(y - d + NY, NY)
            between(8 + d, (src + 1) * NX * NC, chip0 - 1, src < y)
            between(18 + d, chip0 + 2, src * NX * NC - 1, src > y)
    coef[22:24, :] = jnp.zeros((2, 256), f32)


ORDER = (0, 1, 7, 2, 6, 3, 5, 4)


def fetch(blocks, into, sems, first, rows):
    copies = {}
    for k, ref in zip(RELATIVE, blocks[:7]):
        copies[k] = [pltpu.make_async_copy(ref.at[first : first + rows], into.at[k], sems.at[k])]
    if rows == 2 * T:
        copies[4] = [
            pltpu.make_async_copy(blocks[7], into.at[4, 0:T], sems.at[4]),
            pltpu.make_async_copy(blocks[8], into.at[4, T : 2 * T], sems.at[8]),
        ]
    else:
        far = blocks[7 if first == 0 else 8]
        copies[4] = [pltpu.make_async_copy(far, into.at[4], sems.at[4])]
    return copies


def fetch_rows(z, src, into, sems):
    copies = {}
    for k in range(NZ):
        row = pl.multiple_of(lax.rem(z + k, NZ) * W, W)
        copies[k] = [pltpu.make_async_copy(src.at[pl.ds(row, W), :], into.at[k], sems.at[k])]
    return copies


def start(*groups):
    for k in ORDER:
        for group in groups:
            for copy in group[k]:
                copy.start()


def wait(k, *groups):
    for group in groups:
        for copy in group[k]:
            copy.wait()


def project_body(pos, *refs):
    blocks = refs[:9]
    w_out, w_in, isc, up_t, down_t, bt, ct = refs[9:16]
    v_ref, g_ref, mine_ref, sib_ref = refs[16:20]
    held, wo, wi, sems, out_sems, in_sems = refs[20:]
    c, z = pos[2], pos[3]
    groups = (
        fetch(blocks, held, sems, 0, 2 * T),
        fetch_rows(z, w_out, wo, out_sems),
        fetch_rows(z, w_in, wi, in_sems),
    )
    start(*groups)
    acc_g = acc_v = None
    for k in ORDER:
        wait(k, *groups)
        g, v = dot(held[k, :T, :], wo[k]), dot(held[k, T:, :], wi[k])
        acc_g = g if acc_g is None else acc_g + g
        acc_v = v if acc_v is None else acc_v + v
    g_ref[...] = acc_g.astype(bf16)
    v_ref[...] = (acc_v * isc[...]).astype(bf16)

    for base, vals, xt, ew in ((0, v_ref, bt, down_t), (2, g_ref, ct, up_t)):
        for j in range(PAIRS):
            vj = vals[:, 128 * j : 128 * j + 128]
            first = dot((xt[...] * ew[2 * j : 2 * j + 1, :]).astype(bf16), vj)
            second = dot((xt[...] * ew[2 * j + 1 : 2 * j + 2, :]).astype(bf16), vj)
            state = lane_pair(first, second).astype(bf16)

            @pl.when(c == j // 2)
            def _():
                mine_ref[base + j % 2] = state

            @pl.when(c != j // 2)
            def _():
                sib_ref[base + j % 2] = state


def pair_coef(coef, at, i):
    j = i % 2
    return coef[at : at + 1, 128 * j : 128 * j + 128]


def join_chip_body(pos, mine, other, coef, q):
    c = pos[2]
    for i in range(4):
        own, oth = mine[i].astype(f32), other[i].astype(f32)
        s0 = jnp.where(c == 0, own, oth)
        s1 = jnp.where(c == 0, oth, own)
        if i < 2:
            q[i] = (pair_coef(coef, 1, i) * s0 + s1).astype(bf16)
        else:
            q[i] = (s0 + pair_coef(coef, 0, i) * s1).astype(bf16)


def join_row_body(pos, q, g1, g2, g3, coef, u, enter):
    for i in range(4):
        near, end = (2, 5) if i < 2 else (12, 15)
        row = pair_coef(coef, end, i) * q[i].astype(f32)
        reach = jnp.zeros((N, 128), f32)
        for d, g in ((1, g1), (2, g2), (3, g3)):
            val = g[i].astype(f32)
            row += pair_coef(coef, end + d, i) * val
            reach += pair_coef(coef, near + d - 1, i) * val
        u[i] = row.astype(bf16)
        enter[i] = reach


def join_rows_body(pos, enter, g1, g2, g3, mine, other, coef, own, give):
    c = pos[2]
    for i in range(4):
        near = 9 if i < 2 else 19
        chip = enter[i]
        for d, g in ((1, g1), (2, g2), (3, g3)):
            chip += pair_coef(coef, near + d - 1, i) * g[i].astype(f32)
        o, t = mine[i].astype(f32), other[i].astype(f32)
        if i < 2:
            e0 = chip
            e1 = pair_coef(coef, 0, i) * chip + jnp.where(c == 0, o, t)
        else:
            e0 = pair_coef(coef, 1, i) * chip + jnp.where(c == 0, t, o)
            e1 = chip
        own[i] = jnp.where(c == 0, e0, e1).astype(bf16)
        give[i] = jnp.where(c == 0, e1, e0).astype(bf16)


STATES = sds((4, N, 128), bf16)


def exchange(pos, mine, sib, coef, first, second):
    other = swap(sib)
    (q,) = call(join_chip_body, "join_chip", [STATES], (pos, mine, other, coef))
    got = [axis_hop(q, dx=d) for d in (1, 2, 3)]
    *got, one = lax.optimization_barrier((*got, first()))
    u, enter = call(
        join_row_body, "join_row", [STATES, sds((4, N, 128), f32)], (pos, q, *got, coef)
    )
    got = [axis_hop(u, dy=d) for d in (1, 2, 3)]
    *got, two = lax.optimization_barrier((*got, second()))
    own, give = call(
        join_rows_body, "join_rows", [STATES, STATES], (pos, enter, *got, mine, other, coef)
    )
    return own, swap(give), one, two


def local_body(backward, pos, vals, b_ref, c_ref, a_ref, at_ref, out):
    row, col = iota((T, T), 0), iota((T, T), 1)
    first, second = (b_ref, c_ref) if backward else (c_ref, b_ref)
    meet = dot(first[...], second[...], 1, 1)
    keep = (col >= row) if backward else (row >= col)
    for j in range(PAIRS):
        vj = vals[:, 128 * j : 128 * j + 128]
        parts = []
        for h in (2 * j, 2 * j + 1):
            spread = a_ref[:, h : h + 1] - at_ref[h : h + 1, :]
            if backward:
                spread = -spread
            mix = jnp.exp(jnp.where(keep, spread, -1e30)) * meet
            parts.append(dot(mix.astype(bf16), vj))
        out[:, 128 * j : 128 * j + 128] = lane_pair(*parts)


def finish(c, base, local_ref, x_ref, eo_ref, mine_ref, sib_ref, j):
    at = base + j % 2
    state = jnp.where(c == j // 2, mine_ref[at].astype(f32), sib_ref[at].astype(f32)).astype(bf16)
    eo = lane_pair(eo_ref[:, 2 * j : 2 * j + 1], eo_ref[:, 2 * j + 1 : 2 * j + 2])
    return local_ref[:, 128 * j : 128 * j + 128] + eo * dot(x_ref[...], state)


def tokens_body(
    pos, w_in, local_ref, x_ref, eo_ref, mine_ref, sib_ref, isc,
    out, gb_ref, gs_ref, held, buf, in_sems, out_sems,
):
    c, z = pos[2], pos[3]
    rows = fetch_rows(z, w_in, held, in_sems)
    start(rows)
    for j in range(PAIRS):
        vals = finish(c, 2, local_ref, x_ref, eo_ref, mine_ref, sib_ref, j)
        at = slice(128 * j, 128 * j + 128)
        gb_ref[:, at] = vals.astype(bf16)
        gs_ref[:, at] = (vals * isc[:, at]).astype(bf16)
    copies = []
    for k in ORDER:
        wait(k, rows)
        buf[k] = dot(gs_ref[...], held[k], 1, 1).astype(bf16)
        copy = pltpu.make_async_copy(buf.at[k], out.at[lax.rem(z + k, NZ)], out_sems.at[k])
        copy.start()
        copies.append(copy)
    for copy in copies:
        copy.wait()


def store_total(relative, pos, blocks, held, right, keep, send, buf, out_sems):
    y, x, c, z = pos[0], pos[1], pos[2], pos[3]
    kept = pl.multiple_of(256 * c, 256)
    sent = pl.multiple_of(256 - 256 * c, 256)
    copies = []
    for k in ORDER:
        wait(k, blocks)
        buf[k] = dot(held[k], right[...], 0, 0).astype(bf16)
        for i in range(2):
            chip = lax.rem(z + k, NZ) * 2 + i
            cy, cx = chip // NX, lax.rem(chip, NX)
            dy, dx = lax.rem(cy - y + NY, NY), lax.rem(cx - x + NX, NX)
            fy, fx = (dy, dx) if relative else (cy, cx)
            rows = slice(256 * i, 256 * i + 256)
            mine = keep.at[jnp.where(c == 0, fx, fy), jnp.where(c == 0, dy, dx)]
            other = send.at[jnp.where(c == 0, fy, fx), jnp.where(c == 0, dx, dy)]
            for j, (at, to) in enumerate(((kept, mine), (sent, other))):
                copy = pltpu.make_async_copy(
                    buf.at[k, rows, pl.ds(at, 256)], to, out_sems.at[k, 2 * i + j]
                )
                copy.start()
                copies.append(copy)
    for copy in copies:
        copy.wait()


def in_total_body(pos, *refs):
    gb, keep, send, held, buf, sems, out_sems = refs[9:]
    blocks = fetch(refs[:9], held, sems, T, T)
    start(blocks)
    store_total(False, pos, blocks, held, gb, keep, send, buf, out_sems)


def out_total_body(pos, *refs):
    local_ref, x_ref, eo_ref, mine_ref, sib_ref, keep, send, held, buf, sems, out_sems, mb = refs[9:]
    blocks = fetch(refs[:9], held, sems, 0, T)
    start(blocks)
    for j in range(PAIRS):
        at = slice(128 * j, 128 * j + 128)
        vals = finish(pos[2], 0, local_ref, x_ref, eo_ref, mine_ref, sib_ref, j)
        mb[:, at] = vals.astype(bf16)
    store_total(True, pos, blocks, held, mb, keep, send, buf, out_sems)


TOTALS = [sds((4, 4, 256, 256), bf16)] * 2
MATMUL = 2 * T * D * W


def add(*parts):
    total = parts[0].astype(f32)
    for part in parts[1:]:
        total = total + part.astype(f32)
    return total


def scatter_rest(c, total):
    got = [hop(total[d].astype(bf16), d, True) for d in (1, 2, 3)]
    total = add(total[0], *got)
    upper, lower = total[:R], total[R:]
    mine = jnp.where(c == 0, upper, lower)
    theirs = swap(jnp.where(c == 0, lower, upper))
    return jnp.concatenate(
        [jnp.where(c == 0, mine, theirs), jnp.where(c == 0, theirs, mine)], axis=1
    )


def scatter_hops(c, keep, send):
    came = swap(send)
    far = add(keep[2], came[2]).astype(bf16)
    right = hop(far[:2], 1)
    left = hop(far[2:], -1)
    near = jnp.concatenate([add(keep[1, :2], came[1, :2], right), add(keep[1, 2:], came[1, 2:])])
    back = jnp.concatenate([add(keep[3, :2], came[3, :2]), add(keep[3, 2:], came[3, 2:], left)])
    total = add(keep[0], came[0], hop(near.astype(bf16), 1), hop(back.astype(bf16), -1))
    return scatter_rest(c, total)


def scatter_group(c, keep, send):
    both = add(keep, swap(send)).astype(bf16)
    total = lax.psum_scatter(
        both, "seq", scatter_dimension=0, tiled=True, axis_index_groups=FIRST
    )
    return scatter_rest(c, total[0])


def slopes_of(weight, step):
    ratios = weight.astype(f32) / step
    levels = jnp.floor(jnp.clip(ratios, -QMAX, QMAX) + 0.5)
    inside = jnp.abs(ratios) <= QMAX
    return jnp.where(inside, levels - ratios, levels), inside.astype(f32)


def per_device(
    tokens, grad_out, in_weight, in_scale, out_weight, out_scale, state_in, state_out, log_decay
):
    s = lax.axis_index("seq")
    z = lax.axis_index("tp")
    y, x, c = s // (NX * NC), (s // NC) % NX, s % NC
    pos = jnp.stack([y, x, c, z]).astype(jnp.int32)
    scale = in_scale[None, :]

    outs = [sds((2 * T, W), bf16)]
    outs += [sds((R + 16, 256), bf16)] * 2 + [sds((R, W), bf16)]
    outs += [sds((T, HP), f32), sds((HP, T), f32), sds((T, HP), f32), sds((T, HP), f32)]
    outs += [sds((HP, T), f32)] * 2 + [sds((N, T), f32)] * 2
    args = (
        pos, tokens, grad_out, in_weight, scale, out_weight,
        out_scale.reshape(NY * NX * NC, R), log_decay.T, state_in, state_out,
    )
    merged, o_keep, o_give, i_levels, run, run_t, up, down, up_t, down_t, bt, ct = call(
        prep_body, "prep", outs, args
    )

    w_in = lax.all_gather(i_levels, "seq", axis=0, tiled=True)
    out_own = jnp.stack([o_keep, swap(o_give)])
    out_row = jnp.stack([out_own] + [hop(out_own, -d) for d in (1, 2, 3)])
    out_all = [out_row] + [hop(out_row, -d, True) for d in (1, 2, 3)]
    blocks = gather_z(merged)
    w_out, coef = call(
        assemble_body,
        "assemble",
        [sds((D, W), bf16), sds((24, 256), f32)],
        (pos, *out_all, *[swap(v) for v in out_all]),
        10**6,
        [pltpu.VMEM((32, 256), f32)],
    )
    v, g, mine, sib = call(
        project_body,
        "project",
        [sds((T, W), bf16)] * 2 + [STATES] * 2,
        (pos, *blocks, w_out, w_in, scale, up_t, down_t, bt, ct),
        2 * MATMUL,
        [pltpu.VMEM((NZ, 2 * T, W), bf16)]
        + [pltpu.VMEM((NZ, W, W), bf16)] * 2
        + [pltpu.SemaphoreType.DMA((9,))] * 3,
        away=11,
    )
    def local(backward, vals, name):
        return call(
            functools.partial(local_body, backward),
            name,
            [sds((T, W), f32)],
            (pos, vals, state_in, state_out, run, run_t),
            10**9,
        )[0]

    own, came, grad, mixed = exchange(
        pos, mine, sib, coef,
        lambda: local(True, g, "grad_local"),
        lambda: local(False, v, "mixed_local"),
    )
    wide = [pltpu.VMEM((T, W), bf16)]
    sems = [pltpu.SemaphoreType.DMA((9,))] * 2
    parts, gb = call(
        tokens_body,
        "token_parts",
        [sds((NZ, T, W), bf16), sds((T, W), bf16)],
        (pos, w_in, grad, state_in, down, own, came, scale),
        MATMUL,
        wide + [pltpu.VMEM((NZ, W, W), bf16), pltpu.VMEM((NZ, T, W), bf16)] + sems,
        away=1,
        out_away=(0,),
    )
    pieces = lax.all_to_all(parts, "tp", 0, 0, tiled=True)
    held = [
        pltpu.VMEM((NZ, T, W), bf16),
        pltpu.VMEM((NZ, W, W), bf16),
        pltpu.SemaphoreType.DMA((9,)),
        pltpu.SemaphoreType.DMA((NZ, 4)),
    ]
    in_total = scatter_group(
        c,
        *call(
            in_total_body, "in_parts", TOTALS, (pos, *blocks, gb), MATMUL, held, 9, (0, 1)
        ),
    )
    out_total = scatter_hops(
        c,
        *call(
            out_total_body,
            "out_parts",
            TOTALS,
            (pos, *blocks, mixed, state_out, up, own, came),
            MATMUL,
            held + wide,
            9,
            (0, 1),
        ),
    )
    grad_tokens = add(*[pieces[i] for i in range(NZ)]).astype(bf16)
    scale_rows = lax.dynamic_slice_in_dim(out_scale, s * R, R)[:, None]
    out_total = out_total / scale_rows

    in_slopes, in_inside = slopes_of(in_weight, scale)
    out_slopes, out_inside = slopes_of(out_weight, scale_rows)
    in_sum = jnp.sum(in_total * in_slopes, axis=0)[None]
    for bits in (1, 2, 4, 8, 16):
        in_sum = in_sum + seq_xor(in_sum, bits)
    out_sum = jnp.sum(out_total * out_slopes, axis=1)[None]
    for bits in (1, 2, 4):
        out_sum = out_sum + z_xor(out_sum, bits)
    return (
        grad_tokens,
        in_total * in_inside,
        in_sum[0] / jnp.sqrt(f32(D * QMAX)),
        out_total * out_inside,
        out_sum[0] / jnp.sqrt(f32(HEADS * HEAD_DIM * QMAX)),
    )


def solution(mesh):
    placed = (
        P("seq", "tp"),
        P("seq", "tp"),
        P("seq", "tp"),
        P("tp"),
        P("seq", "tp"),
        P(),
        P("seq", None),
        P("seq", None),
        P("seq", "tp"),
    )
    return jax.shard_map(
        per_device,
        mesh=mesh,
        in_specs=placed,
        out_specs=(P("seq", "tp"), P("seq", "tp"), P("tp"), P("seq", "tp"), P("seq")),
        check_vma=False,
    )
```

```python
import functools

import jax
import jax.numpy as jnp
from jax import lax
from jax.experimental import pallas as pl
from jax.experimental.pallas import tpu as pltpu
from jax.sharding import PartitionSpec as P

D = 4096
HEADS = 64
HEAD_DIM = 64
QMAX = 7

NY, NX, NC, NZ = 4, 4, 2, 8
T = 256
W = 512
R = 128
N = 128
HP = 8
PAIRS = 4

f32 = jnp.float32
bf16 = jnp.bfloat16


def seq_at(y, x, c):
    return ((y % NY) * NX + x % NX) * NC + c % NC


def hop(v, d, second=False):
    pairs = []
    for y in range(NY):
        for x in range(NX):
            for c in range(NC):
                along_x = (c == 0) != second
                to = seq_at(y, x + d, c) if along_x else seq_at(y + d, x, c)
                pairs.append((seq_at(y, x, c), to))
    return lax.ppermute(v, "seq", pairs)


def axis_hop(v, dy=0, dx=0):
    pairs = []
    for y in range(NY):
        for x in range(NX):
            for c in range(NC):
                pairs.append((seq_at(y, x, c), seq_at(y + dy, x + dx, c)))
    return lax.ppermute(v, "seq", pairs)


def seq_xor(v, bits):
    return lax.ppermute(v, "seq", [(s, s ^ bits) for s in range(NY * NX * NC)])


def swap(v):
    return seq_xor(v, 1)


def z_hop(v, d):
    return lax.ppermute(v, "tp", [(z, (z + d) % NZ) for z in range(NZ)])


def z_xor(v, b):
    return lax.ppermute(v, "tp", [(z, z ^ b) for z in range(NZ)])


def gather_z(own):
    r1 = z_hop(own, 1)
    l1 = z_hop(own, -1)
    r2 = z_hop(r1, 1)
    l2 = z_hop(l1, -1)
    r3 = z_hop(r2, 1)
    l3 = z_hop(l2, -1)
    top = z_hop(r3[:T], 1)
    bot = z_hop(l3[T:], -1)
    return [own, l1, l2, l3, r3, r2, r1, top, bot]


RELATIVE = (0, 1, 2, 3, 5, 6, 7)
smem = pl.BlockSpec(memory_space=pltpu.SMEM)
vmem = pl.BlockSpec(memory_space=pltpu.VMEM)
anyw = pl.BlockSpec(memory_space=pl.ANY)


def sds(shape, dtype):
    return jax.ShapeDtypeStruct(shape, dtype)


def call(body, name, outs, args, flops=10**6, scratch=(), away=0, out_away=()):
    nbytes = sum(a.size * a.dtype.itemsize for a in args)
    nbytes += sum(o.size * o.dtype.itemsize for o in outs)
    return pl.pallas_call(
        body,
        out_shape=outs,
        in_specs=[smem] + [anyw] * away + [vmem] * (len(args) - 1 - away),
        out_specs=[anyw if i in out_away else vmem for i in range(len(outs))],
        scratch_shapes=scratch,
        compiler_params=pltpu.CompilerParams(vmem_limit_bytes=56 * 2**20),
        cost_estimate=pl.CostEstimate(flops=flops, bytes_accessed=nbytes, transcendentals=0),
        name=name,
    )(*args)


def dot(a, b, ca=1, cb=0):
    return lax.dot_general(a, b, (((ca,), (cb,)), ((), ())), preferred_element_type=f32)


def iota(shape, dim):
    return lax.broadcasted_iota(jnp.int32, shape, dim)


def lane_pair(first, second):
    return jnp.where(iota((1, 128), 1) < HEAD_DIM, first, second)


def split3(v):
    hi = v.astype(bf16)
    rest = v - hi.astype(f32)
    mid = rest.astype(bf16)
    return hi, mid, (rest - mid.astype(f32)).astype(bf16)


def levels_of(weight, step):
    ratios = weight.astype(f32) / step
    return jnp.floor(jnp.clip(ratios, -QMAX, QMAX) + 0.5)


def prep_body(
    pos, tok, go, iw, isc, ow, os_rows, ld_t, b_ref, c_ref,
    merged, o_keep, o_give, i_levels, run, run_t, up, down, up_t, down_t, bt, ct,
):
    c, z = pos[2], pos[3]
    s = (pos[0] * NX + pos[1]) * NC + c
    for i in range(4):
        at = slice(R * i, R * i + R)
        step = os_rows[pl.ds(4 * z + i, 1), :]
        merged[:T, at] = (go[:, at].astype(f32) * step).astype(bf16)
    merged[T:, :] = tok[...]
    square = (R, R)
    eye = iota(square, 0) == iota(square, 1)
    step = jnp.sum(jnp.where(eye, os_rows[pl.ds(s, 1), :], 0.0), axis=1, keepdims=True)
    out_lv = levels_of(ow[...], step).astype(bf16)
    i_levels[...] = levels_of(iw[...], isc[...]).astype(bf16)
    for core in range(2):
        mine, other = slice(256 * core, 256 * core + 256), slice(256 - 256 * core, 512 - 256 * core)

        @pl.when(c == core)
        def _():
            o_keep[0:R, :] = out_lv[:, mine]
            o_give[0:R, :] = out_lv[:, other]

    parts = split3(ld_t[...])
    tri = (iota((T, T), 0) >= iota((T, T), 1)).astype(bf16)
    cum = sum(dot(tri, p, 1, 1) for p in parts)
    cum_t = sum(dot(p, tri, 1, 1) for p in parts)
    total = cum[T - 1 : T, :]
    run[...] = cum
    run_t[...] = cum_t
    up[...] = jnp.exp(cum)
    down[...] = jnp.exp(total - cum)
    up_t[...] = jnp.exp(cum_t)
    down_t[...] = jnp.exp(cum_t[:, T - 1 : T] - cum_t)
    lane = iota((1, 256), 1) // HEAD_DIM
    rows = []
    for half in range(2):
        spread = jnp.zeros((1, 256), f32)
        for h in range(4):
            spread = jnp.where(lane == h, total[:, 4 * half + h : 4 * half + h + 1], spread)
        rows += [p.astype(f32) for p in split3(spread)]
    tile_row = iota((16, 256), 0)
    tile = jnp.zeros((16, 256), f32)
    for i, row in enumerate(rows):
        tile = jnp.where(tile_row == i, row, tile)
    o_keep[R:, :] = tile.astype(bf16)
    o_give[R:, :] = tile.astype(bf16)
    bt[...] = b_ref[...].astype(f32).T
    ct[...] = c_ref[...].astype(f32).T


def place(c, core_of, y, x, first, second):
    ch_y = jnp.where(core_of == 0, second, first)
    ch_x = jnp.where(core_of == 0, first, second)
    return lax.rem(y + ch_y, NY) * NX + lax.rem(x + ch_x, NX)


def assemble_body(pos, *refs):
    mine, theirs = refs[:4], refs[4:8]
    w_out, coef, table = refs[8:]
    y, x, c = pos[0], pos[1], pos[2]

    def copy(side, pieces, half):
        for e in range(4):

            def step(d, _):
                core = lax.rem(c + side, 2)
                chip = place(c, core, y, x, d, e)
                for r in range(2):
                    s = chip * NC + lax.rem(core + r, 2)
                    row = pl.multiple_of(s * R, R)
                    w_out[pl.ds(row, R), 256 * half : 256 * half + 256] = pieces[e][d, r, 0:R, :]
                    if side == 0:
                        tile = pieces[e][d, r, R:, :].astype(f32)
                        low = tile[0:1] + tile[1:2] + tile[2:3]
                        high = tile[3:4] + tile[4:5] + tile[5:6]
                        table[pl.ds(s, 1), :] = jnp.where(c == 0, low, high)
                return 0

            lax.fori_loop(0, 4, step, 0)

    for side, pieces in ((0, mine), (1, theirs)):
        for half in range(2):
            pl.when(lax.rem(c + side, 2) == half)(lambda: copy(side, pieces, half))

    chip0, row0 = (y * NX + x) * NC, y * NX * NC
    number = iota((NY * NX * NC, 1), 0)
    totals = table[...]

    def between(at, first, last, ok=None):
        inside = (number >= first) & (number <= last)
        value = jnp.exp(jnp.sum(jnp.where(inside, totals, 0.0), axis=0, keepdims=True))
        if ok is not None:
            value = jnp.where(ok, value, 0.0)
        coef[at : at + 1, :] = value

    between(0, chip0, chip0)
    between(1, chip0 + 1, chip0 + 1)
    for d in range(4):
        src = lax.rem(x - d + NX, NX)
        between(5 + d, row0 + src * NC + 2, row0 + NX * NC - 1)
        between(15 + d, row0, row0 + src * NC - 1)
        if d:
            between(1 + d, row0 + src * NC + 2, chip0 - 1, src < x)
            between(11 + d, chip0 + 2, row0 + src * NC - 1, src > x)
            src = lax.rem(y - d + NY, NY)
            between(8 + d, (src + 1) * NX * NC, chip0 - 1, src < y)
            between(18 + d, chip0 + 2, src * NX * NC - 1, src > y)
    coef[22:24, :] = jnp.zeros((2, 256), f32)


def fetch(blocks, into, sems, first, rows):
    for k, ref in zip(RELATIVE, blocks[:7]):
        pltpu.make_async_copy(ref.at[first : first + rows], into.at[k], sems.at[k]).start()
    if rows == 2 * T:
        pltpu.make_async_copy(blocks[7], into.at[4, 0:T], sems.at[4]).start()
        pltpu.make_async_copy(blocks[8], into.at[4, T : 2 * T], sems.at[4]).start()
    else:
        far = blocks[7 if first == 0 else 8]
        pltpu.make_async_copy(far, into.at[4], sems.at[4]).start()

    def wait(k):
        pltpu.make_async_copy(blocks[0].at[first : first + rows], into.at[k], sems.at[k]).wait()

    return wait


def fetch_rows(z, src, into, sems):
    def copy(k):
        row = pl.multiple_of(lax.rem(z + k, NZ) * W, W)
        return pltpu.make_async_copy(src.at[pl.ds(row, W), :], into.at[k], sems.at[k])

    for k in range(NZ):
        copy(k).start()
    return lambda k: copy(k).wait()


def each_z(step):
    def two(i, _):
        step(2 * i)
        step(2 * i + 1)
        return 0

    lax.fori_loop(0, NZ // 2, two, 0)


def project_body(pos, *refs):
    blocks = refs[:9]
    w_out, w_in, isc, up_t, down_t, bt, ct = refs[9:16]
    v_ref, g_ref, mine_ref, sib_ref = refs[16:20]
    held, wo, wi, acc_g, acc_v, sems, out_sems, in_sems = refs[20:]
    c, z = pos[2], pos[3]
    waits = (
        fetch_rows(z, w_out, wo, out_sems),
        fetch(blocks, held, sems, 0, 2 * T),
        fetch_rows(z, w_in, wi, in_sems),
    )
    acc_g[...] = jnp.zeros((T, W), f32)
    acc_v[...] = jnp.zeros((T, W), f32)

    def two(i, _):
        for k in (2 * i, 2 * i + 1):
            for wait in waits:
                wait(k)
        k, l = 2 * i, 2 * i + 1
        acc_g[...] += dot(held[k, :T, :], wo[k]) + dot(held[l, :T, :], wo[l])
        acc_v[...] += dot(held[k, T:, :], wi[k]) + dot(held[l, T:, :], wi[l])
        return 0

    lax.fori_loop(0, NZ // 2, two, 0)
    g_ref[...] = acc_g[...].astype(bf16)
    v_ref[...] = (acc_v[...] * isc[...]).astype(bf16)

    for base, vals, xt, ew in ((0, v_ref, bt, down_t), (2, g_ref, ct, up_t)):
        for j in range(PAIRS):
            vj = vals[:, 128 * j : 128 * j + 128]
            first = dot((xt[...] * ew[2 * j : 2 * j + 1, :]).astype(bf16), vj)
            second = dot((xt[...] * ew[2 * j + 1 : 2 * j + 2, :]).astype(bf16), vj)
            state = lane_pair(first, second).astype(bf16)

            @pl.when(c == j // 2)
            def _():
                mine_ref[base + j % 2] = state

            @pl.when(c != j // 2)
            def _():
                sib_ref[base + j % 2] = state


def pair_coef(coef, at, i):
    j = i % 2
    return coef[at : at + 1, 128 * j : 128 * j + 128]


def join_chip_body(pos, mine, other, coef, q):
    c = pos[2]
    for i in range(4):
        own, oth = mine[i].astype(f32), other[i].astype(f32)
        s0 = jnp.where(c == 0, own, oth)
        s1 = jnp.where(c == 0, oth, own)
        if i < 2:
            q[i] = (pair_coef(coef, 1, i) * s0 + s1).astype(bf16)
        else:
            q[i] = (s0 + pair_coef(coef, 0, i) * s1).astype(bf16)


def join_row_body(pos, q, g1, g2, g3, coef, u, enter):
    for i in range(4):
        near, end = (2, 5) if i < 2 else (12, 15)
        row = pair_coef(coef, end, i) * q[i].astype(f32)
        reach = jnp.zeros((N, 128), f32)
        for d, g in ((1, g1), (2, g2), (3, g3)):
            val = g[i].astype(f32)
            row += pair_coef(coef, end + d, i) * val
            reach += pair_coef(coef, near + d - 1, i) * val
        u[i] = row.astype(bf16)
        enter[i] = reach


def join_rows_body(pos, enter, g1, g2, g3, mine, other, coef, own, give):
    c = pos[2]
    for i in range(4):
        near = 9 if i < 2 else 19
        chip = enter[i]
        for d, g in ((1, g1), (2, g2), (3, g3)):
            chip += pair_coef(coef, near + d - 1, i) * g[i].astype(f32)
        o, t = mine[i].astype(f32), other[i].astype(f32)
        if i < 2:
            e0 = chip
            e1 = pair_coef(coef, 0, i) * chip + jnp.where(c == 0, o, t)
        else:
            e0 = pair_coef(coef, 1, i) * chip + jnp.where(c == 0, t, o)
            e1 = chip
        own[i] = jnp.where(c == 0, e0, e1).astype(bf16)
        give[i] = jnp.where(c == 0, e1, e0).astype(bf16)


STATES = sds((4, N, 128), bf16)


def exchange(pos, mine, sib, coef, first, second):
    other = swap(sib)
    (q,) = call(join_chip_body, "join_chip", [STATES], (pos, mine, other, coef))
    got = [axis_hop(q, dx=d) for d in (1, 2, 3)]
    *got, one = lax.optimization_barrier((*got, first()))
    u, enter = call(
        join_row_body, "join_row", [STATES, sds((4, N, 128), f32)], (pos, q, *got, coef)
    )
    got = [axis_hop(u, dy=d) for d in (1, 2, 3)]
    *got, two = lax.optimization_barrier((*got, second()))
    own, give = call(
        join_rows_body, "join_rows", [STATES, STATES], (pos, enter, *got, mine, other, coef)
    )
    return own, swap(give), one, two


def local_body(backward, pos, vals, b_ref, c_ref, a_ref, at_ref, out):
    row, col = iota((T, T), 0), iota((T, T), 1)
    first, second = (b_ref, c_ref) if backward else (c_ref, b_ref)
    meet = dot(first[...], second[...], 1, 1)
    keep = (col >= row) if backward else (row >= col)
    for j in range(PAIRS):
        vj = vals[:, 128 * j : 128 * j + 128]
        parts = []
        for h in (2 * j, 2 * j + 1):
            spread = a_ref[:, h : h + 1] - at_ref[h : h + 1, :]
            if backward:
                spread = -spread
            mix = jnp.exp(jnp.where(keep, spread, -1e30)) * meet
            parts.append(dot(mix.astype(bf16), vj))
        out[:, 128 * j : 128 * j + 128] = lane_pair(*parts)


def finish(c, base, local_ref, x_ref, eo_ref, mine_ref, sib_ref, j):
    at = base + j % 2
    state = jnp.where(c == j // 2, mine_ref[at].astype(f32), sib_ref[at].astype(f32)).astype(bf16)
    eo = lane_pair(eo_ref[:, 2 * j : 2 * j + 1], eo_ref[:, 2 * j + 1 : 2 * j + 2])
    return local_ref[:, 128 * j : 128 * j + 128] + eo * dot(x_ref[...], state)


def tokens_body(
    pos, w_in, local_ref, x_ref, eo_ref, mine_ref, sib_ref, isc,
    out, gb_ref, gs_ref, held, buf, in_sems, out_sems,
):
    c, z = pos[2], pos[3]
    wait = fetch_rows(z, w_in, held, in_sems)
    for j in range(PAIRS):
        vals = finish(c, 2, local_ref, x_ref, eo_ref, mine_ref, sib_ref, j)
        at = slice(128 * j, 128 * j + 128)
        gb_ref[:, at] = vals.astype(bf16)
        gs_ref[:, at] = (vals * isc[:, at]).astype(bf16)

    def back(k):
        return pltpu.make_async_copy(buf.at[k], out.at[lax.rem(z + k, NZ)], out_sems.at[k])

    def step(k):
        wait(k)
        buf[k] = dot(gs_ref[...], held[k], 1, 1).astype(bf16)
        back(k).start()

    each_z(step)
    for k in range(NZ):
        back(k).wait()


def store_total(pos, wait, held, right, keep, send, buf, out_sems):
    y, x, c, z = pos[0], pos[1], pos[2], pos[3]
    kept = pl.multiple_of(256 * c, 256)
    sent = pl.multiple_of(256 - 256 * c, 256)

    def back(k):
        copies = []
        for i in range(2):
            chip = lax.rem(z + k, NZ) * 2 + i
            dy = lax.rem(chip // NX - y + NY, NY)
            dx = lax.rem(lax.rem(chip, NX) - x + NX, NX)
            rows = slice(256 * i, 256 * i + 256)
            mine = keep.at[jnp.where(c == 0, dx, dy), jnp.where(c == 0, dy, dx)]
            other = send.at[jnp.where(c == 0, dy, dx), jnp.where(c == 0, dx, dy)]
            for j, (at, to) in enumerate(((kept, mine), (sent, other))):
                copies.append(
                    pltpu.make_async_copy(
                        buf.at[k, rows, pl.ds(at, 256)], to, out_sems.at[k, 2 * i + j]
                    )
                )
        return copies

    def step(k):
        wait(k)
        buf[k] = dot(held[k], right[...], 0, 0).astype(bf16)
        for copy in back(k):
            copy.start()

    each_z(step)

    def last(k, _):
        for copy in back(k):
            copy.wait()
        return 0

    lax.fori_loop(0, NZ, last, 0)


def in_total_body(pos, *refs):
    gb, keep, send, held, buf, sems, out_sems = refs[9:]
    wait = fetch(refs[:9], held, sems, T, T)
    store_total(pos, wait, held, gb, keep, send, buf, out_sems)


def out_total_body(pos, *refs):
    local_ref, x_ref, eo_ref, mine_ref, sib_ref, keep, send, held, buf, sems, out_sems, mb = refs[9:]
    wait = fetch(refs[:9], held, sems, 0, T)
    for j in range(PAIRS):
        at = slice(128 * j, 128 * j + 128)
        vals = finish(pos[2], 0, local_ref, x_ref, eo_ref, mine_ref, sib_ref, j)
        mb[:, at] = vals.astype(bf16)
    store_total(pos, wait, held, mb, keep, send, buf, out_sems)


TOTALS = [sds((4, 4, 256, 256), bf16)] * 2
MATMUL = 2 * T * D * W


def add(*parts):
    total = parts[0].astype(f32)
    for part in parts[1:]:
        total = total + part.astype(f32)
    return total


def scatter_seq(c, first, second):
    pairs = [(keep, swap(send)) for keep, send in (first, second)]

    def own(d):
        return jnp.stack([add(keep[d], came[d]) for keep, came in pairs], axis=1).astype(bf16)

    far = own(2)
    right = hop(far[:2], 1)
    left = hop(far[2:], -1)
    none = ((0, 0),) * 3
    near = add(own(1), jnp.pad(right, ((0, 2), *none))).astype(bf16)
    back = add(own(3), jnp.pad(left, ((2, 0), *none))).astype(bf16)
    total = add(own(0), hop(near, 1), hop(back, -1))
    got = [hop(total[d].astype(bf16), d, True) for d in (1, 2, 3)]
    total = add(total[0], *got)
    upper, lower = total[:, :R], total[:, R:]
    mine = jnp.where(c == 0, upper, lower)
    theirs = swap(jnp.where(c == 0, lower, upper))
    left, right = jnp.where(c == 0, mine, theirs), jnp.where(c == 0, theirs, mine)
    whole = jnp.concatenate([left, right], axis=2)
    return whole[0], whole[1]


def slopes_of(weight, step):
    ratios = weight.astype(f32) / step
    levels = jnp.floor(jnp.clip(ratios, -QMAX, QMAX) + 0.5)
    inside = jnp.abs(ratios) <= QMAX
    return jnp.where(inside, levels - ratios, levels), inside.astype(f32)


def per_device(
    tokens, grad_out, in_weight, in_scale, out_weight, out_scale, state_in, state_out, log_decay
):
    s = lax.axis_index("seq")
    z = lax.axis_index("tp")
    y, x, c = s // (NX * NC), (s // NC) % NX, s % NC
    pos = jnp.stack([y, x, c, z]).astype(jnp.int32)
    scale = in_scale[None, :]

    outs = [sds((2 * T, W), bf16)]
    outs += [sds((R + 16, 256), bf16)] * 2 + [sds((R, W), bf16)]
    outs += [sds((T, HP), f32), sds((HP, T), f32), sds((T, HP), f32), sds((T, HP), f32)]
    outs += [sds((HP, T), f32)] * 2 + [sds((N, T), f32)] * 2
    args = (
        pos, tokens, grad_out, in_weight, scale, out_weight,
        out_scale.reshape(NY * NX * NC, R), log_decay.T, state_in, state_out,
    )
    merged, o_keep, o_give, i_levels, run, run_t, up, down, up_t, down_t, bt, ct = call(
        prep_body, "prep", outs, args
    )

    w_in = lax.all_gather(i_levels, "seq", axis=0, tiled=True)
    out_own = jnp.stack([o_keep, swap(o_give)])
    out_row = jnp.stack([out_own] + [hop(out_own, -d) for d in (1, 2, 3)])
    out_all = [out_row] + [hop(out_row, -d, True) for d in (1, 2, 3)]
    blocks = gather_z(merged)
    w_out, coef = call(
        assemble_body,
        "assemble",
        [sds((D, W), bf16), sds((24, 256), f32)],
        (pos, *out_all, *[swap(v) for v in out_all]),
        10**6,
        [pltpu.VMEM((32, 256), f32)],
    )
    v, g, mine, sib = call(
        project_body,
        "project",
        [sds((T, W), bf16)] * 2 + [STATES] * 2,
        (pos, *blocks, w_out, w_in, scale, up_t, down_t, bt, ct),
        2 * MATMUL,
        [pltpu.VMEM((NZ, 2 * T, W), bf16)]
        + [pltpu.VMEM((NZ, W, W), bf16)] * 2
        + [pltpu.VMEM((T, W), f32)] * 2
        + [pltpu.SemaphoreType.DMA((NZ,))] * 3,
        away=11,
    )
    def local(backward, vals, name):
        return call(
            functools.partial(local_body, backward),
            name,
            [sds((T, W), f32)],
            (pos, vals, state_in, state_out, run, run_t),
            10**9,
        )[0]

    own, came, grad, mixed = exchange(
        pos, mine, sib, coef,
        lambda: local(True, g, "grad_local"),
        lambda: local(False, v, "mixed_local"),
    )
    wide = [pltpu.VMEM((T, W), bf16)]
    sems = [pltpu.SemaphoreType.DMA((NZ,))] * 2
    parts, gb = call(
        tokens_body,
        "token_parts",
        [sds((NZ, T, W), bf16), sds((T, W), bf16)],
        (pos, w_in, grad, state_in, down, own, came, scale),
        MATMUL,
        wide + [pltpu.VMEM((NZ, W, W), bf16), pltpu.VMEM((NZ, T, W), bf16)] + sems,
        away=1,
        out_away=(0,),
    )
    grad_tokens = lax.psum_scatter(
        parts.reshape(NZ * T, W), "tp", scatter_dimension=0, tiled=True
    )
    held = [
        pltpu.VMEM((NZ, T, W), bf16),
        pltpu.VMEM((NZ, W, W), bf16),
        pltpu.SemaphoreType.DMA((NZ,)),
        pltpu.SemaphoreType.DMA((NZ, 4)),
    ]
    in_parts = call(
        in_total_body, "in_parts", TOTALS, (pos, *blocks, gb), MATMUL, held, 9, (0, 1)
    )
    out_parts = call(
        out_total_body,
        "out_parts",
        TOTALS,
        (pos, *blocks, mixed, state_out, up, own, came),
        MATMUL,
        held + wide,
        9,
        (0, 1),
    )
    in_total, out_total = scatter_seq(c, in_parts, out_parts)
    scale_rows = lax.dynamic_slice_in_dim(out_scale, s * R, R)[:, None]
    out_total = out_total / scale_rows

    in_slopes, in_inside = slopes_of(in_weight, scale)
    out_slopes, out_inside = slopes_of(out_weight, scale_rows)
    in_sum = jnp.sum(in_total * in_slopes, axis=0)[None]
    out_sum = jnp.sum(out_total * out_slopes, axis=1)[None]
    for seq_bits, z_bits in ((2, 1), (4, 2), (8, 4), (16, 0), (1, 0)):
        came_in = seq_xor(in_sum, seq_bits)
        if z_bits:
            came_out = z_xor(out_sum, z_bits)
            came_in, came_out = lax.optimization_barrier((came_in, came_out))
            out_sum = out_sum + came_out
        in_sum = in_sum + came_in
    return (
        grad_tokens,
        in_total * in_inside,
        in_sum[0] / jnp.sqrt(f32(D * QMAX)),
        out_total * out_inside,
        out_sum[0] / jnp.sqrt(f32(HEADS * HEAD_DIM * QMAX)),
    )


def solution(mesh):
    placed = (
        P("seq", "tp"),
        P("seq", "tp"),
        P("seq", "tp"),
        P("tp"),
        P("seq", "tp"),
        P(),
        P("seq", None),
        P("seq", None),
        P("seq", "tp"),
    )
    return jax.shard_map(
        per_device,
        mesh=mesh,
        in_specs=placed,
        out_specs=(P("seq", "tp"), P("seq", "tp"), P("tp"), P("seq", "tp"), P("seq")),
        check_vma=False,
    )
```

```python
import functools

import jax
import jax.numpy as jnp
from jax import lax
from jax.experimental import pallas as pl
from jax.experimental.pallas import tpu as pltpu
from jax.sharding import PartitionSpec as P

D = 4096
HEADS = 64
HEAD_DIM = 64
QMAX = 7

NY, NX, NC, NZ = 4, 4, 2, 8
T = 256
W = 512
R = 128
N = 128
HP = 8
PAIRS = 4

f32 = jnp.float32
bf16 = jnp.bfloat16


def seq_at(y, x, c):
    return ((y % NY) * NX + x % NX) * NC + c % NC


def hop(v, d, second=False):
    pairs = []
    for y in range(NY):
        for x in range(NX):
            for c in range(NC):
                along_x = (c == 0) != second
                to = seq_at(y, x + d, c) if along_x else seq_at(y + d, x, c)
                pairs.append((seq_at(y, x, c), to))
    return lax.ppermute(v, "seq", pairs)


def axis_hop(v, dy=0, dx=0):
    pairs = []
    for y in range(NY):
        for x in range(NX):
            for c in range(NC):
                pairs.append((seq_at(y, x, c), seq_at(y + dy, x + dx, c)))
    return lax.ppermute(v, "seq", pairs)


def seq_xor(v, bits):
    return lax.ppermute(v, "seq", [(s, s ^ bits) for s in range(NY * NX * NC)])


def swap(v):
    return seq_xor(v, 1)


def z_hop(v, d):
    return lax.ppermute(v, "tp", [(z, (z + d) % NZ) for z in range(NZ)])


def gather_z(own):
    r1 = z_hop(own, 1)
    l1 = z_hop(own, -1)
    r2 = z_hop(r1, 1)
    l2 = z_hop(l1, -1)
    r3 = z_hop(r2, 1)
    l3 = z_hop(l2, -1)
    top = z_hop(r3[:T], 1)
    bot = z_hop(l3[T:], -1)
    return [own, l1, l2, l3, r3, r2, r1, top, bot]


RELATIVE = (0, 1, 2, 3, 5, 6, 7)
smem = pl.BlockSpec(memory_space=pltpu.SMEM)
vmem = pl.BlockSpec(memory_space=pltpu.VMEM)
anyw = pl.BlockSpec(memory_space=pl.ANY)


def sds(shape, dtype):
    return jax.ShapeDtypeStruct(shape, dtype)


def call(body, name, outs, args, flops=10**6, scratch=(), away=0, out_away=()):
    nbytes = sum(a.size * a.dtype.itemsize for a in args)
    nbytes += sum(o.size * o.dtype.itemsize for o in outs)
    return pl.pallas_call(
        body,
        out_shape=outs,
        in_specs=[smem] + [anyw] * away + [vmem] * (len(args) - 1 - away),
        out_specs=[anyw if i in out_away else vmem for i in range(len(outs))],
        scratch_shapes=scratch,
        compiler_params=pltpu.CompilerParams(vmem_limit_bytes=56 * 2**20),
        cost_estimate=pl.CostEstimate(flops=flops, bytes_accessed=nbytes, transcendentals=0),
        name=name,
    )(*args)


def dot(a, b, ca=1, cb=0):
    return lax.dot_general(a, b, (((ca,), (cb,)), ((), ())), preferred_element_type=f32)


def iota(shape, dim):
    return lax.broadcasted_iota(jnp.int32, shape, dim)


def lane_pair(first, second):
    return jnp.where(iota((1, 128), 1) < HEAD_DIM, first, second)


def split3(v):
    hi = v.astype(bf16)
    rest = v - hi.astype(f32)
    mid = rest.astype(bf16)
    return hi, mid, (rest - mid.astype(f32)).astype(bf16)


def levels_of(weight, step):
    ratios = weight.astype(f32) / step
    return jnp.floor(jnp.clip(ratios, -QMAX, QMAX) + 0.5)


def prep_body(
    pos, tok, go, iw, isc, ow, os_rows, ld_t, b_ref, c_ref,
    merged, o_keep, o_give, i_levels, run, run_t, up, down, up_t, down_t, bt, ct,
):
    c, z = pos[2], pos[3]
    s = (pos[0] * NX + pos[1]) * NC + c
    for i in range(4):
        at = slice(R * i, R * i + R)
        step = os_rows[pl.ds(4 * z + i, 1), :]
        merged[:T, at] = (go[:, at].astype(f32) * step).astype(bf16)
    merged[T:, :] = tok[...]
    square = (R, R)
    eye = iota(square, 0) == iota(square, 1)
    step = jnp.sum(jnp.where(eye, os_rows[pl.ds(s, 1), :], 0.0), axis=1, keepdims=True)
    out_lv = levels_of(ow[...], step).astype(bf16)
    i_levels[...] = levels_of(iw[...], isc[...]).astype(bf16)
    for core in range(2):
        mine, other = slice(256 * core, 256 * core + 256), slice(256 - 256 * core, 512 - 256 * core)

        @pl.when(c == core)
        def _():
            o_keep[0:R, :] = out_lv[:, mine]
            o_give[0:R, :] = out_lv[:, other]

    parts = split3(ld_t[...])
    tri = (iota((T, T), 0) >= iota((T, T), 1)).astype(bf16)
    cum = sum(dot(tri, p, 1, 1) for p in parts)
    cum_t = sum(dot(p, tri, 1, 1) for p in parts)
    total = cum[T - 1 : T, :]
    run[...] = cum
    run_t[...] = cum_t
    up[...] = jnp.exp(cum)
    down[...] = jnp.exp(total - cum)
    up_t[...] = jnp.exp(cum_t)
    down_t[...] = jnp.exp(cum_t[:, T - 1 : T] - cum_t)
    lane = iota((1, 256), 1) // HEAD_DIM
    rows = []
    for half in range(2):
        spread = jnp.zeros((1, 256), f32)
        for h in range(4):
            spread = jnp.where(lane == h, total[:, 4 * half + h : 4 * half + h + 1], spread)
        rows += [p.astype(f32) for p in split3(spread)]
    tile_row = iota((16, 256), 0)
    tile = jnp.zeros((16, 256), f32)
    for i, row in enumerate(rows):
        tile = jnp.where(tile_row == i, row, tile)
    o_keep[R:, :] = tile.astype(bf16)
    o_give[R:, :] = tile.astype(bf16)
    bt[...] = b_ref[...].astype(f32).T
    ct[...] = c_ref[...].astype(f32).T


def place(c, core_of, y, x, first, second):
    ch_y = jnp.where(core_of == 0, second, first)
    ch_x = jnp.where(core_of == 0, first, second)
    return lax.rem(y + ch_y, NY) * NX + lax.rem(x + ch_x, NX)


def assemble_body(pos, *refs):
    mine, theirs = refs[:4], refs[4:8]
    w_out, coef, table = refs[8:]
    y, x, c = pos[0], pos[1], pos[2]

    def copy(side, pieces, half):
        for e in range(4):

            def step(d, _):
                core = lax.rem(c + side, 2)
                chip = place(c, core, y, x, d, e)
                for r in range(2):
                    s = chip * NC + lax.rem(core + r, 2)
                    row = pl.multiple_of(s * R, R)
                    w_out[pl.ds(row, R), 256 * half : 256 * half + 256] = pieces[e][d, r, 0:R, :]
                    if side == 0:
                        tile = pieces[e][d, r, R:, :].astype(f32)
                        low = tile[0:1] + tile[1:2] + tile[2:3]
                        high = tile[3:4] + tile[4:5] + tile[5:6]
                        table[pl.ds(s, 1), :] = jnp.where(c == 0, low, high)
                return 0

            lax.fori_loop(0, 4, step, 0)

    for side, pieces in ((0, mine), (1, theirs)):
        for half in range(2):
            pl.when(lax.rem(c + side, 2) == half)(lambda: copy(side, pieces, half))

    chip0, row0 = (y * NX + x) * NC, y * NX * NC
    number = iota((NY * NX * NC, 1), 0)
    totals = table[...]

    def between(at, first, last, ok=None):
        inside = (number >= first) & (number <= last)
        value = jnp.exp(jnp.sum(jnp.where(inside, totals, 0.0), axis=0, keepdims=True))
        if ok is not None:
            value = jnp.where(ok, value, 0.0)
        coef[at : at + 1, :] = value

    between(0, chip0, chip0)
    between(1, chip0 + 1, chip0 + 1)
    for d in range(4):
        src = lax.rem(x - d + NX, NX)
        between(5 + d, row0 + src * NC + 2, row0 + NX * NC - 1)
        between(15 + d, row0, row0 + src * NC - 1)
        if d:
            between(1 + d, row0 + src * NC + 2, chip0 - 1, src < x)
            between(11 + d, chip0 + 2, row0 + src * NC - 1, src > x)
            src = lax.rem(y - d + NY, NY)
            between(8 + d, (src + 1) * NX * NC, chip0 - 1, src < y)
            between(18 + d, chip0 + 2, src * NX * NC - 1, src > y)
    coef[22:24, :] = jnp.zeros((2, 256), f32)


def fetch(blocks, into, sems, first, rows):
    for k, ref in zip(RELATIVE, blocks[:7]):
        pltpu.make_async_copy(ref.at[first : first + rows], into.at[k], sems.at[k]).start()
    if rows == 2 * T:
        pltpu.make_async_copy(blocks[7], into.at[4, 0:T], sems.at[4]).start()
        pltpu.make_async_copy(blocks[8], into.at[4, T : 2 * T], sems.at[4]).start()
    else:
        far = blocks[7 if first == 0 else 8]
        pltpu.make_async_copy(far, into.at[4], sems.at[4]).start()

    def wait(k):
        pltpu.make_async_copy(blocks[0].at[first : first + rows], into.at[k], sems.at[k]).wait()

    return wait


def fetch_rows(z, src, into, sems):
    def copy(k):
        row = pl.multiple_of(lax.rem(z + k, NZ) * W, W)
        return pltpu.make_async_copy(src.at[pl.ds(row, W), :], into.at[k], sems.at[k])

    for k in range(NZ):
        copy(k).start()
    return lambda k: copy(k).wait()


def each_z(step):
    def two(i, _):
        step(2 * i)
        step(2 * i + 1)
        return 0

    lax.fori_loop(0, NZ // 2, two, 0)


def project_body(pos, *refs):
    blocks = refs[:9]
    w_out, w_in, isc, up_t, down_t, bt, ct = refs[9:16]
    v_ref, g_ref, mine_ref, sib_ref = refs[16:20]
    held, wo, wi, acc_g, acc_v, sems, out_sems, in_sems = refs[20:]
    c, z = pos[2], pos[3]
    waits = (
        fetch_rows(z, w_out, wo, out_sems),
        fetch(blocks, held, sems, 0, 2 * T),
        fetch_rows(z, w_in, wi, in_sems),
    )
    acc_g[...] = jnp.zeros((T, W), f32)
    acc_v[...] = jnp.zeros((T, W), f32)

    def two(i, _):
        for k in (2 * i, 2 * i + 1):
            for wait in waits:
                wait(k)
        k, l = 2 * i, 2 * i + 1
        acc_g[...] += dot(held[k, :T, :], wo[k]) + dot(held[l, :T, :], wo[l])
        acc_v[...] += dot(held[k, T:, :], wi[k]) + dot(held[l, T:, :], wi[l])
        return 0

    lax.fori_loop(0, NZ // 2, two, 0)
    g_ref[...] = acc_g[...].astype(bf16)
    v_ref[...] = (acc_v[...] * isc[...]).astype(bf16)

    for base, vals, xt, ew in ((0, v_ref, bt, down_t), (2, g_ref, ct, up_t)):
        for j in range(PAIRS):
            vj = vals[:, 128 * j : 128 * j + 128]
            first = dot((xt[...] * ew[2 * j : 2 * j + 1, :]).astype(bf16), vj)
            second = dot((xt[...] * ew[2 * j + 1 : 2 * j + 2, :]).astype(bf16), vj)
            state = lane_pair(first, second).astype(bf16)

            @pl.when(c == j // 2)
            def _():
                mine_ref[base + j % 2] = state

            @pl.when(c != j // 2)
            def _():
                sib_ref[base + j % 2] = state


def pair_coef(coef, at, i):
    j = i % 2
    return coef[at : at + 1, 128 * j : 128 * j + 128]


def join_chip_body(pos, mine, other, coef, q):
    c = pos[2]
    for i in range(4):
        own, oth = mine[i].astype(f32), other[i].astype(f32)
        s0 = jnp.where(c == 0, own, oth)
        s1 = jnp.where(c == 0, oth, own)
        if i < 2:
            q[i] = (pair_coef(coef, 1, i) * s0 + s1).astype(bf16)
        else:
            q[i] = (s0 + pair_coef(coef, 0, i) * s1).astype(bf16)


def join_row_body(pos, q, g1, g2, g3, coef, u, enter):
    for i in range(4):
        near, end = (2, 5) if i < 2 else (12, 15)
        row = pair_coef(coef, end, i) * q[i].astype(f32)
        reach = jnp.zeros((N, 128), f32)
        for d, g in ((1, g1), (2, g2), (3, g3)):
            val = g[i].astype(f32)
            row += pair_coef(coef, end + d, i) * val
            reach += pair_coef(coef, near + d - 1, i) * val
        u[i] = row.astype(bf16)
        enter[i] = reach


def join_rows_body(pos, enter, g1, g2, g3, mine, other, coef, own, give):
    c = pos[2]
    for i in range(4):
        near = 9 if i < 2 else 19
        chip = enter[i]
        for d, g in ((1, g1), (2, g2), (3, g3)):
            chip += pair_coef(coef, near + d - 1, i) * g[i].astype(f32)
        o, t = mine[i].astype(f32), other[i].astype(f32)
        if i < 2:
            e0 = chip
            e1 = pair_coef(coef, 0, i) * chip + jnp.where(c == 0, o, t)
        else:
            e0 = pair_coef(coef, 1, i) * chip + jnp.where(c == 0, t, o)
            e1 = chip
        own[i] = jnp.where(c == 0, e0, e1).astype(bf16)
        give[i] = jnp.where(c == 0, e1, e0).astype(bf16)


STATES = sds((4, N, 128), bf16)


def exchange(pos, mine, sib, coef, first, second):
    other = swap(sib)
    (q,) = call(join_chip_body, "join_chip", [STATES], (pos, mine, other, coef))
    got = [axis_hop(q, dx=d) for d in (1, 2, 3)]
    *got, one = lax.optimization_barrier((*got, first()))
    u, enter = call(
        join_row_body, "join_row", [STATES, sds((4, N, 128), f32)], (pos, q, *got, coef)
    )
    got = [axis_hop(u, dy=d) for d in (1, 2, 3)]
    *got, two = lax.optimization_barrier((*got, second()))
    own, give = call(
        join_rows_body, "join_rows", [STATES, STATES], (pos, enter, *got, mine, other, coef)
    )
    return own, swap(give), one, two


def local_body(backward, pos, vals, b_ref, c_ref, a_ref, at_ref, out):
    row, col = iota((T, T), 0), iota((T, T), 1)
    first, second = (b_ref, c_ref) if backward else (c_ref, b_ref)
    meet = dot(first[...], second[...], 1, 1)
    keep = (col >= row) if backward else (row >= col)
    for j in range(PAIRS):
        vj = vals[:, 128 * j : 128 * j + 128]
        parts = []
        for h in (2 * j, 2 * j + 1):
            spread = a_ref[:, h : h + 1] - at_ref[h : h + 1, :]
            if backward:
                spread = -spread
            mix = jnp.exp(jnp.where(keep, spread, -1e30)) * meet
            parts.append(dot(mix.astype(bf16), vj))
        out[:, 128 * j : 128 * j + 128] = lane_pair(*parts)


def finish(c, base, local_ref, x_ref, eo_ref, mine_ref, sib_ref, j):
    at = base + j % 2
    state = jnp.where(c == j // 2, mine_ref[at].astype(f32), sib_ref[at].astype(f32)).astype(bf16)
    eo = lane_pair(eo_ref[:, 2 * j : 2 * j + 1], eo_ref[:, 2 * j + 1 : 2 * j + 2])
    return local_ref[:, 128 * j : 128 * j + 128] + eo * dot(x_ref[...], state)


def tokens_body(
    pos, w_in, local_ref, x_ref, eo_ref, mine_ref, sib_ref, isc,
    out, gb_ref, gs_ref, held, buf, in_sems, out_sems,
):
    c, z = pos[2], pos[3]
    wait = fetch_rows(z, w_in, held, in_sems)
    for j in range(PAIRS):
        vals = finish(c, 2, local_ref, x_ref, eo_ref, mine_ref, sib_ref, j)
        at = slice(128 * j, 128 * j + 128)
        gb_ref[:, at] = vals.astype(bf16)
        gs_ref[:, at] = (vals * isc[:, at]).astype(bf16)

    def back(k):
        return pltpu.make_async_copy(buf.at[k], out.at[lax.rem(z + k, NZ)], out_sems.at[k])

    def step(k):
        wait(k)
        buf[k] = dot(gs_ref[...], held[k], 1, 1).astype(bf16)
        back(k).start()

    each_z(step)
    for k in range(NZ):
        back(k).wait()


def store_total(pos, wait, held, right, keep, send, buf, out_sems):
    y, x, c, z = pos[0], pos[1], pos[2], pos[3]
    kept = pl.multiple_of(256 * c, 256)
    sent = pl.multiple_of(256 - 256 * c, 256)

    def back(k):
        copies = []
        for i in range(2):
            chip = lax.rem(z + k, NZ) * 2 + i
            dy = lax.rem(chip // NX - y + NY, NY)
            dx = lax.rem(lax.rem(chip, NX) - x + NX, NX)
            rows = slice(256 * i, 256 * i + 256)
            mine = keep.at[jnp.where(c == 0, dx, dy), jnp.where(c == 0, dy, dx)]
            other = send.at[jnp.where(c == 0, dy, dx), jnp.where(c == 0, dx, dy)]
            for j, (at, to) in enumerate(((kept, mine), (sent, other))):
                copies.append(
                    pltpu.make_async_copy(
                        buf.at[k, rows, pl.ds(at, 256)], to, out_sems.at[k, 2 * i + j]
                    )
                )
        return copies

    def step(k):
        wait(k)
        buf[k] = dot(held[k], right[...], 0, 0).astype(bf16)
        for copy in back(k):
            copy.start()

    each_z(step)

    def last(k, _):
        for copy in back(k):
            copy.wait()
        return 0

    lax.fori_loop(0, NZ, last, 0)


def in_total_body(pos, *refs):
    gb, keep, send, held, buf, sems, out_sems = refs[9:]
    wait = fetch(refs[:9], held, sems, T, T)
    store_total(pos, wait, held, gb, keep, send, buf, out_sems)


def out_total_body(pos, *refs):
    local_ref, x_ref, eo_ref, mine_ref, sib_ref, keep, send, held, buf, sems, out_sems, mb = refs[9:]
    wait = fetch(refs[:9], held, sems, 0, T)
    for j in range(PAIRS):
        at = slice(128 * j, 128 * j + 128)
        vals = finish(pos[2], 0, local_ref, x_ref, eo_ref, mine_ref, sib_ref, j)
        mb[:, at] = vals.astype(bf16)
    store_total(pos, wait, held, mb, keep, send, buf, out_sems)


TOTALS = [sds((4, 4, 256, 256), bf16)] * 2
MATMUL = 2 * T * D * W


def add(*parts):
    total = parts[0].astype(f32)
    for part in parts[1:]:
        total = total + part.astype(f32)
    return total


def scatter_seq(c, first, second):
    pairs = [(keep, swap(send)) for keep, send in (first, second)]

    def own(d):
        return jnp.stack([add(keep[d], came[d]) for keep, came in pairs], axis=1).astype(bf16)

    far = own(2)
    right = hop(far[:2], 1)
    left = hop(far[2:], -1)
    none = ((0, 0),) * 3
    near = add(own(1), jnp.pad(right, ((0, 2), *none))).astype(bf16)
    back = add(own(3), jnp.pad(left, ((2, 0), *none))).astype(bf16)
    total = add(own(0), hop(near, 1), hop(back, -1))
    got = [hop(total[d].astype(bf16), d, True) for d in (1, 2, 3)]
    total = add(total[0], *got)
    upper, lower = total[:, :R], total[:, R:]
    mine = jnp.where(c == 0, upper, lower)
    theirs = swap(jnp.where(c == 0, lower, upper))
    left, right = jnp.where(c == 0, mine, theirs), jnp.where(c == 0, theirs, mine)
    whole = jnp.concatenate([left, right], axis=2)
    return whole[0], whole[1]


def everyones(part, axis, count):
    parts = jnp.broadcast_to(part, (count, part.shape[1]))
    return jnp.sum(lax.all_to_all(parts, axis, 0, 0, tiled=True), axis=0)


def slopes_of(weight, step):
    ratios = weight.astype(f32) / step
    levels = jnp.floor(jnp.clip(ratios, -QMAX, QMAX) + 0.5)
    inside = jnp.abs(ratios) <= QMAX
    return jnp.where(inside, levels - ratios, levels), inside.astype(f32)


def per_device(
    tokens, grad_out, in_weight, in_scale, out_weight, out_scale, state_in, state_out, log_decay
):
    s = lax.axis_index("seq")
    z = lax.axis_index("tp")
    y, x, c = s // (NX * NC), (s // NC) % NX, s % NC
    pos = jnp.stack([y, x, c, z]).astype(jnp.int32)
    scale = in_scale[None, :]

    outs = [sds((2 * T, W), bf16)]
    outs += [sds((R + 16, 256), bf16)] * 2 + [sds((R, W), bf16)]
    outs += [sds((T, HP), f32), sds((HP, T), f32), sds((T, HP), f32), sds((T, HP), f32)]
    outs += [sds((HP, T), f32)] * 2 + [sds((N, T), f32)] * 2
    args = (
        pos, tokens, grad_out, in_weight, scale, out_weight,
        out_scale.reshape(NY * NX * NC, R), log_decay.T, state_in, state_out,
    )
    merged, o_keep, o_give, i_levels, run, run_t, up, down, up_t, down_t, bt, ct = call(
        prep_body, "prep", outs, args
    )

    w_in = lax.all_gather(i_levels, "seq", axis=0, tiled=True)
    out_own = jnp.stack([o_keep, swap(o_give)])
    out_row = jnp.stack([out_own] + [hop(out_own, -d) for d in (1, 2, 3)])
    out_all = [out_row] + [hop(out_row, -d, True) for d in (1, 2, 3)]
    blocks = gather_z(merged)
    w_out, coef = call(
        assemble_body,
        "assemble",
        [sds((D, W), bf16), sds((24, 256), f32)],
        (pos, *out_all, *[swap(v) for v in out_all]),
        10**6,
        [pltpu.VMEM((32, 256), f32)],
    )
    v, g, mine, sib = call(
        project_body,
        "project",
        [sds((T, W), bf16)] * 2 + [STATES] * 2,
        (pos, *blocks, w_out, w_in, scale, up_t, down_t, bt, ct),
        2 * MATMUL,
        [pltpu.VMEM((NZ, 2 * T, W), bf16)]
        + [pltpu.VMEM((NZ, W, W), bf16)] * 2
        + [pltpu.VMEM((T, W), f32)] * 2
        + [pltpu.SemaphoreType.DMA((NZ,))] * 3,
        away=11,
    )
    def local(backward, vals, name):
        return call(
            functools.partial(local_body, backward),
            name,
            [sds((T, W), f32)],
            (pos, vals, state_in, state_out, run, run_t),
            10**9,
        )[0]

    own, came, grad, mixed = exchange(
        pos, mine, sib, coef,
        lambda: local(True, g, "grad_local"),
        lambda: local(False, v, "mixed_local"),
    )
    wide = [pltpu.VMEM((T, W), bf16)]
    sems = [pltpu.SemaphoreType.DMA((NZ,))] * 2
    parts, gb = call(
        tokens_body,
        "token_parts",
        [sds((NZ, T, W), bf16), sds((T, W), bf16)],
        (pos, w_in, grad, state_in, down, own, came, scale),
        MATMUL,
        wide + [pltpu.VMEM((NZ, W, W), bf16), pltpu.VMEM((NZ, T, W), bf16)] + sems,
        away=1,
        out_away=(0,),
    )
    grad_tokens = lax.psum_scatter(
        parts.reshape(NZ * T, W), "tp", scatter_dimension=0, tiled=True
    )
    held = [
        pltpu.VMEM((NZ, T, W), bf16),
        pltpu.VMEM((NZ, W, W), bf16),
        pltpu.SemaphoreType.DMA((NZ,)),
        pltpu.SemaphoreType.DMA((NZ, 4)),
    ]
    in_parts = call(
        in_total_body, "in_parts", TOTALS, (pos, *blocks, gb), MATMUL, held, 9, (0, 1)
    )
    out_parts = call(
        out_total_body,
        "out_parts",
        TOTALS,
        (pos, *blocks, mixed, state_out, up, own, came),
        MATMUL,
        held + wide,
        9,
        (0, 1),
    )
    in_total, out_total = scatter_seq(c, in_parts, out_parts)
    scale_rows = lax.dynamic_slice_in_dim(out_scale, s * R, R)[:, None]
    out_total = out_total / scale_rows

    in_slopes, in_inside = slopes_of(in_weight, scale)
    out_slopes, out_inside = slopes_of(out_weight, scale_rows)
    in_sum = jnp.sum(in_total * in_slopes, axis=0)[None]
    out_sum = jnp.sum(out_total * out_slopes, axis=1)[None]
    in_sum = everyones(in_sum, "seq", NY * NX * NC)
    out_sum = everyones(out_sum, "tp", NZ)
    return (
        grad_tokens,
        in_total * in_inside,
        in_sum / jnp.sqrt(f32(D * QMAX)),
        out_total * out_inside,
        out_sum / jnp.sqrt(f32(HEADS * HEAD_DIM * QMAX)),
    )


def solution(mesh):
    placed = (
        P("seq", "tp"),
        P("seq", "tp"),
        P("seq", "tp"),
        P("tp"),
        P("seq", "tp"),
        P(),
        P("seq", None),
        P("seq", None),
        P("seq", "tp"),
    )
    return jax.shard_map(
        per_device,
        mesh=mesh,
        in_specs=placed,
        out_specs=(P("seq", "tp"), P("seq", "tp"), P("tp"), P("seq", "tp"), P("seq")),
        check_vma=False,
    )
```

```python
import functools

import jax
import jax.numpy as jnp
from jax import lax
from jax.experimental import pallas as pl
from jax.experimental.pallas import tpu as pltpu
from jax.sharding import PartitionSpec as P

D = 4096
HEADS = 64
HEAD_DIM = 64
QMAX = 7

NY, NX, NC, NZ = 4, 4, 2, 8
T = 256
W = 512
R = 128
N = 128
HP = 8
PAIRS = 4

f32 = jnp.float32
bf16 = jnp.bfloat16


def seq_at(y, x, c):
    return ((y % NY) * NX + x % NX) * NC + c % NC


def hop(v, d, second=False):
    pairs = []
    for y in range(NY):
        for x in range(NX):
            for c in range(NC):
                along_x = (c == 0) != second
                to = seq_at(y, x + d, c) if along_x else seq_at(y + d, x, c)
                pairs.append((seq_at(y, x, c), to))
    return lax.ppermute(v, "seq", pairs)


def axis_hop(v, dy=0, dx=0):
    pairs = []
    for y in range(NY):
        for x in range(NX):
            for c in range(NC):
                pairs.append((seq_at(y, x, c), seq_at(y + dy, x + dx, c)))
    return lax.ppermute(v, "seq", pairs)


def seq_xor(v, bits):
    return lax.ppermute(v, "seq", [(s, s ^ bits) for s in range(NY * NX * NC)])


def swap(v):
    return seq_xor(v, 1)


def z_hop(v, d):
    return lax.ppermute(v, "tp", [(z, (z + d) % NZ) for z in range(NZ)])


SECOND = [[seq_at(y, x, 0) for y in range(NY)] for x in range(NX)] + [
    [seq_at(y, x, 1) for x in range(NX)] for y in range(NY)
]


def z_xor(v, b):
    return lax.ppermute(v, "tp", [(z, z ^ b) for z in range(NZ)])


def after(v, others):
    return lax.optimization_barrier((v, *others))[0]


def gather_z(own):
    r1 = z_hop(own, 1)
    l1 = z_hop(own, -1)
    r2 = z_hop(r1, 1)
    l2 = z_hop(l1, -1)
    r3 = z_hop(r2, 1)
    l3 = z_hop(l2, -1)
    top = z_hop(r3[:T], 1)
    bot = z_hop(l3[T:], -1)
    return [own, l1, l2, l3, r3, r2, r1, top, bot]


RELATIVE = (0, 1, 2, 3, 5, 6, 7)
smem = pl.BlockSpec(memory_space=pltpu.SMEM)
vmem = pl.BlockSpec(memory_space=pltpu.VMEM)
anyw = pl.BlockSpec(memory_space=pl.ANY)


def sds(shape, dtype):
    return jax.ShapeDtypeStruct(shape, dtype)


def call(body, name, outs, args, flops=10**6, scratch=(), away=0, out_away=()):
    nbytes = sum(a.size * a.dtype.itemsize for a in args)
    nbytes += sum(o.size * o.dtype.itemsize for o in outs)
    return pl.pallas_call(
        body,
        out_shape=outs,
        in_specs=[smem] + [anyw] * away + [vmem] * (len(args) - 1 - away),
        out_specs=[anyw if i in out_away else vmem for i in range(len(outs))],
        scratch_shapes=scratch,
        compiler_params=pltpu.CompilerParams(vmem_limit_bytes=56 * 2**20),
        cost_estimate=pl.CostEstimate(flops=flops, bytes_accessed=nbytes, transcendentals=0),
        name=name,
    )(*args)


def dot(a, b, ca=1, cb=0):
    return lax.dot_general(a, b, (((ca,), (cb,)), ((), ())), preferred_element_type=f32)


def iota(shape, dim):
    return lax.broadcasted_iota(jnp.int32, shape, dim)


def lane_pair(first, second):
    return jnp.where(iota((1, 128), 1) < HEAD_DIM, first, second)


def split3(v):
    hi = v.astype(bf16)
    rest = v - hi.astype(f32)
    mid = rest.astype(bf16)
    return hi, mid, (rest - mid.astype(f32)).astype(bf16)


def levels_of(weight, step):
    ratios = weight.astype(f32) / step
    return jnp.floor(jnp.clip(ratios, -QMAX, QMAX) + 0.5)


def prep_body(
    pos, tok, go, iw, isc, ow, os_rows, ld_t, b_ref, c_ref,
    merged, o_keep, o_give, run, run_t, up, down, up_t, down_t, bt, ct,
):
    c, z = pos[2], pos[3]
    s = (pos[0] * NX + pos[1]) * NC + c
    for i in range(4):
        at = slice(R * i, R * i + R)
        step = os_rows[pl.ds(4 * z + i, 1), :]
        merged[:T, at] = (go[:, at].astype(f32) * step).astype(bf16)
    merged[T:, :] = tok[...]
    square = (R, R)
    eye = iota(square, 0) == iota(square, 1)
    step = jnp.sum(jnp.where(eye, os_rows[pl.ds(s, 1), :], 0.0), axis=1, keepdims=True)
    out_lv = levels_of(ow[...], step).astype(bf16)
    in_lv = levels_of(iw[...], isc[...]).astype(bf16)
    for core in range(2):
        mine, other = slice(256 * core, 256 * core + 256), slice(256 - 256 * core, 512 - 256 * core)

        @pl.when(c == core)
        def _():
            o_keep[0:R, :] = out_lv[:, mine]
            o_give[0:R, :] = out_lv[:, other]
            o_keep[R + 16 :, :] = in_lv[:, mine]
            o_give[R + 16 :, :] = in_lv[:, other]

    parts = split3(ld_t[...])
    tri = (iota((T, T), 0) >= iota((T, T), 1)).astype(bf16)
    cum = sum(dot(tri, p, 1, 1) for p in parts)
    cum_t = sum(dot(p, tri, 1, 1) for p in parts)
    total = cum[T - 1 : T, :]
    run[...] = cum
    run_t[...] = cum_t
    up[...] = jnp.exp(cum)
    down[...] = jnp.exp(total - cum)
    up_t[...] = jnp.exp(cum_t)
    down_t[...] = jnp.exp(cum_t[:, T - 1 : T] - cum_t)
    lane = iota((1, 256), 1) // HEAD_DIM
    rows = []
    for half in range(2):
        spread = jnp.zeros((1, 256), f32)
        for h in range(4):
            spread = jnp.where(lane == h, total[:, 4 * half + h : 4 * half + h + 1], spread)
        rows += [p.astype(f32) for p in split3(spread)]
    tile_row = iota((16, 256), 0)
    tile = jnp.zeros((16, 256), f32)
    for i, row in enumerate(rows):
        tile = jnp.where(tile_row == i, row, tile)
    o_keep[R : R + 16, :] = tile.astype(bf16)
    o_give[R : R + 16, :] = tile.astype(bf16)
    bt[...] = b_ref[...].astype(f32).T
    ct[...] = c_ref[...].astype(f32).T


def place(c, core_of, y, x, first, second):
    ch_y = jnp.where(core_of == 0, second, first)
    ch_x = jnp.where(core_of == 0, first, second)
    return lax.rem(y + ch_y, NY) * NX + lax.rem(x + ch_x, NX)


def assemble_body(pos, *refs):
    mine, i_mine, i_theirs = refs[:4], refs[6], refs[7]
    theirs = [refs[4]] + [refs[5].at[i] for i in range(3)]
    w_out, w_in, coef, table = refs[8:]
    y, x, c = pos[0], pos[1], pos[2]

    def copy(side, pieces, within, half):
        core = lax.rem(c + side, 2)
        at = slice(256 * half, 256 * half + 256)
        for e in range(4):

            def step(d, _):
                chip = place(c, core, y, x, d, e)
                second = jnp.where(core == 0, y, x)
                ahead = lax.rem(second + e, 4)
                for r in range(2):
                    s = chip * NC + lax.rem(core + r, 2)
                    row = pl.multiple_of(s * R, R)
                    w_out[pl.ds(row, R), at] = pieces[e][d, r, 0:R, :]
                    w_in[pl.ds(row, R), at] = within[ahead * 8 + d * 2 + r]
                    if side == 0:
                        tile = pieces[e][d, r, R:, :].astype(f32)
                        low = tile[0:1] + tile[1:2] + tile[2:3]
                        high = tile[3:4] + tile[4:5] + tile[5:6]
                        table[pl.ds(s, 1), :] = jnp.where(c == 0, low, high)
                return 0

            lax.fori_loop(0, 4, step, 0)

    for side, pieces, within in ((0, mine, i_mine), (1, theirs, i_theirs)):
        for half in range(2):
            pl.when(lax.rem(c + side, 2) == half)(lambda: copy(side, pieces, within, half))

    chip0, row0 = (y * NX + x) * NC, y * NX * NC
    number = iota((NY * NX * NC, 1), 0)
    totals = table[...]

    def between(at, first, last, ok=None):
        inside = (number >= first) & (number <= last)
        value = jnp.exp(jnp.sum(jnp.where(inside, totals, 0.0), axis=0, keepdims=True))
        if ok is not None:
            value = jnp.where(ok, value, 0.0)
        coef[at : at + 1, :] = value

    between(0, chip0, chip0)
    between(1, chip0 + 1, chip0 + 1)
    for d in range(4):
        src = lax.rem(x - d + NX, NX)
        between(5 + d, row0 + src * NC + 2, row0 + NX * NC - 1)
        between(15 + d, row0, row0 + src * NC - 1)
        if d:
            between(1 + d, row0 + src * NC + 2, chip0 - 1, src < x)
            between(11 + d, chip0 + 2, row0 + src * NC - 1, src > x)
            src = lax.rem(y - d + NY, NY)
            between(8 + d, (src + 1) * NX * NC, chip0 - 1, src < y)
            between(18 + d, chip0 + 2, src * NX * NC - 1, src > y)
    coef[22:24, :] = jnp.zeros((2, 256), f32)


def fetch(blocks, into, sems, first, rows):
    for k, ref in zip(RELATIVE, blocks[:7]):
        pltpu.make_async_copy(ref.at[first : first + rows], into.at[k], sems.at[k]).start()
    if rows == 2 * T:
        pltpu.make_async_copy(blocks[7], into.at[4, 0:T], sems.at[4]).start()
        pltpu.make_async_copy(blocks[8], into.at[4, T : 2 * T], sems.at[4]).start()
    else:
        far = blocks[7 if first == 0 else 8]
        pltpu.make_async_copy(far, into.at[4], sems.at[4]).start()

    def wait(k):
        pltpu.make_async_copy(blocks[0].at[first : first + rows], into.at[k], sems.at[k]).wait()

    return wait


def fetch_rows(z, src, into, sems):
    def copy(k):
        row = pl.multiple_of(lax.rem(z + k, NZ) * W, W)
        return pltpu.make_async_copy(src.at[pl.ds(row, W), :], into.at[k], sems.at[k])

    for k in range(NZ):
        copy(k).start()
    return lambda k: copy(k).wait()


def each_z(step):
    def two(i, _):
        step(2 * i)
        step(2 * i + 1)
        return 0

    lax.fori_loop(0, NZ // 2, two, 0)


def project_body(pos, *refs):
    blocks = refs[:9]
    w_out, w_in, isc, up_t, down_t, bt, ct = refs[9:16]
    v_ref, g_ref, mine_ref, sib_ref = refs[16:20]
    held, wo, wi, acc_g, acc_v, sems, out_sems, in_sems = refs[20:]
    c, z = pos[2], pos[3]
    waits = (
        fetch_rows(z, w_out, wo, out_sems),
        fetch(blocks, held, sems, 0, 2 * T),
        fetch_rows(z, w_in, wi, in_sems),
    )
    acc_g[...] = jnp.zeros((T, W), f32)
    acc_v[...] = jnp.zeros((T, W), f32)

    def two(i, _):
        for k in (2 * i, 2 * i + 1):
            for wait in waits:
                wait(k)
        k, l = 2 * i, 2 * i + 1
        acc_g[...] += dot(held[k, :T, :], wo[k]) + dot(held[l, :T, :], wo[l])
        acc_v[...] += dot(held[k, T:, :], wi[k]) + dot(held[l, T:, :], wi[l])
        return 0

    lax.fori_loop(0, NZ // 2, two, 0)
    g_ref[...] = acc_g[...].astype(bf16)
    v_ref[...] = (acc_v[...] * isc[...]).astype(bf16)

    for base, vals, xt, ew in ((0, v_ref, bt, down_t), (2, g_ref, ct, up_t)):
        for j in range(PAIRS):
            vj = vals[:, 128 * j : 128 * j + 128]
            first = dot((xt[...] * ew[2 * j : 2 * j + 1, :]).astype(bf16), vj)
            second = dot((xt[...] * ew[2 * j + 1 : 2 * j + 2, :]).astype(bf16), vj)
            state = lane_pair(first, second).astype(bf16)

            @pl.when(c == j // 2)
            def _():
                mine_ref[base + j % 2] = state

            @pl.when(c != j // 2)
            def _():
                sib_ref[base + j % 2] = state


def pair_coef(coef, at, i):
    j = i % 2
    return coef[at : at + 1, 128 * j : 128 * j + 128]


def join_chip_body(pos, mine, other, coef, q):
    c = pos[2]
    for i in range(4):
        own, oth = mine[i].astype(f32), other[i].astype(f32)
        s0 = jnp.where(c == 0, own, oth)
        s1 = jnp.where(c == 0, oth, own)
        if i < 2:
            q[i] = (pair_coef(coef, 1, i) * s0 + s1).astype(bf16)
        else:
            q[i] = (s0 + pair_coef(coef, 0, i) * s1).astype(bf16)


def join_row_body(pos, q, g1, g2, g3, coef, u, enter):
    for i in range(4):
        near, end = (2, 5) if i < 2 else (12, 15)
        row = pair_coef(coef, end, i) * q[i].astype(f32)
        reach = jnp.zeros((N, 128), f32)
        for d, g in ((1, g1), (2, g2), (3, g3)):
            val = g[i].astype(f32)
            row += pair_coef(coef, end + d, i) * val
            reach += pair_coef(coef, near + d - 1, i) * val
        u[i] = row.astype(bf16)
        enter[i] = reach


def join_rows_body(pos, enter, g1, g2, g3, mine, other, coef, own, give):
    c = pos[2]
    for i in range(4):
        near = 9 if i < 2 else 19
        chip = enter[i]
        for d, g in ((1, g1), (2, g2), (3, g3)):
            chip += pair_coef(coef, near + d - 1, i) * g[i].astype(f32)
        o, t = mine[i].astype(f32), other[i].astype(f32)
        if i < 2:
            e0 = chip
            e1 = pair_coef(coef, 0, i) * chip + jnp.where(c == 0, o, t)
        else:
            e0 = pair_coef(coef, 1, i) * chip + jnp.where(c == 0, t, o)
            e1 = chip
        own[i] = jnp.where(c == 0, e0, e1).astype(bf16)
        give[i] = jnp.where(c == 0, e1, e0).astype(bf16)


STATES = sds((4, N, 128), bf16)


def exchange(pos, mine, sib, coef, first, second):
    other = swap(sib)
    (q,) = call(join_chip_body, "join_chip", [STATES], (pos, mine, other, coef))
    got = [axis_hop(q, dx=d) for d in (1, 2, 3)]
    *got, one = lax.optimization_barrier((*got, first()))
    u, enter = call(
        join_row_body, "join_row", [STATES, sds((4, N, 128), f32)], (pos, q, *got, coef)
    )
    got = [axis_hop(u, dy=d) for d in (1, 2, 3)]
    *got, two = lax.optimization_barrier((*got, second()))
    own, give = call(
        join_rows_body, "join_rows", [STATES, STATES], (pos, enter, *got, mine, other, coef)
    )
    return own, swap(give), one, two


def local_body(backward, pos, vals, b_ref, c_ref, a_ref, at_ref, out):
    row, col = iota((T, T), 0), iota((T, T), 1)
    first, second = (b_ref, c_ref) if backward else (c_ref, b_ref)
    meet = dot(first[...], second[...], 1, 1)
    keep = (col >= row) if backward else (row >= col)
    for j in range(PAIRS):
        vj = vals[:, 128 * j : 128 * j + 128]
        parts = []
        for h in (2 * j, 2 * j + 1):
            spread = a_ref[:, h : h + 1] - at_ref[h : h + 1, :]
            if backward:
                spread = -spread
            mix = jnp.exp(jnp.where(keep, spread, -1e30)) * meet
            parts.append(dot(mix.astype(bf16), vj))
        out[:, 128 * j : 128 * j + 128] = lane_pair(*parts)


def finish(c, base, local_ref, x_ref, eo_ref, mine_ref, sib_ref, j):
    at = base + j % 2
    state = jnp.where(c == j // 2, mine_ref[at].astype(f32), sib_ref[at].astype(f32)).astype(bf16)
    eo = lane_pair(eo_ref[:, 2 * j : 2 * j + 1], eo_ref[:, 2 * j + 1 : 2 * j + 2])
    return local_ref[:, 128 * j : 128 * j + 128] + eo * dot(x_ref[...], state)


def tokens_body(
    pos, w_in, local_ref, x_ref, eo_ref, mine_ref, sib_ref, isc,
    out, gb_ref, gs_ref, held, buf, in_sems, out_sems,
):
    c, z = pos[2], pos[3]
    wait = fetch_rows(z, w_in, held, in_sems)
    for j in range(PAIRS):
        vals = finish(c, 2, local_ref, x_ref, eo_ref, mine_ref, sib_ref, j)
        at = slice(128 * j, 128 * j + 128)
        gb_ref[:, at] = vals.astype(bf16)
        gs_ref[:, at] = (vals * isc[:, at]).astype(bf16)

    def back(k):
        return pltpu.make_async_copy(buf.at[k], out.at[lax.rem(z + k, NZ)], out_sems.at[k])

    def step(k):
        wait(k)
        buf[k] = dot(gs_ref[...], held[k], 1, 1).astype(bf16)
        back(k).start()

    each_z(step)
    for k in range(NZ):
        back(k).wait()


def store_total(pos, wait, held, right, keep, send, buf, out_sems):
    y, x, c, z = pos[0], pos[1], pos[2], pos[3]
    kept = pl.multiple_of(256 * c, 256)
    sent = pl.multiple_of(256 - 256 * c, 256)

    def back(k):
        copies = []
        for i in range(2):
            chip = lax.rem(z + k, NZ) * 2 + i
            dy = lax.rem(chip // NX - y + NY, NY)
            dx = lax.rem(lax.rem(chip, NX) - x + NX, NX)
            rows = slice(256 * i, 256 * i + 256)
            mine = keep.at[jnp.where(c == 0, dx, dy), jnp.where(c == 0, dy, dx)]
            other = send.at[jnp.where(c == 0, dy, dx), jnp.where(c == 0, dx, dy)]
            for j, (at, to) in enumerate(((kept, mine), (sent, other))):
                copies.append(
                    pltpu.make_async_copy(
                        buf.at[k, rows, pl.ds(at, 256)], to, out_sems.at[k, 2 * i + j]
                    )
                )
        return copies

    def step(k):
        wait(k)
        buf[k] = dot(held[k], right[...], 0, 0).astype(bf16)
        for copy in back(k):
            copy.start()

    each_z(step)

    def last(k, _):
        for copy in back(k):
            copy.wait()
        return 0

    lax.fori_loop(0, NZ, last, 0)


def in_total_body(pos, *refs):
    gb, keep, send, held, buf, sems, out_sems = refs[9:]
    wait = fetch(refs[:9], held, sems, T, T)
    store_total(pos, wait, held, gb, keep, send, buf, out_sems)


def out_total_body(pos, *refs):
    local_ref, x_ref, eo_ref, mine_ref, sib_ref, keep, send, held, buf, sems, out_sems, mb = refs[9:]
    wait = fetch(refs[:9], held, sems, 0, T)
    for j in range(PAIRS):
        at = slice(128 * j, 128 * j + 128)
        vals = finish(pos[2], 0, local_ref, x_ref, eo_ref, mine_ref, sib_ref, j)
        mb[:, at] = vals.astype(bf16)
    store_total(pos, wait, held, mb, keep, send, buf, out_sems)


TOTALS = [sds((4, 4, 256, 256), bf16)] * 2
MATMUL = 2 * T * D * W


def add(*parts):
    total = parts[0].astype(f32)
    for part in parts[1:]:
        total = total + part.astype(f32)
    return total


def scatter_seq(c, first, second):
    pairs = [(keep, swap(send)) for keep, send in (first, second)]

    def own(d):
        return jnp.stack([add(keep[d], came[d]) for keep, came in pairs], axis=1).astype(bf16)

    far = own(2)
    right = hop(far[:2], 1)
    left = hop(far[2:], -1)
    none = ((0, 0),) * 3
    near = add(own(1), jnp.pad(right, ((0, 2), *none))).astype(bf16)
    back = add(own(3), jnp.pad(left, ((2, 0), *none))).astype(bf16)
    total = add(own(0), hop(near, 1), hop(back, -1))
    got = [hop(total[d].astype(bf16), d, True) for d in (1, 2, 3)]
    total = add(total[0], *got)
    upper, lower = total[:, :R], total[:, R:]
    mine = jnp.where(c == 0, upper, lower)
    theirs = swap(jnp.where(c == 0, lower, upper))
    left, right = jnp.where(c == 0, mine, theirs), jnp.where(c == 0, theirs, mine)
    whole = jnp.concatenate([left, right], axis=2)
    return whole[0], whole[1]


def everyones(part, axis, count):
    parts = jnp.broadcast_to(part, (count, 8, part.shape[1]))
    return jnp.sum(lax.all_to_all(parts, axis, 0, 0, tiled=True)[:, 0], axis=0)


def slopes_of(weight, step):
    ratios = weight.astype(f32) / step
    levels = jnp.floor(jnp.clip(ratios, -QMAX, QMAX) + 0.5)
    inside = jnp.abs(ratios) <= QMAX
    return jnp.where(inside, levels - ratios, levels), inside.astype(f32)


def per_device(
    tokens, grad_out, in_weight, in_scale, out_weight, out_scale, state_in, state_out, log_decay
):
    s = lax.axis_index("seq")
    z = lax.axis_index("tp")
    y, x, c = s // (NX * NC), (s // NC) % NX, s % NC
    pos = jnp.stack([y, x, c, z]).astype(jnp.int32)
    scale = in_scale[None, :]

    outs = [sds((2 * T, W), bf16)]
    outs += [sds((2 * R + 16, 256), bf16)] * 2
    outs += [sds((T, HP), f32), sds((HP, T), f32), sds((T, HP), f32), sds((T, HP), f32)]
    outs += [sds((HP, T), f32)] * 2 + [sds((N, T), f32)] * 2
    args = (
        pos, tokens, grad_out, in_weight, scale, out_weight,
        out_scale.reshape(NY * NX * NC, R), log_decay.T, state_in, state_out,
    )
    merged, keep, give, run, run_t, up, down, up_t, down_t, bt, ct = call(
        prep_body, "prep", outs, args
    )

    own = jnp.stack([keep, swap(give)])
    row = [own] + [hop(own, -d) for d in (1, 2, 3)]
    blocks = gather_z(merged)
    near = (blocks[1], blocks[6])
    in_row = after(jnp.concatenate([v[:, R + 16 :] for v in row]), near)
    in_all = lax.all_gather(in_row, "seq", axis=0, tiled=True, axis_index_groups=SECOND)
    in_all = after(in_all, (blocks[3], blocks[4]))
    out_row = after(jnp.stack([v[:, : R + 16] for v in row]), near)
    out_all = [out_row] + [hop(out_row, -d, True) for d in (1, 2, 3)]
    w_out, w_in, coef = call(
        assemble_body,
        "assemble",
        [sds((D, W), bf16)] * 2 + [sds((24, 256), f32)],
        (pos, *out_all, swap(out_row), swap(jnp.stack(out_all[1:])), in_all, swap(in_all)),
        10**6,
        [pltpu.VMEM((32, 256), f32)],
    )
    v, g, mine, sib = call(
        project_body,
        "project",
        [sds((T, W), bf16)] * 2 + [STATES] * 2,
        (pos, *blocks, w_out, w_in, scale, up_t, down_t, bt, ct),
        2 * MATMUL,
        [pltpu.VMEM((NZ, 2 * T, W), bf16)]
        + [pltpu.VMEM((NZ, W, W), bf16)] * 2
        + [pltpu.VMEM((T, W), f32)] * 2
        + [pltpu.SemaphoreType.DMA((NZ,))] * 3,
        away=11,
    )
    def local(backward, vals, name):
        return call(
            functools.partial(local_body, backward),
            name,
            [sds((T, W), f32)],
            (pos, vals, state_in, state_out, run, run_t),
            10**9,
        )[0]

    own, came, grad, mixed = exchange(
        pos, mine, sib, coef,
        lambda: local(True, g, "grad_local"),
        lambda: local(False, v, "mixed_local"),
    )
    wide = [pltpu.VMEM((T, W), bf16)]
    sems = [pltpu.SemaphoreType.DMA((NZ,))] * 2
    parts, gb = call(
        tokens_body,
        "token_parts",
        [sds((NZ, T, W), bf16), sds((T, W), bf16)],
        (pos, w_in, grad, state_in, down, own, came, scale),
        MATMUL,
        wide + [pltpu.VMEM((NZ, W, W), bf16), pltpu.VMEM((NZ, T, W), bf16)] + sems,
        away=1,
        out_away=(0,),
    )
    grad_tokens = lax.psum_scatter(
        parts.reshape(NZ * T, W), "tp", scatter_dimension=0, tiled=True
    )
    held = [
        pltpu.VMEM((NZ, T, W), bf16),
        pltpu.VMEM((NZ, W, W), bf16),
        pltpu.SemaphoreType.DMA((NZ,)),
        pltpu.SemaphoreType.DMA((NZ, 4)),
    ]
    in_parts = call(
        in_total_body, "in_parts", TOTALS, (pos, *blocks, gb), MATMUL, held, 9, (0, 1)
    )
    out_parts = call(
        out_total_body,
        "out_parts",
        TOTALS,
        (pos, *blocks, mixed, state_out, up, own, came),
        MATMUL,
        held + wide,
        9,
        (0, 1),
    )
    in_total, out_total = scatter_seq(c, in_parts, out_parts)
    scale_rows = lax.dynamic_slice_in_dim(out_scale, s * R, R)[:, None]
    out_total = out_total / scale_rows

    in_slopes, in_inside = slopes_of(in_weight, scale)
    out_slopes, out_inside = slopes_of(out_weight, scale_rows)
    in_sum = jnp.sum(in_total * in_slopes, axis=0)[None]
    out_sum = jnp.sum(out_total * out_slopes, axis=1)[None]
    in_sum = everyones(in_sum, "seq", NY * NX * NC)
    for bits in (1, 2, 4):
        out_sum = out_sum + z_xor(out_sum, bits)
    out_sum = out_sum[0]
    return (
        grad_tokens,
        in_total * in_inside,
        in_sum / jnp.sqrt(f32(D * QMAX)),
        out_total * out_inside,
        out_sum / jnp.sqrt(f32(HEADS * HEAD_DIM * QMAX)),
    )


def solution(mesh):
    placed = (
        P("seq", "tp"),
        P("seq", "tp"),
        P("seq", "tp"),
        P("tp"),
        P("seq", "tp"),
        P(),
        P("seq", None),
        P("seq", None),
        P("seq", "tp"),
    )
    return jax.shard_map(
        per_device,
        mesh=mesh,
        in_specs=placed,
        out_specs=(P("seq", "tp"), P("seq", "tp"), P("tp"), P("seq", "tp"), P("seq")),
        check_vma=False,
    )
```

```python
import functools

import jax
import jax.numpy as jnp
from jax import lax
from jax.experimental import pallas as pl
from jax.experimental.pallas import tpu as pltpu
from jax.sharding import PartitionSpec as P

D = 4096
HEADS = 64
HEAD_DIM = 64
QMAX = 7

NY, NX, NC, NZ = 4, 4, 2, 8
T = 256
W = 512
R = 128
N = 128
HP = 8
PAIRS = 4

f32 = jnp.float32
bf16 = jnp.bfloat16


def seq_at(y, x, c):
    return ((y % NY) * NX + x % NX) * NC + c % NC


def hop(v, d, second=False):
    pairs = []
    for y in range(NY):
        for x in range(NX):
            for c in range(NC):
                along_x = (c == 0) != second
                to = seq_at(y, x + d, c) if along_x else seq_at(y + d, x, c)
                pairs.append((seq_at(y, x, c), to))
    return lax.ppermute(v, "seq", pairs)


def axis_hop(v, dy=0, dx=0):
    pairs = []
    for y in range(NY):
        for x in range(NX):
            for c in range(NC):
                pairs.append((seq_at(y, x, c), seq_at(y + dy, x + dx, c)))
    return lax.ppermute(v, "seq", pairs)


def seq_xor(v, bits):
    return lax.ppermute(v, "seq", [(s, s ^ bits) for s in range(NY * NX * NC)])


def swap(v):
    return seq_xor(v, 1)


def z_hop(v, d):
    return lax.ppermute(v, "tp", [(z, (z + d) % NZ) for z in range(NZ)])


def after(v, other):
    return lax.optimization_barrier((v, other))[0]


def gather_z(own):
    r1 = z_hop(own, 1)
    l1 = z_hop(own, -1)
    r2 = z_hop(r1, 1)
    l2 = z_hop(l1, -1)
    r3 = z_hop(r2, 1)
    l3 = z_hop(l2, -1)
    top = z_hop(r3[:T], 1)
    bot = z_hop(l3[T:], -1)
    return [own, l1, l2, l3, r3, r2, r1, top, bot]


RELATIVE = (0, 1, 2, 3, 5, 6, 7)
smem = pl.BlockSpec(memory_space=pltpu.SMEM)
vmem = pl.BlockSpec(memory_space=pltpu.VMEM)
anyw = pl.BlockSpec(memory_space=pl.ANY)


def sds(shape, dtype):
    return jax.ShapeDtypeStruct(shape, dtype)


def call(body, name, outs, args, flops=10**6, scratch=(), away=0, out_away=()):
    nbytes = sum(a.size * a.dtype.itemsize for a in args)
    nbytes += sum(o.size * o.dtype.itemsize for o in outs)
    return pl.pallas_call(
        body,
        out_shape=outs,
        in_specs=[smem] + [anyw] * away + [vmem] * (len(args) - 1 - away),
        out_specs=[anyw if i in out_away else vmem for i in range(len(outs))],
        scratch_shapes=scratch,
        compiler_params=pltpu.CompilerParams(vmem_limit_bytes=56 * 2**20),
        cost_estimate=pl.CostEstimate(flops=flops, bytes_accessed=nbytes, transcendentals=0),
        name=name,
    )(*args)


def dot(a, b, ca=1, cb=0):
    return lax.dot_general(a, b, (((ca,), (cb,)), ((), ())), preferred_element_type=f32)


def iota(shape, dim):
    return lax.broadcasted_iota(jnp.int32, shape, dim)


def lane_pair(first, second):
    return jnp.where(iota((1, 128), 1) < HEAD_DIM, first, second)


def split3(v):
    hi = v.astype(bf16)
    rest = v - hi.astype(f32)
    mid = rest.astype(bf16)
    return hi, mid, (rest - mid.astype(f32)).astype(bf16)


def levels_of(weight, step):
    ratios = weight.astype(f32) / step
    return jnp.floor(jnp.clip(ratios, -QMAX, QMAX) + 0.5)


def prep_body(
    pos, tok, go, iw, isc, ow, os_rows, ld_t, b_ref, c_ref,
    merged, o_keep, o_give, i_levels, run, run_t, up, down, up_t, down_t, bt, ct,
):
    c, z = pos[2], pos[3]
    s = (pos[0] * NX + pos[1]) * NC + c
    for i in range(4):
        at = slice(R * i, R * i + R)
        step = os_rows[pl.ds(4 * z + i, 1), :]
        merged[:T, at] = (go[:, at].astype(f32) * step).astype(bf16)
    merged[T:, :] = tok[...]
    square = (R, R)
    eye = iota(square, 0) == iota(square, 1)
    step = jnp.sum(jnp.where(eye, os_rows[pl.ds(s, 1), :], 0.0), axis=1, keepdims=True)
    out_lv = levels_of(ow[...], step).astype(bf16)
    i_levels[...] = levels_of(iw[...], isc[...]).astype(bf16)
    for core in range(2):
        mine, other = slice(256 * core, 256 * core + 256), slice(256 - 256 * core, 512 - 256 * core)

        @pl.when(c == core)
        def _():
            o_keep[0:R, :] = out_lv[:, mine]
            o_give[0:R, :] = out_lv[:, other]

    parts = split3(ld_t[...])
    tri = (iota((T, T), 0) >= iota((T, T), 1)).astype(bf16)
    cum = sum(dot(tri, p, 1, 1) for p in parts)
    cum_t = sum(dot(p, tri, 1, 1) for p in parts)
    total = cum[T - 1 : T, :]
    run[...] = cum
    run_t[...] = cum_t
    up[...] = jnp.exp(cum)
    down[...] = jnp.exp(total - cum)
    up_t[...] = jnp.exp(cum_t)
    down_t[...] = jnp.exp(cum_t[:, T - 1 : T] - cum_t)
    lane = iota((1, 256), 1) // HEAD_DIM
    rows = []
    for half in range(2):
        spread = jnp.zeros((1, 256), f32)
        for h in range(4):
            spread = jnp.where(lane == h, total[:, 4 * half + h : 4 * half + h + 1], spread)
        rows += [p.astype(f32) for p in split3(spread)]
    tile_row = iota((16, 256), 0)
    tile = jnp.zeros((16, 256), f32)
    for i, row in enumerate(rows):
        tile = jnp.where(tile_row == i, row, tile)
    o_keep[R:, :] = tile.astype(bf16)
    o_give[R:, :] = tile.astype(bf16)
    bt[...] = b_ref[...].astype(f32).T
    ct[...] = c_ref[...].astype(f32).T


def place(c, core_of, y, x, first, second):
    ch_y = jnp.where(core_of == 0, second, first)
    ch_x = jnp.where(core_of == 0, first, second)
    return lax.rem(y + ch_y, NY) * NX + lax.rem(x + ch_x, NX)


def assemble_body(pos, *refs):
    mine, theirs = refs[:4], refs[4:8]
    w_out, coef, table = refs[8:]
    y, x, c = pos[0], pos[1], pos[2]

    def copy(side, pieces, half):
        for e in range(4):

            def step(d, _):
                core = lax.rem(c + side, 2)
                chip = place(c, core, y, x, d, e)
                for r in range(2):
                    s = chip * NC + lax.rem(core + r, 2)
                    row = pl.multiple_of(s * R, R)
                    w_out[pl.ds(row, R), 256 * half : 256 * half + 256] = pieces[e][d, r, 0:R, :]
                    if side == 0:
                        tile = pieces[e][d, r, R:, :].astype(f32)
                        low = tile[0:1] + tile[1:2] + tile[2:3]
                        high = tile[3:4] + tile[4:5] + tile[5:6]
                        table[pl.ds(s, 1), :] = jnp.where(c == 0, low, high)
                return 0

            lax.fori_loop(0, 4, step, 0)

    for side, pieces in ((0, mine), (1, theirs)):
        for half in range(2):
            pl.when(lax.rem(c + side, 2) == half)(lambda: copy(side, pieces, half))

    chip0, row0 = (y * NX + x) * NC, y * NX * NC
    number = iota((NY * NX * NC, 1), 0)
    totals = table[...]

    def between(at, first, last, ok=None):
        inside = (number >= first) & (number <= last)
        value = jnp.exp(jnp.sum(jnp.where(inside, totals, 0.0), axis=0, keepdims=True))
        if ok is not None:
            value = jnp.where(ok, value, 0.0)
        coef[at : at + 1, :] = value

    between(0, chip0, chip0)
    between(1, chip0 + 1, chip0 + 1)
    for d in range(4):
        src = lax.rem(x - d + NX, NX)
        between(5 + d, row0 + src * NC + 2, row0 + NX * NC - 1)
        between(15 + d, row0, row0 + src * NC - 1)
        if d:
            between(1 + d, row0 + src * NC + 2, chip0 - 1, src < x)
            between(11 + d, chip0 + 2, row0 + src * NC - 1, src > x)
            src = lax.rem(y - d + NY, NY)
            between(8 + d, (src + 1) * NX * NC, chip0 - 1, src < y)
            between(18 + d, chip0 + 2, src * NX * NC - 1, src > y)
    coef[22:24, :] = jnp.zeros((2, 256), f32)


def fetch(blocks, into, sems, first, rows):
    for k, ref in zip(RELATIVE, blocks[:7]):
        pltpu.make_async_copy(ref.at[first : first + rows], into.at[k], sems.at[k]).start()
    if rows == 2 * T:
        pltpu.make_async_copy(blocks[7], into.at[4, 0:T], sems.at[4]).start()
        pltpu.make_async_copy(blocks[8], into.at[4, T : 2 * T], sems.at[4]).start()
    else:
        far = blocks[7 if first == 0 else 8]
        pltpu.make_async_copy(far, into.at[4], sems.at[4]).start()

    def wait(k):
        pltpu.make_async_copy(blocks[0].at[first : first + rows], into.at[k], sems.at[k]).wait()

    return wait


def fetch_rows(z, src, into, sems):
    def copy(k):
        row = pl.multiple_of(lax.rem(z + k, NZ) * W, W)
        return pltpu.make_async_copy(src.at[pl.ds(row, W), :], into.at[k], sems.at[k])

    for k in range(NZ):
        copy(k).start()
    return lambda k: copy(k).wait()


def each_z(step):
    def two(i, _):
        step(2 * i)
        step(2 * i + 1)
        return 0

    lax.fori_loop(0, NZ // 2, two, 0)


def project_body(pos, *refs):
    blocks = refs[:9]
    w_out, w_in, isc, up_t, down_t, bt, ct = refs[9:16]
    v_ref, g_ref, mine_ref, sib_ref = refs[16:20]
    held, wo, wi, acc_g, acc_v, sems, out_sems, in_sems = refs[20:]
    c, z = pos[2], pos[3]
    waits = (
        fetch_rows(z, w_out, wo, out_sems),
        fetch(blocks, held, sems, 0, 2 * T),
        fetch_rows(z, w_in, wi, in_sems),
    )
    acc_g[...] = jnp.zeros((T, W), f32)
    acc_v[...] = jnp.zeros((T, W), f32)

    def two(i, _):
        for k in (2 * i, 2 * i + 1):
            for wait in waits:
                wait(k)
        k, l = 2 * i, 2 * i + 1
        acc_g[...] += dot(held[k, :T, :], wo[k]) + dot(held[l, :T, :], wo[l])
        acc_v[...] += dot(held[k, T:, :], wi[k]) + dot(held[l, T:, :], wi[l])
        return 0

    lax.fori_loop(0, NZ // 2, two, 0)
    g_ref[...] = acc_g[...].astype(bf16)
    v_ref[...] = (acc_v[...] * isc[...]).astype(bf16)

    for base, vals, xt, ew in ((0, v_ref, bt, down_t), (2, g_ref, ct, up_t)):
        for j in range(PAIRS):
            vj = vals[:, 128 * j : 128 * j + 128]
            first = dot((xt[...] * ew[2 * j : 2 * j + 1, :]).astype(bf16), vj)
            second = dot((xt[...] * ew[2 * j + 1 : 2 * j + 2, :]).astype(bf16), vj)
            state = lane_pair(first, second).astype(bf16)

            @pl.when(c == j // 2)
            def _():
                mine_ref[base + j % 2] = state

            @pl.when(c != j // 2)
            def _():
                sib_ref[base + j % 2] = state


def pair_coef(coef, at, i):
    j = i % 2
    return coef[at : at + 1, 128 * j : 128 * j + 128]


def join_chip_body(pos, mine, other, coef, q):
    c = pos[2]
    for i in range(4):
        own, oth = mine[i].astype(f32), other[i].astype(f32)
        s0 = jnp.where(c == 0, own, oth)
        s1 = jnp.where(c == 0, oth, own)
        if i < 2:
            q[i] = (pair_coef(coef, 1, i) * s0 + s1).astype(bf16)
        else:
            q[i] = (s0 + pair_coef(coef, 0, i) * s1).astype(bf16)


def join_row_body(pos, q, g1, g2, g3, coef, u, enter):
    for i in range(4):
        near, end = (2, 5) if i < 2 else (12, 15)
        row = pair_coef(coef, end, i) * q[i].astype(f32)
        reach = jnp.zeros((N, 128), f32)
        for d, g in ((1, g1), (2, g2), (3, g3)):
            val = g[i].astype(f32)
            row += pair_coef(coef, end + d, i) * val
            reach += pair_coef(coef, near + d - 1, i) * val
        u[i] = row.astype(bf16)
        enter[i] = reach


def join_rows_body(pos, enter, g1, g2, g3, mine, other, coef, own, give):
    c = pos[2]
    for i in range(4):
        near = 9 if i < 2 else 19
        chip = enter[i]
        for d, g in ((1, g1), (2, g2), (3, g3)):
            chip += pair_coef(coef, near + d - 1, i) * g[i].astype(f32)
        o, t = mine[i].astype(f32), other[i].astype(f32)
        if i < 2:
            e0 = chip
            e1 = pair_coef(coef, 0, i) * chip + jnp.where(c == 0, o, t)
        else:
            e0 = pair_coef(coef, 1, i) * chip + jnp.where(c == 0, t, o)
            e1 = chip
        own[i] = jnp.where(c == 0, e0, e1).astype(bf16)
        give[i] = jnp.where(c == 0, e1, e0).astype(bf16)


STATES = sds((4, N, 128), bf16)


def exchange(pos, mine, sib, coef, first, second):
    other = swap(sib)
    (q,) = call(join_chip_body, "join_chip", [STATES], (pos, mine, other, coef))
    got = [axis_hop(q, dx=d) for d in (1, 2, 3)]
    *got, one = lax.optimization_barrier((*got, first()))
    u, enter = call(
        join_row_body, "join_row", [STATES, sds((4, N, 128), f32)], (pos, q, *got, coef)
    )
    got = [axis_hop(u, dy=d) for d in (1, 2, 3)]
    *got, two = lax.optimization_barrier((*got, second()))
    own, give = call(
        join_rows_body, "join_rows", [STATES, STATES], (pos, enter, *got, mine, other, coef)
    )
    return own, swap(give), one, two


def local_body(backward, pos, vals, b_ref, c_ref, a_ref, at_ref, out):
    row, col = iota((T, T), 0), iota((T, T), 1)
    first, second = (b_ref, c_ref) if backward else (c_ref, b_ref)
    meet = dot(first[...], second[...], 1, 1)
    keep = (col >= row) if backward else (row >= col)
    for j in range(PAIRS):
        vj = vals[:, 128 * j : 128 * j + 128]
        parts = []
        for h in (2 * j, 2 * j + 1):
            spread = a_ref[:, h : h + 1] - at_ref[h : h + 1, :]
            if backward:
                spread = -spread
            mix = jnp.exp(jnp.where(keep, spread, -1e30)) * meet
            parts.append(dot(mix.astype(bf16), vj))
        out[:, 128 * j : 128 * j + 128] = lane_pair(*parts)


def finish(c, base, local_ref, x_ref, eo_ref, mine_ref, sib_ref, j):
    at = base + j % 2
    state = jnp.where(c == j // 2, mine_ref[at].astype(f32), sib_ref[at].astype(f32)).astype(bf16)
    eo = lane_pair(eo_ref[:, 2 * j : 2 * j + 1], eo_ref[:, 2 * j + 1 : 2 * j + 2])
    return local_ref[:, 128 * j : 128 * j + 128] + eo * dot(x_ref[...], state)


def tokens_body(pos, w_in, gs_ref, out, held, buf, in_sems, out_sems):
    z = pos[3]
    wait = fetch_rows(z, w_in, held, in_sems)

    def back(k):
        return pltpu.make_async_copy(buf.at[k], out.at[lax.rem(z + k, NZ)], out_sems.at[k])

    def step(k):
        wait(k)
        buf[k] = dot(gs_ref[...], held[k], 1, 1).astype(bf16)
        back(k).start()

    each_z(step)
    for k in range(NZ):
        back(k).wait()


def store_total(pos, wait, held, right, keep, send, buf, out_sems):
    y, x, c, z = pos[0], pos[1], pos[2], pos[3]
    kept = pl.multiple_of(256 * c, 256)
    sent = pl.multiple_of(256 - 256 * c, 256)

    def back(k):
        copies = []
        for i in range(2):
            chip = lax.rem(z + k, NZ) * 2 + i
            dy = lax.rem(chip // NX - y + NY, NY)
            dx = lax.rem(lax.rem(chip, NX) - x + NX, NX)
            rows = slice(256 * i, 256 * i + 256)
            mine = keep.at[jnp.where(c == 0, dx, dy), jnp.where(c == 0, dy, dx)]
            other = send.at[jnp.where(c == 0, dy, dx), jnp.where(c == 0, dx, dy)]
            for j, (at, to) in enumerate(((kept, mine), (sent, other))):
                copies.append(
                    pltpu.make_async_copy(
                        buf.at[k, rows, pl.ds(at, 256)], to, out_sems.at[k, 2 * i + j]
                    )
                )
        return copies

    def step(k):
        wait(k)
        buf[k] = dot(held[k], right[...], 0, 0).astype(bf16)
        for copy in back(k):
            copy.start()

    each_z(step)

    def last(k, _):
        for copy in back(k):
            copy.wait()
        return 0

    lax.fori_loop(0, NZ, last, 0)


def in_total_body(pos, *refs):
    local_ref, x_ref, eo_ref, mine_ref, sib_ref, isc, keep, send, gs_ref = refs[9:18]
    held, buf, sems, out_sems, gb = refs[18:]
    wait = fetch(refs[:9], held, sems, T, T)
    for j in range(PAIRS):
        at = slice(128 * j, 128 * j + 128)
        vals = finish(pos[2], 2, local_ref, x_ref, eo_ref, mine_ref, sib_ref, j)
        gb[:, at] = vals.astype(bf16)
        gs_ref[:, at] = (vals * isc[:, at]).astype(bf16)
    store_total(pos, wait, held, gb, keep, send, buf, out_sems)


def out_total_body(pos, *refs):
    local_ref, x_ref, eo_ref, mine_ref, sib_ref, keep, send, held, buf, sems, out_sems, mb = refs[9:]
    wait = fetch(refs[:9], held, sems, 0, T)
    for j in range(PAIRS):
        at = slice(128 * j, 128 * j + 128)
        vals = finish(pos[2], 0, local_ref, x_ref, eo_ref, mine_ref, sib_ref, j)
        mb[:, at] = vals.astype(bf16)
    store_total(pos, wait, held, mb, keep, send, buf, out_sems)


TOTALS = [sds((4, 4, 256, 256), bf16)] * 2
MATMUL = 2 * T * D * W


def add(*parts):
    total = parts[0].astype(f32)
    for part in parts[1:]:
        total = total + part.astype(f32)
    return total


def scatter_seq(c, first, second, meanwhile):
    pairs = [(keep, after(swap(send), meanwhile)) for keep, send in (first, second)]

    def own(d):
        return jnp.stack([add(keep[d], came[d]) for keep, came in pairs], axis=1).astype(bf16)

    far = own(2)
    right = hop(far[:2], 1)
    left = hop(far[2:], -1)
    none = ((0, 0),) * 3
    near = add(own(1), jnp.pad(right, ((0, 2), *none))).astype(bf16)
    back = add(own(3), jnp.pad(left, ((2, 0), *none))).astype(bf16)
    total = add(own(0), hop(near, 1), hop(back, -1))
    got = [hop(total[d].astype(bf16), d, True) for d in (1, 2, 3)]
    total = add(total[0], *got)
    upper, lower = total[:, :R], total[:, R:]
    mine = jnp.where(c == 0, upper, lower)
    theirs = swap(jnp.where(c == 0, lower, upper))
    left, right = jnp.where(c == 0, mine, theirs), jnp.where(c == 0, theirs, mine)
    whole = jnp.concatenate([left, right], axis=2)
    return whole[0], whole[1]


def everyones(part, axis, count, copies):
    parts = jnp.broadcast_to(part, (count, copies, part.shape[1]))
    return jnp.sum(lax.all_to_all(parts, axis, 0, 0, tiled=True)[:, 0], axis=0)


def slopes_of(weight, step):
    ratios = weight.astype(f32) / step
    levels = jnp.floor(jnp.clip(ratios, -QMAX, QMAX) + 0.5)
    inside = jnp.abs(ratios) <= QMAX
    return jnp.where(inside, levels - ratios, levels), inside.astype(f32)


def per_device(
    tokens, grad_out, in_weight, in_scale, out_weight, out_scale, state_in, state_out, log_decay
):
    s = lax.axis_index("seq")
    z = lax.axis_index("tp")
    y, x, c = s // (NX * NC), (s // NC) % NX, s % NC
    pos = jnp.stack([y, x, c, z]).astype(jnp.int32)
    scale = in_scale[None, :]

    outs = [sds((2 * T, W), bf16)]
    outs += [sds((R + 16, 256), bf16)] * 2 + [sds((R, W), bf16)]
    outs += [sds((T, HP), f32), sds((HP, T), f32), sds((T, HP), f32), sds((T, HP), f32)]
    outs += [sds((HP, T), f32)] * 2 + [sds((N, T), f32)] * 2
    args = (
        pos, tokens, grad_out, in_weight, scale, out_weight,
        out_scale.reshape(NY * NX * NC, R), log_decay.T, state_in, state_out,
    )
    merged, o_keep, o_give, i_levels, run, run_t, up, down, up_t, down_t, bt, ct = call(
        prep_body, "prep", outs, args
    )

    w_in = lax.all_gather(i_levels, "seq", axis=0, tiled=True)
    out_own = jnp.stack([o_keep, swap(o_give)])
    out_row = jnp.stack([out_own] + [hop(out_own, -d) for d in (1, 2, 3)])
    out_all = [out_row] + [hop(out_row, -d, True) for d in (1, 2, 3)]
    blocks = gather_z(merged)
    w_out, coef = call(
        assemble_body,
        "assemble",
        [sds((D, W), bf16), sds((24, 256), f32)],
        (pos, *out_all, *[swap(v) for v in out_all]),
        10**6,
        [pltpu.VMEM((32, 256), f32)],
    )
    v, g, mine, sib = call(
        project_body,
        "project",
        [sds((T, W), bf16)] * 2 + [STATES] * 2,
        (pos, *blocks, w_out, w_in, scale, up_t, down_t, bt, ct),
        2 * MATMUL,
        [pltpu.VMEM((NZ, 2 * T, W), bf16)]
        + [pltpu.VMEM((NZ, W, W), bf16)] * 2
        + [pltpu.VMEM((T, W), f32)] * 2
        + [pltpu.SemaphoreType.DMA((NZ,))] * 3,
        away=11,
    )
    def local(backward, vals, name):
        return call(
            functools.partial(local_body, backward),
            name,
            [sds((T, W), f32)],
            (pos, vals, state_in, state_out, run, run_t),
            10**9,
        )[0]

    own, came, grad, mixed = exchange(
        pos, mine, sib, coef,
        lambda: local(True, g, "grad_local"),
        lambda: local(False, v, "mixed_local"),
    )
    wide = [pltpu.VMEM((T, W), bf16)]
    sems = [pltpu.SemaphoreType.DMA((NZ,))] * 2
    held = [
        pltpu.VMEM((NZ, T, W), bf16),
        pltpu.VMEM((NZ, W, W), bf16),
        pltpu.SemaphoreType.DMA((NZ,)),
        pltpu.SemaphoreType.DMA((NZ, 4)),
    ]
    in_keep, in_send, gs = call(
        in_total_body,
        "in_parts",
        TOTALS + [sds((T, W), bf16)],
        (pos, *blocks, grad, state_in, down, own, came, scale),
        MATMUL,
        held + wide,
        9,
        (0, 1),
    )
    out_keep, out_send = call(
        out_total_body,
        "out_parts",
        TOTALS,
        (pos, *blocks, mixed, state_out, up, own, came),
        MATMUL,
        held + wide,
        9,
        (0, 1),
    )
    (parts,) = call(
        tokens_body,
        "token_parts",
        [sds((NZ, T, W), bf16)],
        (pos, w_in, after(gs, out_keep)),
        MATMUL,
        [pltpu.VMEM((NZ, W, W), bf16), pltpu.VMEM((NZ, T, W), bf16)] + sems,
        away=1,
        out_away=(0,),
    )
    grad_tokens = lax.psum_scatter(
        parts.reshape(NZ * T, W), "tp", scatter_dimension=0, tiled=True
    )
    in_total, out_total = scatter_seq(c, (in_keep, in_send), (out_keep, out_send), parts)
    scale_rows = lax.dynamic_slice_in_dim(out_scale, s * R, R)[:, None]
    out_total = out_total / scale_rows

    in_slopes, in_inside = slopes_of(in_weight, scale)
    out_slopes, out_inside = slopes_of(out_weight, scale_rows)
    in_sum = jnp.sum(in_total * in_slopes, axis=0)[None]
    out_sum = jnp.sum(out_total * out_slopes, axis=1)[None]
    in_sum = everyones(in_sum, "seq", NY * NX * NC, 8)
    out_sum = everyones(out_sum, "tp", NZ, 1)
    return (
        grad_tokens,
        in_total * in_inside,
        in_sum / jnp.sqrt(f32(D * QMAX)),
        out_total * out_inside,
        out_sum / jnp.sqrt(f32(HEADS * HEAD_DIM * QMAX)),
    )


def solution(mesh):
    placed = (
        P("seq", "tp"),
        P("seq", "tp"),
        P("seq", "tp"),
        P("tp"),
        P("seq", "tp"),
        P(),
        P("seq", None),
        P("seq", None),
        P("seq", "tp"),
    )
    return jax.shard_map(
        per_device,
        mesh=mesh,
        in_specs=placed,
        out_specs=(P("seq", "tp"), P("seq", "tp"), P("tp"), P("seq", "tp"), P("seq")),
        check_vma=False,
    )
```

```python
import functools

import jax
import jax.numpy as jnp
from jax import lax
from jax.experimental import pallas as pl
from jax.experimental.pallas import tpu as pltpu
from jax.sharding import PartitionSpec as P

D = 4096
HEADS = 64
HEAD_DIM = 64
QMAX = 7

NY, NX, NC, NZ = 4, 4, 2, 8
T = 256
W = 512
R = 128
N = 128
HP = 8
PAIRS = 4

f32 = jnp.float32
bf16 = jnp.bfloat16


def seq_at(y, x, c):
    return ((y % NY) * NX + x % NX) * NC + c % NC


def hop(v, d, second=False):
    pairs = []
    for y in range(NY):
        for x in range(NX):
            for c in range(NC):
                along_x = (c == 0) != second
                to = seq_at(y, x + d, c) if along_x else seq_at(y + d, x, c)
                pairs.append((seq_at(y, x, c), to))
    return lax.ppermute(v, "seq", pairs)


def axis_hop(v, dy=0, dx=0):
    pairs = []
    for y in range(NY):
        for x in range(NX):
            for c in range(NC):
                pairs.append((seq_at(y, x, c), seq_at(y + dy, x + dx, c)))
    return lax.ppermute(v, "seq", pairs)


def seq_xor(v, bits):
    return lax.ppermute(v, "seq", [(s, s ^ bits) for s in range(NY * NX * NC)])


def swap(v):
    return seq_xor(v, 1)


def z_hop(v, d):
    return lax.ppermute(v, "tp", [(z, (z + d) % NZ) for z in range(NZ)])


def z_xor(v, b):
    return lax.ppermute(v, "tp", [(z, z ^ b) for z in range(NZ)])


def after(v, other):
    return lax.optimization_barrier((v, other))[0]


def gather_z(own):
    r1 = z_hop(own, 1)
    l1 = z_hop(own, -1)
    r2 = z_hop(r1, 1)
    l2 = z_hop(l1, -1)
    r3 = z_hop(r2, 1)
    l3 = z_hop(l2, -1)
    top = z_hop(r3[:T], 1)
    bot = z_hop(l3[T:], -1)
    return [own, l1, l2, l3, r3, r2, r1, top, bot]


RELATIVE = (0, 1, 2, 3, 5, 6, 7)
smem = pl.BlockSpec(memory_space=pltpu.SMEM)
vmem = pl.BlockSpec(memory_space=pltpu.VMEM)
anyw = pl.BlockSpec(memory_space=pl.ANY)


def sds(shape, dtype):
    return jax.ShapeDtypeStruct(shape, dtype)


def call(body, name, outs, args, flops=10**6, scratch=(), away=0, out_away=()):
    nbytes = sum(a.size * a.dtype.itemsize for a in args)
    nbytes += sum(o.size * o.dtype.itemsize for o in outs)
    return pl.pallas_call(
        body,
        out_shape=outs,
        in_specs=[smem] + [anyw] * away + [vmem] * (len(args) - 1 - away),
        out_specs=[anyw if i in out_away else vmem for i in range(len(outs))],
        scratch_shapes=scratch,
        compiler_params=pltpu.CompilerParams(vmem_limit_bytes=56 * 2**20),
        cost_estimate=pl.CostEstimate(flops=flops, bytes_accessed=nbytes, transcendentals=0),
        name=name,
    )(*args)


def dot(a, b, ca=1, cb=0):
    return lax.dot_general(a, b, (((ca,), (cb,)), ((), ())), preferred_element_type=f32)


def iota(shape, dim):
    return lax.broadcasted_iota(jnp.int32, shape, dim)


def lane_pair(first, second):
    return jnp.where(iota((1, 128), 1) < HEAD_DIM, first, second)


def split3(v):
    hi = v.astype(bf16)
    rest = v - hi.astype(f32)
    mid = rest.astype(bf16)
    return hi, mid, (rest - mid.astype(f32)).astype(bf16)


def levels_of(weight, step):
    ratios = weight.astype(f32) / step
    return jnp.floor(jnp.clip(ratios, -QMAX, QMAX) + 0.5)


def prep_body(
    pos, tok, go, iw, isc, ow, os_rows, ld_t, b_ref, c_ref,
    merged, o_keep, o_give, i_levels, run, run_t, up, down, up_t, down_t, bt, ct,
):
    c, z = pos[2], pos[3]
    s = (pos[0] * NX + pos[1]) * NC + c
    for i in range(4):
        at = slice(R * i, R * i + R)
        step = os_rows[pl.ds(4 * z + i, 1), :]
        merged[:T, at] = (go[:, at].astype(f32) * step).astype(bf16)
    merged[T:, :] = tok[...]
    square = (R, R)
    eye = iota(square, 0) == iota(square, 1)
    step = jnp.sum(jnp.where(eye, os_rows[pl.ds(s, 1), :], 0.0), axis=1, keepdims=True)
    out_lv = levels_of(ow[...], step).astype(bf16)
    i_levels[...] = levels_of(iw[...], isc[...]).astype(bf16)
    for core in range(2):
        mine, other = slice(256 * core, 256 * core + 256), slice(256 - 256 * core, 512 - 256 * core)

        @pl.when(c == core)
        def _():
            o_keep[0:R, :] = out_lv[:, mine]
            o_give[0:R, :] = out_lv[:, other]

    parts = split3(ld_t[...])
    tri = (iota((T, T), 0) >= iota((T, T), 1)).astype(bf16)
    cum = sum(dot(tri, p, 1, 1) for p in parts)
    cum_t = sum(dot(p, tri, 1, 1) for p in parts)
    total = cum[T - 1 : T, :]
    run[...] = cum
    run_t[...] = cum_t
    up[...] = jnp.exp(cum)
    down[...] = jnp.exp(total - cum)
    up_t[...] = jnp.exp(cum_t)
    down_t[...] = jnp.exp(cum_t[:, T - 1 : T] - cum_t)
    lane = iota((1, 256), 1) // HEAD_DIM
    rows = []
    for half in range(2):
        spread = jnp.zeros((1, 256), f32)
        for h in range(4):
            spread = jnp.where(lane == h, total[:, 4 * half + h : 4 * half + h + 1], spread)
        rows += [p.astype(f32) for p in split3(spread)]
    tile_row = iota((16, 256), 0)
    tile = jnp.zeros((16, 256), f32)
    for i, row in enumerate(rows):
        tile = jnp.where(tile_row == i, row, tile)
    o_keep[R:, :] = tile.astype(bf16)
    o_give[R:, :] = tile.astype(bf16)
    bt[...] = b_ref[...].astype(f32).T
    ct[...] = c_ref[...].astype(f32).T


def place(c, core_of, y, x, first, second):
    ch_y = jnp.where(core_of == 0, second, first)
    ch_x = jnp.where(core_of == 0, first, second)
    return lax.rem(y + ch_y, NY) * NX + lax.rem(x + ch_x, NX)


def assemble_body(pos, *refs):
    mine, theirs = refs[:4], [refs[4]] + [refs[5].at[i] for i in range(3)]
    w_out, coef, table = refs[6:]
    y, x, c = pos[0], pos[1], pos[2]

    def copy(side, pieces, half):
        for e in range(4):

            def step(d, _):
                core = lax.rem(c + side, 2)
                chip = place(c, core, y, x, d, e)
                for r in range(2):
                    s = chip * NC + lax.rem(core + r, 2)
                    row = pl.multiple_of(s * R, R)
                    w_out[pl.ds(row, R), 256 * half : 256 * half + 256] = pieces[e][d, r, 0:R, :]
                    if side == 0:
                        tile = pieces[e][d, r, R:, :].astype(f32)
                        low = tile[0:1] + tile[1:2] + tile[2:3]
                        high = tile[3:4] + tile[4:5] + tile[5:6]
                        table[pl.ds(s, 1), :] = jnp.where(c == 0, low, high)
                return 0

            lax.fori_loop(0, 4, step, 0)

    for side, pieces in ((0, mine), (1, theirs)):
        for half in range(2):
            pl.when(lax.rem(c + side, 2) == half)(lambda: copy(side, pieces, half))

    chip0, row0 = (y * NX + x) * NC, y * NX * NC
    number = iota((NY * NX * NC, 1), 0)
    totals = table[...]

    def between(at, first, last, ok=None):
        inside = (number >= first) & (number <= last)
        value = jnp.exp(jnp.sum(jnp.where(inside, totals, 0.0), axis=0, keepdims=True))
        if ok is not None:
            value = jnp.where(ok, value, 0.0)
        coef[at : at + 1, :] = value

    between(0, chip0, chip0)
    between(1, chip0 + 1, chip0 + 1)
    for d in range(4):
        src = lax.rem(x - d + NX, NX)
        between(5 + d, row0 + src * NC + 2, row0 + NX * NC - 1)
        between(15 + d, row0, row0 + src * NC - 1)
        if d:
            between(1 + d, row0 + src * NC + 2, chip0 - 1, src < x)
            between(11 + d, chip0 + 2, row0 + src * NC - 1, src > x)
            src = lax.rem(y - d + NY, NY)
            between(8 + d, (src + 1) * NX * NC, chip0 - 1, src < y)
            between(18 + d, chip0 + 2, src * NX * NC - 1, src > y)
    coef[22:24, :] = jnp.zeros((2, 256), f32)


def fetch(blocks, into, sems, first, rows):
    for k, ref in zip(RELATIVE, blocks[:7]):
        pltpu.make_async_copy(ref.at[first : first + rows], into.at[k], sems.at[k]).start()
    if rows == 2 * T:
        pltpu.make_async_copy(blocks[7], into.at[4, 0:T], sems.at[4]).start()
        pltpu.make_async_copy(blocks[8], into.at[4, T : 2 * T], sems.at[4]).start()
    else:
        far = blocks[7 if first == 0 else 8]
        pltpu.make_async_copy(far, into.at[4], sems.at[4]).start()

    def wait(k):
        pltpu.make_async_copy(blocks[0].at[first : first + rows], into.at[k], sems.at[k]).wait()

    return wait


def fetch_rows(z, src, into, sems):
    def copy(k):
        row = pl.multiple_of(lax.rem(z + k, NZ) * W, W)
        return pltpu.make_async_copy(src.at[pl.ds(row, W), :], into.at[k], sems.at[k])

    for k in range(NZ):
        copy(k).start()
    return lambda k: copy(k).wait()


def each_z(step):
    def two(i, _):
        step(2 * i)
        step(2 * i + 1)
        return 0

    lax.fori_loop(0, NZ // 2, two, 0)


def project_body(pos, *refs):
    blocks = refs[:9]
    w_out, w_in, isc, up_t, down_t, bt, ct = refs[9:16]
    v_ref, g_ref, mine_ref, sib_ref = refs[16:20]
    held, wo, wi, acc_g, acc_v, sems, out_sems, in_sems = refs[20:]
    c, z = pos[2], pos[3]
    waits = (
        fetch_rows(z, w_out, wo, out_sems),
        fetch(blocks, held, sems, 0, 2 * T),
        fetch_rows(z, w_in, wi, in_sems),
    )
    acc_g[...] = jnp.zeros((T, W), f32)
    acc_v[...] = jnp.zeros((T, W), f32)

    def two(i, _):
        for k in (2 * i, 2 * i + 1):
            for wait in waits:
                wait(k)
        k, l = 2 * i, 2 * i + 1
        acc_g[...] += dot(held[k, :T, :], wo[k]) + dot(held[l, :T, :], wo[l])
        acc_v[...] += dot(held[k, T:, :], wi[k]) + dot(held[l, T:, :], wi[l])
        return 0

    lax.fori_loop(0, NZ // 2, two, 0)
    g_ref[...] = acc_g[...].astype(bf16)
    v_ref[...] = (acc_v[...] * isc[...]).astype(bf16)

    for base, vals, xt, ew in ((0, v_ref, bt, down_t), (2, g_ref, ct, up_t)):
        for j in range(PAIRS):
            vj = vals[:, 128 * j : 128 * j + 128]
            first = dot((xt[...] * ew[2 * j : 2 * j + 1, :]).astype(bf16), vj)
            second = dot((xt[...] * ew[2 * j + 1 : 2 * j + 2, :]).astype(bf16), vj)
            state = lane_pair(first, second).astype(bf16)

            @pl.when(c == j // 2)
            def _():
                mine_ref[base + j % 2] = state

            @pl.when(c != j // 2)
            def _():
                sib_ref[base + j % 2] = state


def pair_coef(coef, at, i):
    j = i % 2
    return coef[at : at + 1, 128 * j : 128 * j + 128]


def join_chip_body(pos, mine, other, coef, q):
    c = pos[2]
    for i in range(4):
        own, oth = mine[i].astype(f32), other[i].astype(f32)
        s0 = jnp.where(c == 0, own, oth)
        s1 = jnp.where(c == 0, oth, own)
        if i < 2:
            q[i] = (pair_coef(coef, 1, i) * s0 + s1).astype(bf16)
        else:
            q[i] = (s0 + pair_coef(coef, 0, i) * s1).astype(bf16)


def join_row_body(pos, q, g1, g2, g3, coef, u, enter):
    for i in range(4):
        near, end = (2, 5) if i < 2 else (12, 15)
        row = pair_coef(coef, end, i) * q[i].astype(f32)
        reach = jnp.zeros((N, 128), f32)
        for d, g in ((1, g1), (2, g2), (3, g3)):
            val = g[i].astype(f32)
            row += pair_coef(coef, end + d, i) * val
            reach += pair_coef(coef, near + d - 1, i) * val
        u[i] = row.astype(bf16)
        enter[i] = reach


def join_rows_body(pos, enter, g1, g2, g3, mine, other, coef, own, give):
    c = pos[2]
    for i in range(4):
        near = 9 if i < 2 else 19
        chip = enter[i]
        for d, g in ((1, g1), (2, g2), (3, g3)):
            chip += pair_coef(coef, near + d - 1, i) * g[i].astype(f32)
        o, t = mine[i].astype(f32), other[i].astype(f32)
        if i < 2:
            e0 = chip
            e1 = pair_coef(coef, 0, i) * chip + jnp.where(c == 0, o, t)
        else:
            e0 = pair_coef(coef, 1, i) * chip + jnp.where(c == 0, t, o)
            e1 = chip
        own[i] = jnp.where(c == 0, e0, e1).astype(bf16)
        give[i] = jnp.where(c == 0, e1, e0).astype(bf16)


STATES = sds((4, N, 128), bf16)


def exchange(pos, mine, sib, coef, first, second):
    other = swap(sib)
    (q,) = call(join_chip_body, "join_chip", [STATES], (pos, mine, other, coef))
    got = [axis_hop(q, dx=d) for d in (1, 2, 3)]
    *got, one = lax.optimization_barrier((*got, first()))
    u, enter = call(
        join_row_body, "join_row", [STATES, sds((4, N, 128), f32)], (pos, q, *got, coef)
    )
    got = [axis_hop(u, dy=d) for d in (1, 2, 3)]
    *got, two = lax.optimization_barrier((*got, second()))
    own, give = call(
        join_rows_body, "join_rows", [STATES, STATES], (pos, enter, *got, mine, other, coef)
    )
    return own, swap(give), one, two


def local_body(backward, pos, vals, b_ref, c_ref, a_ref, at_ref, out):
    row, col = iota((T, T), 0), iota((T, T), 1)
    first, second = (b_ref, c_ref) if backward else (c_ref, b_ref)
    meet = dot(first[...], second[...], 1, 1)
    keep = (col >= row) if backward else (row >= col)
    for j in range(PAIRS):
        vj = vals[:, 128 * j : 128 * j + 128]
        parts = []
        for h in (2 * j, 2 * j + 1):
            spread = a_ref[:, h : h + 1] - at_ref[h : h + 1, :]
            if backward:
                spread = -spread
            mix = jnp.exp(jnp.where(keep, spread, -1e30)) * meet
            parts.append(dot(mix.astype(bf16), vj))
        out[:, 128 * j : 128 * j + 128] = lane_pair(*parts)


def finish(c, base, local_ref, x_ref, eo_ref, mine_ref, sib_ref, j):
    at = base + j % 2
    state = jnp.where(c == j // 2, mine_ref[at].astype(f32), sib_ref[at].astype(f32)).astype(bf16)
    eo = lane_pair(eo_ref[:, 2 * j : 2 * j + 1], eo_ref[:, 2 * j + 1 : 2 * j + 2])
    return local_ref[:, 128 * j : 128 * j + 128] + eo * dot(x_ref[...], state)


def tokens_body(pos, w_in, gs_ref, out, held, buf, in_sems, out_sems):
    z = pos[3]
    wait = fetch_rows(z, w_in, held, in_sems)

    def back(k):
        return pltpu.make_async_copy(buf.at[k], out.at[lax.rem(z + k, NZ)], out_sems.at[k])

    def step(k):
        wait(k)
        buf[k] = dot(gs_ref[...], held[k], 1, 1).astype(bf16)
        back(k).start()

    each_z(step)
    for k in range(NZ):
        back(k).wait()


def store_total(pos, wait, held, right, keep, send, buf, out_sems):
    y, x, c, z = pos[0], pos[1], pos[2], pos[3]
    kept = pl.multiple_of(256 * c, 256)
    sent = pl.multiple_of(256 - 256 * c, 256)

    def back(k):
        copies = []
        for i in range(2):
            chip = lax.rem(z + k, NZ) * 2 + i
            dy = lax.rem(chip // NX - y + NY, NY)
            dx = lax.rem(lax.rem(chip, NX) - x + NX, NX)
            rows = slice(256 * i, 256 * i + 256)
            mine = keep.at[jnp.where(c == 0, dx, dy), jnp.where(c == 0, dy, dx)]
            other = send.at[jnp.where(c == 0, dy, dx), jnp.where(c == 0, dx, dy)]
            for j, (at, to) in enumerate(((kept, mine), (sent, other))):
                copies.append(
                    pltpu.make_async_copy(
                        buf.at[k, rows, pl.ds(at, 256)], to, out_sems.at[k, 2 * i + j]
                    )
                )
        return copies

    def step(k):
        wait(k)
        buf[k] = dot(held[k], right[...], 0, 0).astype(bf16)
        for copy in back(k):
            copy.start()

    each_z(step)

    def last(k, _):
        for copy in back(k):
            copy.wait()
        return 0

    lax.fori_loop(0, NZ, last, 0)


def in_total_body(pos, *refs):
    local_ref, x_ref, eo_ref, mine_ref, sib_ref, isc, keep, send, gs_ref = refs[9:18]
    held, buf, sems, out_sems, gb = refs[18:]
    wait = fetch(refs[:9], held, sems, T, T)
    for j in range(PAIRS):
        at = slice(128 * j, 128 * j + 128)
        vals = finish(pos[2], 2, local_ref, x_ref, eo_ref, mine_ref, sib_ref, j)
        gb[:, at] = vals.astype(bf16)
        gs_ref[:, at] = (vals * isc[:, at]).astype(bf16)
    store_total(pos, wait, held, gb, keep, send, buf, out_sems)


def out_total_body(pos, *refs):
    local_ref, x_ref, eo_ref, mine_ref, sib_ref, keep, send, held, buf, sems, out_sems, mb = refs[9:]
    wait = fetch(refs[:9], held, sems, 0, T)
    for j in range(PAIRS):
        at = slice(128 * j, 128 * j + 128)
        vals = finish(pos[2], 0, local_ref, x_ref, eo_ref, mine_ref, sib_ref, j)
        mb[:, at] = vals.astype(bf16)
    store_total(pos, wait, held, mb, keep, send, buf, out_sems)


TOTALS = [sds((4, 4, 256, 256), bf16)] * 2
MATMUL = 2 * T * D * W


def add(*parts):
    total = parts[0].astype(f32)
    for part in parts[1:]:
        total = total + part.astype(f32)
    return total


def scatter_seq(c, first, second, meanwhile):
    pairs = [(keep, after(swap(send), meanwhile)) for keep, send in (first, second)]

    def own(d):
        return jnp.stack([add(keep[d], came[d]) for keep, came in pairs], axis=1).astype(bf16)

    far = own(2)
    right = hop(far[:2], 1)
    left = hop(far[2:], -1)
    none = ((0, 0),) * 3
    near = add(own(1), jnp.pad(right, ((0, 2), *none))).astype(bf16)
    back = add(own(3), jnp.pad(left, ((2, 0), *none))).astype(bf16)
    total = add(own(0), hop(near, 1), hop(back, -1))
    got = [hop(total[d].astype(bf16), d, True) for d in (1, 2, 3)]
    total = add(total[0], *got)
    upper, lower = total[:, :R], total[:, R:]
    mine = jnp.where(c == 0, upper, lower)
    theirs = swap(jnp.where(c == 0, lower, upper))
    left, right = jnp.where(c == 0, mine, theirs), jnp.where(c == 0, theirs, mine)
    whole = jnp.concatenate([left, right], axis=2)
    return whole[0], whole[1]


def everyones(part, axis, count, copies):
    parts = jnp.broadcast_to(part, (count, copies, part.shape[1]))
    return jnp.sum(lax.all_to_all(parts, axis, 0, 0, tiled=True)[:, 0], axis=0)


def slopes_of(weight, step):
    ratios = weight.astype(f32) / step
    levels = jnp.floor(jnp.clip(ratios, -QMAX, QMAX) + 0.5)
    inside = jnp.abs(ratios) <= QMAX
    return jnp.where(inside, levels - ratios, levels), inside.astype(f32)


def per_device(
    tokens, grad_out, in_weight, in_scale, out_weight, out_scale, state_in, state_out, log_decay
):
    s = lax.axis_index("seq")
    z = lax.axis_index("tp")
    y, x, c = s // (NX * NC), (s // NC) % NX, s % NC
    pos = jnp.stack([y, x, c, z]).astype(jnp.int32)
    scale = in_scale[None, :]

    outs = [sds((2 * T, W), bf16)]
    outs += [sds((R + 16, 256), bf16)] * 2 + [sds((R, W), bf16)]
    outs += [sds((T, HP), f32), sds((HP, T), f32), sds((T, HP), f32), sds((T, HP), f32)]
    outs += [sds((HP, T), f32)] * 2 + [sds((N, T), f32)] * 2
    args = (
        pos, tokens, grad_out, in_weight, scale, out_weight,
        out_scale.reshape(NY * NX * NC, R), log_decay.T, state_in, state_out,
    )
    merged, o_keep, o_give, i_levels, run, run_t, up, down, up_t, down_t, bt, ct = call(
        prep_body, "prep", outs, args
    )

    w_in = lax.all_gather(i_levels, "seq", axis=0, tiled=True)
    out_own = jnp.stack([o_keep, swap(o_give)])
    out_row = jnp.stack([out_own] + [hop(out_own, -d) for d in (1, 2, 3)])
    blocks = gather_z(merged)
    out_row = after(out_row, (blocks[1], blocks[6]))
    out_all = [out_row] + [hop(out_row, -d, True) for d in (1, 2, 3)]
    rest = jnp.stack(after(out_all[1:], (blocks[3], blocks[4])))
    w_out, coef = call(
        assemble_body,
        "assemble",
        [sds((D, W), bf16), sds((24, 256), f32)],
        (pos, *out_all, swap(out_row), swap(rest)),
        10**6,
        [pltpu.VMEM((32, 256), f32)],
    )
    v, g, mine, sib = call(
        project_body,
        "project",
        [sds((T, W), bf16)] * 2 + [STATES] * 2,
        (pos, *blocks, w_out, w_in, scale, up_t, down_t, bt, ct),
        2 * MATMUL,
        [pltpu.VMEM((NZ, 2 * T, W), bf16)]
        + [pltpu.VMEM((NZ, W, W), bf16)] * 2
        + [pltpu.VMEM((T, W), f32)] * 2
        + [pltpu.SemaphoreType.DMA((NZ,))] * 3,
        away=11,
    )
    def local(backward, vals, name):
        return call(
            functools.partial(local_body, backward),
            name,
            [sds((T, W), f32)],
            (pos, vals, state_in, state_out, run, run_t),
            10**9,
        )[0]

    own, came, grad, mixed = exchange(
        pos, mine, sib, coef,
        lambda: local(True, g, "grad_local"),
        lambda: local(False, v, "mixed_local"),
    )
    wide = [pltpu.VMEM((T, W), bf16)]
    sems = [pltpu.SemaphoreType.DMA((NZ,))] * 2
    held = [
        pltpu.VMEM((NZ, T, W), bf16),
        pltpu.VMEM((NZ, W, W), bf16),
        pltpu.SemaphoreType.DMA((NZ,)),
        pltpu.SemaphoreType.DMA((NZ, 4)),
    ]
    in_keep, in_send, gs = call(
        in_total_body,
        "in_parts",
        TOTALS + [sds((T, W), bf16)],
        (pos, *blocks, grad, state_in, down, own, came, scale),
        MATMUL,
        held + wide,
        9,
        (0, 1),
    )
    out_keep, out_send = call(
        out_total_body,
        "out_parts",
        TOTALS,
        (pos, *blocks, mixed, state_out, up, own, came),
        MATMUL,
        held + wide,
        9,
        (0, 1),
    )
    (parts,) = call(
        tokens_body,
        "token_parts",
        [sds((NZ, T, W), bf16)],
        (pos, w_in, after(gs, out_keep)),
        MATMUL,
        [pltpu.VMEM((NZ, W, W), bf16), pltpu.VMEM((NZ, T, W), bf16)] + sems,
        away=1,
        out_away=(0,),
    )
    grad_tokens = lax.psum_scatter(
        parts.reshape(NZ * T, W), "tp", scatter_dimension=0, tiled=True
    )
    in_total, out_total = scatter_seq(c, (in_keep, in_send), (out_keep, out_send), parts)
    scale_rows = lax.dynamic_slice_in_dim(out_scale, s * R, R)[:, None]
    out_total = out_total / scale_rows

    in_slopes, in_inside = slopes_of(in_weight, scale)
    out_slopes, out_inside = slopes_of(out_weight, scale_rows)
    in_sum = jnp.sum(in_total * in_slopes, axis=0)[None]
    out_sum = jnp.sum(out_total * out_slopes, axis=1)[None]
    in_sum = everyones(in_sum, "seq", NY * NX * NC, 8)
    for bits in (1, 2, 4):
        out_sum = out_sum + z_xor(out_sum, bits)
    out_sum = out_sum[0]
    return (
        grad_tokens,
        in_total * in_inside,
        in_sum / jnp.sqrt(f32(D * QMAX)),
        out_total * out_inside,
        out_sum / jnp.sqrt(f32(HEADS * HEAD_DIM * QMAX)),
    )


def solution(mesh):
    placed = (
        P("seq", "tp"),
        P("seq", "tp"),
        P("seq", "tp"),
        P("tp"),
        P("seq", "tp"),
        P(),
        P("seq", None),
        P("seq", None),
        P("seq", "tp"),
    )
    return jax.shard_map(
        per_device,
        mesh=mesh,
        in_specs=placed,
        out_specs=(P("seq", "tp"), P("seq", "tp"), P("tp"), P("seq", "tp"), P("seq")),
        check_vma=False,
    )
```

```python
import functools

import jax
import jax.numpy as jnp
from jax import lax
from jax.experimental import pallas as pl
from jax.experimental.pallas import tpu as pltpu
from jax.sharding import PartitionSpec as P

D = 4096
HEADS = 64
HEAD_DIM = 64
QMAX = 7

NY, NX, NC, NZ = 4, 4, 2, 8
T = 256
W = 512
R = 128
N = 128
HP = 8
PAIRS = 4

f32 = jnp.float32
bf16 = jnp.bfloat16


def seq_at(y, x, c):
    return ((y % NY) * NX + x % NX) * NC + c % NC


def hop(v, d, second=False):
    pairs = []
    for y in range(NY):
        for x in range(NX):
            for c in range(NC):
                along_x = (c == 0) != second
                to = seq_at(y, x + d, c) if along_x else seq_at(y + d, x, c)
                pairs.append((seq_at(y, x, c), to))
    return lax.ppermute(v, "seq", pairs)


def axis_hop(v, dy=0, dx=0):
    pairs = []
    for y in range(NY):
        for x in range(NX):
            for c in range(NC):
                pairs.append((seq_at(y, x, c), seq_at(y + dy, x + dx, c)))
    return lax.ppermute(v, "seq", pairs)


def seq_xor(v, bits):
    return lax.ppermute(v, "seq", [(s, s ^ bits) for s in range(NY * NX * NC)])


def swap(v):
    return seq_xor(v, 1)


def z_hop(v, d):
    return lax.ppermute(v, "tp", [(z, (z + d) % NZ) for z in range(NZ)])


def z_xor(v, b):
    return lax.ppermute(v, "tp", [(z, z ^ b) for z in range(NZ)])


def after(v, other):
    return lax.optimization_barrier((v, other))[0]


def gather_z(own):
    r1 = z_hop(own, 1)
    l1 = z_hop(own, -1)
    r2 = z_hop(r1, 1)
    l2 = z_hop(l1, -1)
    r3 = z_hop(r2, 1)
    l3 = z_hop(l2, -1)
    top = z_hop(r3[:T], 1)
    bot = z_hop(l3[T:], -1)
    return [own, l1, l2, l3, r3, r2, r1, top, bot]


RELATIVE = (0, 1, 2, 3, 5, 6, 7)
smem = pl.BlockSpec(memory_space=pltpu.SMEM)
vmem = pl.BlockSpec(memory_space=pltpu.VMEM)
anyw = pl.BlockSpec(memory_space=pl.ANY)


def sds(shape, dtype):
    return jax.ShapeDtypeStruct(shape, dtype)


def call(body, name, outs, args, flops=10**6, scratch=(), away=0, out_away=()):
    nbytes = sum(a.size * a.dtype.itemsize for a in args)
    nbytes += sum(o.size * o.dtype.itemsize for o in outs)
    return pl.pallas_call(
        body,
        out_shape=outs,
        in_specs=[smem] + [anyw] * away + [vmem] * (len(args) - 1 - away),
        out_specs=[anyw if i in out_away else vmem for i in range(len(outs))],
        scratch_shapes=scratch,
        compiler_params=pltpu.CompilerParams(vmem_limit_bytes=56 * 2**20),
        cost_estimate=pl.CostEstimate(flops=flops, bytes_accessed=nbytes, transcendentals=0),
        name=name,
    )(*args)


def dot(a, b, ca=1, cb=0):
    return lax.dot_general(a, b, (((ca,), (cb,)), ((), ())), preferred_element_type=f32)


def iota(shape, dim):
    return lax.broadcasted_iota(jnp.int32, shape, dim)


def lane_pair(first, second):
    return jnp.where(iota((1, 128), 1) < HEAD_DIM, first, second)


def split3(v):
    hi = v.astype(bf16)
    rest = v - hi.astype(f32)
    mid = rest.astype(bf16)
    return hi, mid, (rest - mid.astype(f32)).astype(bf16)


def levels_of(weight, step):
    ratios = weight.astype(f32) / step
    return jnp.floor(jnp.clip(ratios, -QMAX, QMAX) + 0.5)


def prep_body(
    pos, tok, go, iw, isc, ow, os_rows, ld_t, b_ref, c_ref,
    merged, o_keep, o_give, i_levels, run, run_t, up, down, up_t, down_t, bt, ct,
):
    c, z = pos[2], pos[3]
    s = (pos[0] * NX + pos[1]) * NC + c
    for i in range(4):
        at = slice(R * i, R * i + R)
        step = os_rows[pl.ds(4 * z + i, 1), :]
        merged[:T, at] = (go[:, at].astype(f32) * step).astype(bf16)
    merged[T:, :] = tok[...]
    square = (R, R)
    eye = iota(square, 0) == iota(square, 1)
    step = jnp.sum(jnp.where(eye, os_rows[pl.ds(s, 1), :], 0.0), axis=1, keepdims=True)
    out_lv = levels_of(ow[...], step).astype(bf16)
    i_levels[...] = levels_of(iw[...], isc[...]).astype(bf16)
    for core in range(2):
        mine, other = slice(256 * core, 256 * core + 256), slice(256 - 256 * core, 512 - 256 * core)

        @pl.when(c == core)
        def _():
            o_keep[0:R, :] = out_lv[:, mine]
            o_give[0:R, :] = out_lv[:, other]

    parts = split3(ld_t[...])
    tri = (iota((T, T), 0) >= iota((T, T), 1)).astype(bf16)
    cum = sum(dot(tri, p, 1, 1) for p in parts)
    cum_t = sum(dot(p, tri, 1, 1) for p in parts)
    total = cum[T - 1 : T, :]
    run[...] = cum
    run_t[...] = cum_t
    up[...] = jnp.exp(cum)
    down[...] = jnp.exp(total - cum)
    up_t[...] = jnp.exp(cum_t)
    down_t[...] = jnp.exp(cum_t[:, T - 1 : T] - cum_t)
    lane = iota((1, 256), 1) // HEAD_DIM
    rows = []
    for half in range(2):
        spread = jnp.zeros((1, 256), f32)
        for h in range(4):
            spread = jnp.where(lane == h, total[:, 4 * half + h : 4 * half + h + 1], spread)
        rows += [p.astype(f32) for p in split3(spread)]
    tile_row = iota((16, 256), 0)
    tile = jnp.zeros((16, 256), f32)
    for i, row in enumerate(rows):
        tile = jnp.where(tile_row == i, row, tile)
    o_keep[R:, :] = tile.astype(bf16)
    o_give[R:, :] = tile.astype(bf16)
    bt[...] = b_ref[...].astype(f32).T
    ct[...] = c_ref[...].astype(f32).T


def place(c, core_of, y, x, first, second):
    ch_y = jnp.where(core_of == 0, second, first)
    ch_x = jnp.where(core_of == 0, first, second)
    return lax.rem(y + ch_y, NY) * NX + lax.rem(x + ch_x, NX)


def assemble_body(pos, *refs):
    mine, theirs = refs[:4], refs[4:8]
    w_out, coef, table = refs[8:]
    y, x, c = pos[0], pos[1], pos[2]

    def copy(side, pieces, half):
        for e in range(4):

            def step(d, _):
                core = lax.rem(c + side, 2)
                chip = place(c, core, y, x, d, e)
                for r in range(2):
                    s = chip * NC + lax.rem(core + r, 2)
                    row = pl.multiple_of(s * R, R)
                    w_out[pl.ds(row, R), 256 * half : 256 * half + 256] = pieces[e][d, r, 0:R, :]
                    if side == 0:
                        tile = pieces[e][d, r, R:, :].astype(f32)
                        low = tile[0:1] + tile[1:2] + tile[2:3]
                        high = tile[3:4] + tile[4:5] + tile[5:6]
                        table[pl.ds(s, 1), :] = jnp.where(c == 0, low, high)
                return 0

            lax.fori_loop(0, 4, step, 0)

    for side, pieces in ((0, mine), (1, theirs)):
        for half in range(2):
            pl.when(lax.rem(c + side, 2) == half)(lambda: copy(side, pieces, half))

    chip0, row0 = (y * NX + x) * NC, y * NX * NC
    number = iota((NY * NX * NC, 1), 0)
    totals = table[...]

    def between(at, first, last, ok=None):
        inside = (number >= first) & (number <= last)
        value = jnp.exp(jnp.sum(jnp.where(inside, totals, 0.0), axis=0, keepdims=True))
        if ok is not None:
            value = jnp.where(ok, value, 0.0)
        coef[at : at + 1, :] = value

    between(0, chip0, chip0)
    between(1, chip0 + 1, chip0 + 1)
    for d in range(4):
        src = lax.rem(x - d + NX, NX)
        between(5 + d, row0 + src * NC + 2, row0 + NX * NC - 1)
        between(15 + d, row0, row0 + src * NC - 1)
        if d:
            between(1 + d, row0 + src * NC + 2, chip0 - 1, src < x)
            between(11 + d, chip0 + 2, row0 + src * NC - 1, src > x)
            src = lax.rem(y - d + NY, NY)
            between(8 + d, (src + 1) * NX * NC, chip0 - 1, src < y)
            between(18 + d, chip0 + 2, src * NX * NC - 1, src > y)
    coef[22:24, :] = jnp.zeros((2, 256), f32)


def fetch(blocks, into, sems, first, rows):
    for k, ref in zip(RELATIVE, blocks[:7]):
        pltpu.make_async_copy(ref.at[first : first + rows], into.at[k], sems.at[k]).start()
    if rows == 2 * T:
        pltpu.make_async_copy(blocks[7], into.at[4, 0:T], sems.at[4]).start()
        pltpu.make_async_copy(blocks[8], into.at[4, T : 2 * T], sems.at[4]).start()
    else:
        far = blocks[7 if first == 0 else 8]
        pltpu.make_async_copy(far, into.at[4], sems.at[4]).start()

    def wait(k):
        pltpu.make_async_copy(blocks[0].at[first : first + rows], into.at[k], sems.at[k]).wait()

    return wait


def fetch_rows(z, src, into, sems):
    def copy(k):
        row = pl.multiple_of(lax.rem(z + k, NZ) * W, W)
        return pltpu.make_async_copy(src.at[pl.ds(row, W), :], into.at[k], sems.at[k])

    for k in range(NZ):
        copy(k).start()
    return lambda k: copy(k).wait()


def each_z(step):
    def one(k, _):
        step(k)
        return 0

    lax.fori_loop(0, NZ, one, 0)


def project_body(pos, *refs):
    blocks = refs[:9]
    w_out, w_in, isc, up_t, down_t, bt, ct = refs[9:16]
    v_ref, g_ref, mine_ref, sib_ref = refs[16:20]
    held, wo, wi, acc_g, acc_v, sems, out_sems, in_sems = refs[20:]
    c, z = pos[2], pos[3]
    waits = (
        fetch_rows(z, w_out, wo, out_sems),
        fetch(blocks, held, sems, 0, 2 * T),
        fetch_rows(z, w_in, wi, in_sems),
    )
    acc_g[...] = jnp.zeros((T, W), f32)
    acc_v[...] = jnp.zeros((T, W), f32)

    def two(i, _):
        for k in (2 * i, 2 * i + 1):
            for wait in waits:
                wait(k)
        k, l = 2 * i, 2 * i + 1
        acc_g[...] += dot(held[k, :T, :], wo[k]) + dot(held[l, :T, :], wo[l])
        acc_v[...] += dot(held[k, T:, :], wi[k]) + dot(held[l, T:, :], wi[l])
        return 0

    lax.fori_loop(0, NZ // 2, two, 0)
    g_ref[...] = acc_g[...].astype(bf16)
    v_ref[...] = (acc_v[...] * isc[...]).astype(bf16)

    for base, vals, xt, ew in ((0, v_ref, bt, down_t), (2, g_ref, ct, up_t)):
        for j in range(PAIRS):
            vj = vals[:, 128 * j : 128 * j + 128]
            first = dot((xt[...] * ew[2 * j : 2 * j + 1, :]).astype(bf16), vj)
            second = dot((xt[...] * ew[2 * j + 1 : 2 * j + 2, :]).astype(bf16), vj)
            state = lane_pair(first, second).astype(bf16)

            @pl.when(c == j // 2)
            def _():
                mine_ref[base + j % 2] = state

            @pl.when(c != j // 2)
            def _():
                sib_ref[base + j % 2] = state


def pair_coef(coef, at, i):
    j = i % 2
    return coef[at : at + 1, 128 * j : 128 * j + 128]


def join_chip_body(pos, mine, other, coef, q):
    c = pos[2]
    for i in range(4):
        own, oth = mine[i].astype(f32), other[i].astype(f32)
        s0 = jnp.where(c == 0, own, oth)
        s1 = jnp.where(c == 0, oth, own)
        if i < 2:
            q[i] = (pair_coef(coef, 1, i) * s0 + s1).astype(bf16)
        else:
            q[i] = (s0 + pair_coef(coef, 0, i) * s1).astype(bf16)


def join_row_body(pos, q, g1, g2, g3, coef, u, enter):
    for i in range(4):
        near, end = (2, 5) if i < 2 else (12, 15)
        row = pair_coef(coef, end, i) * q[i].astype(f32)
        reach = jnp.zeros((N, 128), f32)
        for d, g in ((1, g1), (2, g2), (3, g3)):
            val = g[i].astype(f32)
            row += pair_coef(coef, end + d, i) * val
            reach += pair_coef(coef, near + d - 1, i) * val
        u[i] = row.astype(bf16)
        enter[i] = reach


def join_rows_body(pos, enter, g1, g2, g3, mine, other, coef, own, give):
    c = pos[2]
    for i in range(4):
        near = 9 if i < 2 else 19
        chip = enter[i]
        for d, g in ((1, g1), (2, g2), (3, g3)):
            chip += pair_coef(coef, near + d - 1, i) * g[i].astype(f32)
        o, t = mine[i].astype(f32), other[i].astype(f32)
        if i < 2:
            e0 = chip
            e1 = pair_coef(coef, 0, i) * chip + jnp.where(c == 0, o, t)
        else:
            e0 = pair_coef(coef, 1, i) * chip + jnp.where(c == 0, t, o)
            e1 = chip
        own[i] = jnp.where(c == 0, e0, e1).astype(bf16)
        give[i] = jnp.where(c == 0, e1, e0).astype(bf16)


STATES = sds((4, N, 128), bf16)


def exchange(pos, mine, sib, coef, first, second):
    other = swap(sib)
    (q,) = call(join_chip_body, "join_chip", [STATES], (pos, mine, other, coef))
    got = [axis_hop(q, dx=d) for d in (1, 2, 3)]
    *got, one = lax.optimization_barrier((*got, first()))
    u, enter = call(
        join_row_body, "join_row", [STATES, sds((4, N, 128), f32)], (pos, q, *got, coef)
    )
    got = [axis_hop(u, dy=d) for d in (1, 2, 3)]
    *got, two = lax.optimization_barrier((*got, second()))
    own, give = call(
        join_rows_body, "join_rows", [STATES, STATES], (pos, enter, *got, mine, other, coef)
    )
    return own, swap(give), one, two


def local_body(backward, pos, vals, b_ref, c_ref, a_ref, at_ref, out):
    row, col = iota((T, T), 0), iota((T, T), 1)
    first, second = (b_ref, c_ref) if backward else (c_ref, b_ref)
    meet = dot(first[...], second[...], 1, 1)
    keep = (col >= row) if backward else (row >= col)
    for j in range(PAIRS):
        vj = vals[:, 128 * j : 128 * j + 128]
        parts = []
        for h in (2 * j, 2 * j + 1):
            spread = a_ref[:, h : h + 1] - at_ref[h : h + 1, :]
            if backward:
                spread = -spread
            mix = jnp.exp(jnp.where(keep, spread, -1e30)) * meet
            parts.append(dot(mix.astype(bf16), vj))
        out[:, 128 * j : 128 * j + 128] = lane_pair(*parts)


def finish(c, base, local_ref, x_ref, eo_ref, mine_ref, sib_ref, j):
    at = base + j % 2
    state = jnp.where(c == j // 2, mine_ref[at].astype(f32), sib_ref[at].astype(f32)).astype(bf16)
    eo = lane_pair(eo_ref[:, 2 * j : 2 * j + 1], eo_ref[:, 2 * j + 1 : 2 * j + 2])
    return local_ref[:, 128 * j : 128 * j + 128] + eo * dot(x_ref[...], state)


def tokens_body(pos, w_in, gs_ref, out, held, buf, in_sems, out_sems):
    z = pos[3]
    wait = fetch_rows(z, w_in, held, in_sems)

    def back(k):
        return pltpu.make_async_copy(buf.at[k], out.at[lax.rem(z + k, NZ)], out_sems.at[k])

    def step(k):
        wait(k)
        buf[k] = dot(gs_ref[...], held[k], 1, 1).astype(bf16)
        back(k).start()

    each_z(step)
    for k in range(NZ):
        back(k).wait()


def store_total(pos, wait, held, right, keep, send, buf, out_sems):
    y, x, c, z = pos[0], pos[1], pos[2], pos[3]
    kept = pl.multiple_of(256 * c, 256)
    sent = pl.multiple_of(256 - 256 * c, 256)

    def back(k):
        copies = []
        for i in range(2):
            chip = lax.rem(z + k, NZ) * 2 + i
            dy = lax.rem(chip // NX - y + NY, NY)
            dx = lax.rem(lax.rem(chip, NX) - x + NX, NX)
            rows = slice(256 * i, 256 * i + 256)
            mine = keep.at[jnp.where(c == 0, dx, dy), jnp.where(c == 0, dy, dx)]
            other = send.at[jnp.where(c == 0, dy, dx), jnp.where(c == 0, dx, dy)]
            for j, (at, to) in enumerate(((kept, mine), (sent, other))):
                copies.append(
                    pltpu.make_async_copy(
                        buf.at[k, rows, pl.ds(at, 256)], to, out_sems.at[k, 2 * i + j]
                    )
                )
        return copies

    def step(k):
        wait(k)
        buf[k] = dot(held[k], right[...], 0, 0).astype(bf16)
        for copy in back(k):
            copy.start()

    each_z(step)

    def last(k, _):
        for copy in back(k):
            copy.wait()
        return 0

    lax.fori_loop(0, NZ, last, 0)


def in_total_body(pos, *refs):
    local_ref, x_ref, eo_ref, mine_ref, sib_ref, isc, keep, send, gs_ref = refs[9:18]
    held, buf, sems, out_sems, gb = refs[18:]
    wait = fetch(refs[:9], held, sems, T, T)
    for j in range(PAIRS):
        at = slice(128 * j, 128 * j + 128)
        vals = finish(pos[2], 2, local_ref, x_ref, eo_ref, mine_ref, sib_ref, j)
        gb[:, at] = vals.astype(bf16)
        gs_ref[:, at] = (vals * isc[:, at]).astype(bf16)
    store_total(pos, wait, held, gb, keep, send, buf, out_sems)


def out_total_body(pos, *refs):
    local_ref, x_ref, eo_ref, mine_ref, sib_ref, keep, send, held, buf, sems, out_sems, mb = refs[9:]
    wait = fetch(refs[:9], held, sems, 0, T)
    for j in range(PAIRS):
        at = slice(128 * j, 128 * j + 128)
        vals = finish(pos[2], 0, local_ref, x_ref, eo_ref, mine_ref, sib_ref, j)
        mb[:, at] = vals.astype(bf16)
    store_total(pos, wait, held, mb, keep, send, buf, out_sems)


TOTALS = [sds((4, 4, 256, 256), bf16)] * 2
MATMUL = 2 * T * D * W


def add(*parts):
    total = parts[0].astype(f32)
    for part in parts[1:]:
        total = total + part.astype(f32)
    return total


def scatter_seq(c, first, second, meanwhile):
    pairs = [(keep, after(swap(send), meanwhile)) for keep, send in (first, second)]

    def own(d):
        return jnp.stack([add(keep[d], came[d]) for keep, came in pairs], axis=1).astype(bf16)

    far = own(2)
    right = hop(far[:2], 1)
    left = hop(far[2:], -1)
    none = ((0, 0),) * 3
    near = add(own(1), jnp.pad(right, ((0, 2), *none))).astype(bf16)
    back = add(own(3), jnp.pad(left, ((2, 0), *none))).astype(bf16)
    total = add(own(0), hop(near, 1), hop(back, -1))
    got = [hop(total[d].astype(bf16), d, True) for d in (1, 2, 3)]
    total = add(total[0], *got)
    upper, lower = total[:, :R], total[:, R:]
    mine = jnp.where(c == 0, upper, lower)
    theirs = swap(jnp.where(c == 0, lower, upper))
    left, right = jnp.where(c == 0, mine, theirs), jnp.where(c == 0, theirs, mine)
    whole = jnp.concatenate([left, right], axis=2)
    return whole[0], whole[1]


def everyones(part, axis, count, copies):
    parts = jnp.broadcast_to(part, (count, copies, part.shape[1]))
    return jnp.sum(lax.all_to_all(parts, axis, 0, 0, tiled=True)[:, 0], axis=0)


def slopes_of(weight, step):
    ratios = weight.astype(f32) / step
    levels = jnp.floor(jnp.clip(ratios, -QMAX, QMAX) + 0.5)
    inside = jnp.abs(ratios) <= QMAX
    return jnp.where(inside, levels - ratios, levels), inside.astype(f32)


def per_device(
    tokens, grad_out, in_weight, in_scale, out_weight, out_scale, state_in, state_out, log_decay
):
    s = lax.axis_index("seq")
    z = lax.axis_index("tp")
    y, x, c = s // (NX * NC), (s // NC) % NX, s % NC
    pos = jnp.stack([y, x, c, z]).astype(jnp.int32)
    scale = in_scale[None, :]

    outs = [sds((2 * T, W), bf16)]
    outs += [sds((R + 16, 256), bf16)] * 2 + [sds((R, W), bf16)]
    outs += [sds((T, HP), f32), sds((HP, T), f32), sds((T, HP), f32), sds((T, HP), f32)]
    outs += [sds((HP, T), f32)] * 2 + [sds((N, T), f32)] * 2
    args = (
        pos, tokens, grad_out, in_weight, scale, out_weight,
        out_scale.reshape(NY * NX * NC, R), log_decay.T, state_in, state_out,
    )
    merged, o_keep, o_give, i_levels, run, run_t, up, down, up_t, down_t, bt, ct = call(
        prep_body, "prep", outs, args
    )

    w_in = lax.all_gather(i_levels, "seq", axis=0, tiled=True)
    out_own = jnp.stack([o_keep, swap(o_give)])
    out_row = jnp.stack([out_own] + [hop(out_own, -d) for d in (1, 2, 3)])
    out_all = [out_row] + [hop(out_row, -d, True) for d in (1, 2, 3)]
    blocks = gather_z(merged)
    w_out, coef = call(
        assemble_body,
        "assemble",
        [sds((D, W), bf16), sds((24, 256), f32)],
        (pos, *out_all, *[swap(v) for v in out_all]),
        10**6,
        [pltpu.VMEM((32, 256), f32)],
    )
    v, g, mine, sib = call(
        project_body,
        "project",
        [sds((T, W), bf16)] * 2 + [STATES] * 2,
        (pos, *blocks, w_out, w_in, scale, up_t, down_t, bt, ct),
        2 * MATMUL,
        [pltpu.VMEM((NZ, 2 * T, W), bf16)]
        + [pltpu.VMEM((NZ, W, W), bf16)] * 2
        + [pltpu.VMEM((T, W), f32)] * 2
        + [pltpu.SemaphoreType.DMA((NZ,))] * 3,
        away=11,
    )
    def local(backward, vals, name):
        return call(
            functools.partial(local_body, backward),
            name,
            [sds((T, W), f32)],
            (pos, vals, state_in, state_out, run, run_t),
            10**9,
        )[0]

    own, came, grad, mixed = exchange(
        pos, mine, sib, coef,
        lambda: local(True, g, "grad_local"),
        lambda: local(False, v, "mixed_local"),
    )
    wide = [pltpu.VMEM((T, W), bf16)]
    sems = [pltpu.SemaphoreType.DMA((NZ,))] * 2
    held = [
        pltpu.VMEM((NZ, T, W), bf16),
        pltpu.VMEM((NZ, W, W), bf16),
        pltpu.SemaphoreType.DMA((NZ,)),
        pltpu.SemaphoreType.DMA((NZ, 4)),
    ]
    in_keep, in_send, gs = call(
        in_total_body,
        "in_parts",
        TOTALS + [sds((T, W), bf16)],
        (pos, *blocks, grad, state_in, down, own, came, scale),
        MATMUL,
        held + wide,
        9,
        (0, 1),
    )
    out_keep, out_send = call(
        out_total_body,
        "out_parts",
        TOTALS,
        (pos, *blocks, mixed, state_out, up, own, came),
        MATMUL,
        held + wide,
        9,
        (0, 1),
    )
    (parts,) = call(
        tokens_body,
        "token_parts",
        [sds((NZ, T, W), bf16)],
        (pos, w_in, after(gs, out_keep)),
        MATMUL,
        [pltpu.VMEM((NZ, W, W), bf16), pltpu.VMEM((NZ, T, W), bf16)] + sems,
        away=1,
        out_away=(0,),
    )
    grad_tokens = lax.psum_scatter(
        parts.reshape(NZ * T, W), "tp", scatter_dimension=0, tiled=True
    )
    in_total, out_total = scatter_seq(c, (in_keep, in_send), (out_keep, out_send), parts)
    scale_rows = lax.dynamic_slice_in_dim(out_scale, s * R, R)[:, None]
    out_total = out_total / scale_rows

    in_slopes, in_inside = slopes_of(in_weight, scale)
    out_slopes, out_inside = slopes_of(out_weight, scale_rows)
    in_sum = jnp.sum(in_total * in_slopes, axis=0)[None]
    out_sum = jnp.sum(out_total * out_slopes, axis=1)[None]
    in_sum = everyones(in_sum, "seq", NY * NX * NC, 8)
    for bits in (1, 2, 4):
        out_sum = out_sum + z_xor(out_sum, bits)
    out_sum = out_sum[0]
    return (
        grad_tokens,
        in_total * in_inside,
        in_sum / jnp.sqrt(f32(D * QMAX)),
        out_total * out_inside,
        out_sum / jnp.sqrt(f32(HEADS * HEAD_DIM * QMAX)),
    )


def solution(mesh):
    placed = (
        P("seq", "tp"),
        P("seq", "tp"),
        P("seq", "tp"),
        P("tp"),
        P("seq", "tp"),
        P(),
        P("seq", None),
        P("seq", None),
        P("seq", "tp"),
    )
    return jax.shard_map(
        per_device,
        mesh=mesh,
        in_specs=placed,
        out_specs=(P("seq", "tp"), P("seq", "tp"), P("tp"), P("seq", "tp"), P("seq")),
        check_vma=False,
    )
```
